32 devices in a mesh: parts: 2 (over y), space: 4 (over z), mem: 4 (over x, core).
Axes of the slice: x: 2, y: 2, z: 4, core: 2. Of those that a mesh axis runs over, the one named last changes fastest.
Arguments:
- prior_replicas: float32 [128, 2, 32, 2048], P(('parts', 'mem'), None, 'space'), parts along dimension 0, may hold values from -6 to 6
- wind_field: float32 [4, 2, 32, 2048], P('parts', None, 'space'), parts along dimension 0, may hold values from -0.4 to 0.4
- obs_index: int32 [16384], P(('parts', 'space')), parts along dimension 0, may hold values from 0 to 32767, as said below
- obs_count: int32 [8], P(('parts', 'space')), parts along dimension 0, may hold values from 256 to 2048, as said below
- obs_value: float32 [16384], P(('parts', 'space')), parts along dimension 0, may hold values from -6 to 6
- obs_weight: float32 [16384], P(('parts', 'space')), parts along dimension 0, may hold values from 0.05 to 0.5
Outputs:
- analysis: float32 [128, 2, 32, 2048], P(('parts', 'mem'), None, 'space'), parts along dimension 0
The draws below stay inside these ranges and needn't reach their ends.
There are 2 independent parts, one for each index of `parts`. The reference program is written for one: setup_inputs(seed, part) draws one part's arguments, and reference() takes and returns one part's arrays. A program takes and returns all parts, laid end to end along the dimension named above; each array names one. Nothing has to cross between parts.
Inputs may be any that keep to these rules, and one draw needn't show every extreme that they name: `obs_index`: the slots of one strip name distinct cells of that strip, as f * 8 * 2048 + r * 2048 + c for field f, local row r and column c. `obs_count`: one entry per strip; some strip uses all 2048 slots.
All inputs are finite; a program needn't handle non-finite values.
Results may differ from the reference program's by a relative error of at most 0.0038.
Values may be sent and summed in bfloat16 or wider, within the bound.
No kernel may reach another device: no remote copies, remote signals or barrier semaphores. Data moves between devices by JAX's collectives and lax.ppermute only.
A program may use at most 128 MiB of HBM per device.

```python
import math
import jax
import jax.numpy as jnp
from jax import lax

REPLICA_COUNT = 64
ROWS_DEV = 8
COLS = 2048
NS_ITERS = 5
NROWS = 32
OBS_CAP = 2048
N_SPACE = 4


def draw_obs_count(key, part):
    offset = jax.random.randint(jax.random.fold_in(key, 11), (), 0, N_SPACE)
    rank = (jnp.arange(N_SPACE, dtype=jnp.int32) + offset) % N_SPACE
    lowest = OBS_CAP // 8
    ramp = lowest + (OBS_CAP - lowest) * rank * rank // ((N_SPACE - 1) * (N_SPACE - 1))
    jitter = jax.random.randint(jax.random.fold_in(key, 12), (N_SPACE,), 0, max(OBS_CAP // 16, 1))
    return jnp.minimum(ramp + jitter, OBS_CAP).astype(jnp.int32)


def draw_obs_index(key, part):
    cells = 2 * ROWS_DEV * COLS
    strip_keys = jax.random.split(jax.random.fold_in(key, 13), N_SPACE)

    def one_strip(strip_key):
        return jax.random.permutation(strip_key, cells)[:OBS_CAP]
    chosen = jax.vmap(one_strip)(strip_keys)
    return chosen.reshape(-1).astype(jnp.int32)


def levels(stream_key, dims, cuts, smallest, largest):
    level = 1.0
    for axis_at, parts in cuts:
        steps = jax.random.uniform(jax.random.fold_in(jax.random.fold_in(stream_key, 6), axis_at), (parts,), jnp.float32, smallest / len(cuts), largest / len(cuts))
        level = level * jnp.repeat(jnp.exp(steps), dims[axis_at] // parts).reshape((-1,) + (1,) * (len(dims) - 1 - axis_at))
    return level


def noise(key, shape, scale, limit, shards=(), kind=jnp.bfloat16):
    gain = levels(key, shape, shards, -0.22, 0.18) if shards else 1.0
    entries = jax.random.normal(key, shape, jnp.float32) * scale * gain
    return jnp.minimum(jnp.maximum(entries, -limit), limit).astype(kind)


def setup_inputs(seed: int = 0, part: int = 0) -> dict:
    key_of = jax.random.split(jax.random.key(seed), 7)
    part_splits = jax.random.split(jax.random.fold_in(key_of[6], part), 7)
    return {
        "prior_replicas": noise(part_splits[0], (REPLICA_COUNT, 2, NROWS, COLS), 1.0, 6.0, ((0, 4), (2, 4)), jnp.float32),
        "wind_field": jnp.clip(jax.random.uniform(part_splits[1], (2, 2, NROWS, COLS), jnp.float32, -0.4, 0.4) * levels(part_splits[1], (2, 2, NROWS, COLS), ((2, 4),), -0.4, 0.0), -0.4, 0.4),
        "obs_index": draw_obs_index(jax.random.fold_in(jax.random.fold_in(key_of[6], part), 71), part),
        "obs_count": draw_obs_count(jax.random.fold_in(jax.random.fold_in(key_of[6], part), 71), part),
        "obs_value": noise(part_splits[4], (N_SPACE * OBS_CAP,), 1.0, 6.0, ((0, 4),), jnp.float32),
        "obs_weight": jnp.clip(jnp.exp(math.log(0.5) - 2.3025851 * jax.random.uniform(part_splits[5], (N_SPACE * OBS_CAP,), jnp.float32) ** levels(part_splits[5], (N_SPACE * OBS_CAP,), ((0, 4),), -0.2, 0.2)), 0.05, 0.5),
    }


DIFFUSION = (0.05, 0.15)

def shift_columns(field, offset):
    width = field.shape[-1]
    blank = jnp.zeros(field.shape[:-1] + (abs(offset),), field.dtype)
    if offset > 0:
        return jnp.concatenate([field[..., offset:], blank], -1)
    return jnp.concatenate([blank, field[..., :width + offset]], -1)

def advance(extended, wind_rows):
    center = extended[:, :, 2:-2]
    north_one = extended[:, :, 3:-1]
    south_one = extended[:, :, 1:-3]
    north_two = extended[:, :, 4:]
    south_two = extended[:, :, :-4]
    east_one = shift_columns(center, 1)
    west_one = shift_columns(center, -1)
    east_two = shift_columns(center, 2)
    west_two = shift_columns(center, -2)
    grad_row = (8.0 * (north_one - south_one) - (north_two - south_two)) / 12.0
    grad_col = (8.0 * (east_one - west_one) - (east_two - west_two)) / 12.0
    laplace = north_one + south_one + east_one + west_one - 4.0 * center
    diffusion = jnp.array(DIFFUSION, jnp.float32).reshape(2, 1, 1)
    return center - wind_rows[0] * grad_row - wind_rows[1] * grad_col + diffusion * laplace

def shard_terms(observed, slot_weight, obs_value):
    obs_mean = lax.optimization_barrier(jnp.sum(observed, 0)) / REPLICA_COUNT
    obs_anomaly = observed - obs_mean
    weighted = obs_anomaly * slot_weight
    gram = jnp.dot(weighted, obs_anomaly.T, precision=lax.Precision.HIGHEST, preferred_element_type=jnp.float32)
    drive = jnp.dot(weighted, obs_value - obs_mean, precision=lax.Precision.HIGHEST, preferred_element_type=jnp.float32)
    return (gram, drive)

def ensemble_weights(gram, drive):
    ident = jnp.eye(REPLICA_COUNT, dtype=jnp.float32)
    system = (REPLICA_COUNT - 1.0) * ident + gram
    scale = jnp.sqrt(jnp.sum(system * system))

    def newton_turn(turn, carry):
        root, inverse_root = carry
        middle_term = 0.5 * (3.0 * ident - jnp.dot(inverse_root, root, precision=lax.Precision.HIGHEST, preferred_element_type=jnp.float32))
        root = jnp.dot(root, middle_term, precision=lax.Precision.HIGHEST, preferred_element_type=jnp.float32)
        inverse_root = jnp.dot(middle_term, inverse_root, precision=lax.Precision.HIGHEST, preferred_element_type=jnp.float32)
        return (root, inverse_root)
    root, inverse_root = lax.fori_loop(0, NS_ITERS, newton_turn, (system / scale, ident))
    half = inverse_root / jnp.sqrt(scale)
    precision_matrix = jnp.dot(half, half, precision=lax.Precision.HIGHEST, preferred_element_type=jnp.float32)
    mean_weight = jnp.dot(precision_matrix, drive, precision=lax.Precision.HIGHEST, preferred_element_type=jnp.float32)
    spread = jnp.sqrt(REPLICA_COUNT - 1.0) * half
    return (mean_weight[:, None] + spread).astype(jnp.bfloat16)

def reference(prior_replicas, wind_field, obs_index, obs_count, obs_value, obs_weight):

    def integrate_replica(member_state):
        state = member_state[None]
        for step_index in range(2):
            extended = jnp.pad(state, ((0, 0), (0, 0), (2, 2), (0, 0)))
            state = advance(extended, wind_field[step_index])
        return state[0]
    predicted_replicas = lax.map(integrate_replica, prior_replicas)
    raveled_vector = predicted_replicas.reshape(REPLICA_COUNT, -1)
    slots = obs_index.reshape(N_SPACE, OBS_CAP)
    strip_cells = ROWS_DEV * COLS
    field_part = slots // strip_cells
    remainder = slots % strip_cells
    strip_index = jnp.arange(N_SPACE, dtype=jnp.int32)[:, None]
    location = field_part * (NROWS * COLS) + strip_index * strip_cells + remainder
    observed = jnp.take(raveled_vector, location.reshape(-1).astype(jnp.int32), axis=1)
    slot_number = jnp.arange(OBS_CAP, dtype=jnp.int32)[None, :]
    valid = (slot_number < obs_count[:, None]).astype(jnp.float32).reshape(-1)
    slot_weight = obs_weight * valid
    gram, drive = shard_terms(observed, slot_weight, obs_value)
    transform = ensemble_weights(gram, drive)
    replica_centroid = lax.optimization_barrier(jnp.sum(predicted_replicas, 0)) / REPLICA_COUNT
    replica_departure = (predicted_replicas - replica_centroid).astype(jnp.bfloat16)
    posterior_correction = jnp.dot(transform.T, replica_departure.reshape(REPLICA_COUNT, -1), preferred_element_type=jnp.float32)
    return posterior_correction.reshape(predicted_replicas.shape) + replica_centroid
```

```python
import jax
import jax.numpy as jnp
from jax import lax
from jax.experimental import pallas as pl
from jax.experimental.pallas import tpu as pltpu
from jax.sharding import PartitionSpec as P

REPLICA_COUNT = 64
NS_ITERS = 5


DIFFUSION = (0.05, 0.15)


def padded(value, sides, width):
    for axis, dim in sides:
        peers, length = (lax.axis_size(axis), value.shape[dim])
        up = [(i, (i + 1) % peers) for i in range(peers - 1)]
        down = [(j, i) for i, j in up]
        last = lax.slice_in_dim(value, length - width, length, axis=dim)
        initial = lax.slice_in_dim(value, 0, width, axis=dim)
        before = lax.ppermute(last, axis, up)
        after = lax.ppermute(initial, axis, down)
        value = jnp.concatenate([before, value, after], axis=dim)
    return value


def shift_columns(field, offset):
    width = field.shape[-1]
    blank = jnp.zeros(field.shape[:-1] + (abs(offset),), field.dtype)
    if offset > 0:
        return jnp.concatenate([field[..., offset:], blank], -1)
    return jnp.concatenate([blank, field[..., : width + offset]], -1)


def advance(extended, wind_rows):
    center = extended[:, :, 2:-2]
    north_one = extended[:, :, 3:-1]
    south_one = extended[:, :, 1:-3]
    north_two = extended[:, :, 4:]
    south_two = extended[:, :, :-4]
    east_one = shift_columns(center, 1)
    west_one = shift_columns(center, -1)
    east_two = shift_columns(center, 2)
    west_two = shift_columns(center, -2)
    grad_row = (8.0 * (north_one - south_one) - (north_two - south_two)) / 12.0
    grad_col = (8.0 * (east_one - west_one) - (east_two - west_two)) / 12.0
    laplace = north_one + south_one + east_one + west_one - 4.0 * center
    diffusion = jnp.array(DIFFUSION, jnp.float32).reshape(2, 1, 1)
    return center - wind_rows[0] * grad_row - wind_rows[1] * grad_col + diffusion * laplace


def shard_terms(observed, slot_weight, obs_value):
    obs_mean = jnp.sum(observed, 0) / REPLICA_COUNT
    obs_anomaly = observed - obs_mean
    weighted = obs_anomaly * slot_weight
    gram = jnp.dot(
        weighted, obs_anomaly.T, precision=lax.Precision.HIGHEST, preferred_element_type=jnp.float32
    )
    drive = jnp.dot(
        weighted,
        obs_value - obs_mean,
        precision=lax.Precision.HIGHEST,
        preferred_element_type=jnp.float32,
    )
    return (gram, drive)


def ensemble_weights(gram, drive):
    ident = jnp.eye(REPLICA_COUNT, dtype=jnp.float32)
    system = (REPLICA_COUNT - 1.0) * ident + gram
    scale = jnp.sqrt(jnp.sum(system * system))

    def newton_turn(turn, carry):
        root, inverse_root = carry
        middle_term = 0.5 * (
            3.0 * ident
            - jnp.dot(
                inverse_root,
                root,
                precision=lax.Precision.HIGHEST,
                preferred_element_type=jnp.float32,
            )
        )
        root = jnp.dot(
            root, middle_term, precision=lax.Precision.HIGHEST, preferred_element_type=jnp.float32
        )
        inverse_root = jnp.dot(
            middle_term,
            inverse_root,
            precision=lax.Precision.HIGHEST,
            preferred_element_type=jnp.float32,
        )
        return (root, inverse_root)

    root, inverse_root = lax.fori_loop(0, NS_ITERS, newton_turn, (system / scale, ident))
    half = inverse_root / jnp.sqrt(scale)
    precision_matrix = jnp.dot(
        half, half, precision=lax.Precision.HIGHEST, preferred_element_type=jnp.float32
    )
    mean_weight = jnp.dot(
        precision_matrix, drive, precision=lax.Precision.HIGHEST, preferred_element_type=jnp.float32
    )
    spread = jnp.sqrt(REPLICA_COUNT - 1.0) * half
    return (mean_weight[:, None] + spread).astype(jnp.bfloat16)


def local_generic(prior_replicas, wind_field, obs_index, obs_count, obs_value, obs_weight):
    member_count, field_count, row_count, col_count = prior_replicas.shape
    state = prior_replicas
    for step_index in range(2):
        extended = padded(state, (("space", 2),), 2)
        state = advance(extended, wind_field[step_index])
    capacity = obs_index.shape[0]
    raveled_vector = state.reshape(member_count, -1)
    local_obs = jnp.take(raveled_vector, obs_index, axis=1)
    slot_number = jnp.arange(capacity, dtype=jnp.int32)
    slot_weight = obs_weight * (slot_number < obs_count[0]).astype(jnp.float32)
    gathered = lax.all_gather(local_obs, "mem", axis=0, tiled=True)
    gram, drive = shard_terms(gathered, slot_weight, obs_value)
    gram, drive = lax.psum((gram, drive), "space")
    transform = ensemble_weights(gram, drive)
    transform_rows = transform.T
    block = lax.all_to_all(state, "mem", split_axis=3, concat_axis=0, tiled=True)
    replica_centroid = jnp.sum(block, 0) / REPLICA_COUNT
    replica_departure = (block - replica_centroid).astype(jnp.bfloat16)
    posterior_correction = jnp.dot(
        transform_rows,
        replica_departure.reshape(REPLICA_COUNT, -1),
        preferred_element_type=jnp.float32,
    )
    analysed = posterior_correction.reshape(block.shape) + replica_centroid
    return lax.all_to_all(analysed, "mem", split_axis=0, concat_axis=3, tiled=True)


BF = jnp.bfloat16
F32 = jnp.float32
PAD = 128


def vmem():
    return pl.BlockSpec(memory_space=pltpu.VMEM)


def smem():
    return pl.BlockSpec(memory_space=pltpu.SMEM)


def params():
    return pltpu.CompilerParams(vmem_limit_bytes=44 * 1024 * 1024)


def pack_kernel(pos, prior, wind, turned, pay_a, pay_b):
    for f in range(2):
        turned[f] = jnp.swapaxes(prior[:, f], 0, 1)
    even = (pos[0] % 2) == 0
    start_a = jnp.where(even, 4, 0)
    start_b = 4 - start_a
    for f in range(2):
        for r in range(4):
            at = (f * 4 + r) * 16
            pay_a[at : at + 16, :] = turned[f, start_a + r].astype(BF)
            pay_b[at : at + 16, :] = turned[f, start_b + r].astype(BF)
    first = jnp.concatenate([wind[0, 0, 0:2], wind[0, 1, 0:2]], 0)
    last = jnp.concatenate([wind[0, 0, 6:8], wind[0, 1, 6:8]], 0)
    first_high = first.astype(BF).astype(F32)
    last_high = last.astype(BF).astype(F32)
    first = jnp.concatenate([first_high, first - first_high], 0)
    last = jnp.concatenate([last_high, last - last_high], 0)
    pay_a[128:136, :] = jnp.where(even, last, first).astype(BF)
    pay_b[128:136, :] = jnp.where(even, first, last).astype(BF)


def maps_kernel(pos, index, count, weight, value, root_map, value_map):
    slots = index.shape[1]
    n = index[...]
    used = lax.broadcasted_iota(jnp.int32, (1, slots), 1) < count[0]
    root = jnp.where(used, jnp.sqrt(weight[...]), 0.0)
    rooted = root * value[...]
    block = n // 128 - pos[2] * 64
    lane = n % 128
    hit = lax.broadcasted_iota(jnp.int32, (64, slots), 0) == block
    hit = jnp.where(hit, 1.0, 0.0).astype(BF)
    lane_hit = lax.broadcasted_iota(jnp.int32, (128, slots), 0) == lane
    pieces = []
    for v in (root, rooted):
        high = v.astype(BF).astype(F32)
        for part in (high, v - high):
            pieces.append(jnp.where(lane_hit, part, 0.0).astype(BF))
    spread = jnp.concatenate(pieces, 0)
    out = lax.dot_general(
        hit, spread, (((1,), (1,)), ((), ())), preferred_element_type=F32
    )
    root_map[...] = out[:, 0:128] + out[:, 128:256]
    value_map[...] = out[:, 256:384] + out[:, 384:512]


def stencil_row(rows, wind_r, wind_c, nu):
    south_two, south_one, center, north_one, north_two = rows
    width = center.shape[1]
    east_one = pltpu.roll(center, width - 1, 1)
    west_one = pltpu.roll(center, 1, 1)
    east_two = pltpu.roll(center, width - 2, 1)
    west_two = pltpu.roll(center, 2, 1)
    grad_r = 8.0 * (north_one - south_one) - (north_two - south_two)
    grad_c = 8.0 * (east_one - west_one) - (east_two - west_two)
    ring = (north_one + south_one) + (east_one + west_one)
    out = (1.0 - 4.0 * nu) * center + nu * ring
    cut = width - PAD
    return out[:, :cut] - wind_r * grad_r[:, :cut] - wind_c * grad_c[:, :cut]


def stencil_kernel(
    pos, turned, recv_a, recv_b, wind, out_near, out_far, out_diag, ext, mid, wide, wide2
):
    cols = turned.shape[3]
    even = (pos[0] % 2) == 0
    start_a = jnp.where(even, 12, 0)
    start_b = 12 - start_a
    zeros = jnp.zeros((16, PAD), F32)
    for f in range(2):
        for r in range(16):
            ext[f, r, :, cols:] = zeros
        for r in range(12):
            mid[f, r, :, cols:] = zeros
        for r in range(8):
            ext[f, r + 4, :, :cols] = turned[f, r]
        for r in range(4):
            at = (f * 4 + r) * 16
            ext[f, start_a + r, :, :cols] = recv_a[at : at + 16, :].astype(F32)
            ext[f, start_b + r, :, :cols] = recv_b[at : at + 16, :].astype(F32)
    got_a = recv_a[128:136, :].astype(F32)
    got_a = got_a[0:4] + got_a[4:8]
    got_b = recv_b[128:136, :].astype(F32)
    got_b = got_b[0:4] + got_b[4:8]
    before = jnp.where(even, got_b, got_a)
    after = jnp.where(even, got_a, got_b)
    twelfth = 1.0 / 12.0
    for c in range(2):
        for r in range(12):
            if r < 2:
                row = before[2 * c + r : 2 * c + r + 1]
            elif r < 10:
                row = wind[0, c, r - 2 : r - 1]
            else:
                row = after[2 * c + r - 10 : 2 * c + r - 9]
            wide[c, r] = jnp.broadcast_to(row * twelfth, (8, cols))
        for r in range(8):
            row = wind[1, c, r : r + 1]
            wide2[c, r] = jnp.broadcast_to(row * twelfth, (8, cols))

    for f in range(2):

        def first_step(r, carry, f=f):
            for g in range(2):
                span = pl.ds(g * 8, 8)
                rows = [ext[f, r + i, span, :] for i in range(5)]
                mid[f, r, span, :cols] = stencil_row(
                    rows, wide[0, r], wide[1, r], DIFFUSION[f]
                )
            return carry

        lax.fori_loop(0, 12, first_step, 0)

    @pl.when(pos[0] == 0)
    def _():
        mid[:, 0:2] = jnp.zeros((2, 2) + mid.shape[2:], F32)

    @pl.when(pos[0] == pos[1] - 1)
    def _():
        mid[:, 10:12] = jnp.zeros((2, 2) + mid.shape[2:], F32)

    for slot, out, place in ((2, out_far, 0), (3, out_diag, 0), (0, out_near, 0), (1, out_near, 1)):
        quarter = jnp.bitwise_xor(pos[2], slot)
        f = quarter // 2
        base = (quarter % 2) * 4
        nu = jnp.where(f == 0, DIFFUSION[0], DIFFUSION[1])

        def second_step(r, carry, f=f, base=base, nu=nu, out=out, place=place):
            row = base + r
            both = []
            for g in range(2):
                span = pl.ds(g * 8, 8)
                rows = [mid[f, row + i, span, :] for i in range(5)]
                both.append(stencil_row(rows, wide2[0, row], wide2[1, row], nu))
            value = jnp.concatenate(both, 0).astype(BF)
            if place is None:
                out[r] = value
            else:
                out[place * 4 + r] = value
            return carry

        lax.fori_loop(0, 4, second_step, 0)


def gram_kernel(pos, own, mate, far, diag, root_map, value_map, out, spread):
    tiles = own.shape[2] // 128
    spread[4] = jnp.zeros(spread.shape[1:], BF)
    for r in range(4):
        for t in range(tiles):
            cut = slice(t * 128, (t + 1) * 128)
            at = r * tiles + t
            into = slice(at * 128, (at + 1) * 128)
            parts = [
                own[r, :, cut].astype(F32),
                mate[4 + r, :, cut].astype(F32),
                far[r, :, cut].astype(F32),
                diag[r, :, cut].astype(F32),
            ]
            total = (parts[0] + parts[1]) + (parts[2] + parts[3])
            mean = jnp.sum(total, 0, keepdims=True) * (1.0 / REPLICA_COUNT)
            root = root_map[at : at + 1, :]
            gap = value_map[at : at + 1, :] - root * mean
            for g in range(4):
                spread[jnp.bitwise_xor(pos[2], g), :, into] = ((parts[g] - mean) * root).astype(BF)
            high = gap.astype(BF).astype(F32)
            pair = jnp.concatenate([high, gap - high, jnp.zeros((14, 128), F32)], 0)
            spread[4, :, into] = pair.astype(BF)
    cells = spread.shape[2]
    left = spread[...].reshape(80, cells)
    right = spread[0:4].reshape(64, cells)
    out[...] = lax.dot_general(
        left, right, (((1,), (1,)), ((), ())), preferred_element_type=F32
    )


def exact(a, b):
    return jnp.dot(a, b, precision=lax.Precision.HIGHEST, preferred_element_type=F32)


def weights_kernel(pos, one, two, out, keep):
    total = one[...] + two[...]
    gram = total[0:64]
    drive = total[64:65] + total[65:66]
    row = lax.broadcasted_iota(jnp.int32, (64, 64), 0)
    col = lax.broadcasted_iota(jnp.int32, (64, 64), 1)
    ident = jnp.where(row == col, 1.0, 0.0)
    system = (REPLICA_COUNT - 1.0) * ident + gram
    square = jnp.sum(jnp.sum(system * system, 1, keepdims=True), 0, keepdims=True)
    scale = jnp.sqrt(square)
    root = system / scale
    inverse_root = ident
    for turn in range(NS_ITERS):
        if turn == 0:
            middle = 0.5 * (3.0 * ident - root)
            inverse_next = middle
        else:
            middle = 0.5 * (3.0 * ident - exact(inverse_root, root))
            inverse_next = exact(middle, inverse_root)
        if turn < NS_ITERS - 1:
            root = exact(root, middle)
        inverse_root = inverse_next
    half = inverse_root / jnp.sqrt(scale)
    drive8 = jnp.broadcast_to(drive, (8, 64))
    mean_weight = exact(exact(drive8, half), half)[0:1]
    transform_t = (mean_weight + (REPLICA_COUNT - 1.0) ** 0.5 * half).astype(BF).astype(F32)
    total_t = jnp.sum(transform_t, 1, keepdims=True)
    keep[...] = transform_t + (1.0 - total_t) * (1.0 / REPLICA_COUNT)
    mine = keep[pl.ds(pl.multiple_of(pos[2] * 16, 16), 16), :]
    swap1 = jnp.concatenate([mine[:, 16:32], mine[:, 0:16], mine[:, 48:64], mine[:, 32:48]], 1)
    mine = jnp.where((pos[2] % 2) == 1, swap1, mine)
    swap2 = jnp.concatenate([mine[:, 32:64], mine[:, 0:32]], 1)
    mine = jnp.where(pos[2] >= 2, swap2, mine)
    high = mine.astype(BF).astype(F32)
    out[...] = jnp.concatenate([high, mine - high], 0).astype(BF)


def final_kernel(
    pos, weights, own_near, own_far, own_diag, mate_near, mate_far, mate_diag,
    far, far_mate, far_near, diag, diag_mate, diag_near, out, keep
):
    m = weights[...]
    for t in range(4):
        quarter = jnp.bitwise_xor(pos[2], t)
        f = quarter // 2
        base = (quarter % 2) * 4
        for r in range(4):
            if t == 0:
                parts = [own_near[r], mate_near[4 + r], far[r], diag[r]]
            elif t == 1:
                parts = [own_near[4 + r], mate_near[r], far_mate[r], diag_mate[r]]
            elif t == 2:
                parts = [own_far[r], mate_diag[r], far_near[r], diag_near[4 + r]]
            else:
                parts = [own_diag[r], mate_far[r], far_near[4 + r], diag_near[r]]
            state = jnp.concatenate(parts, 0)
            both = jnp.dot(m, state, preferred_element_type=F32)
            keep[f, base + r] = both[0:16] + both[16:32]
    for f in range(2):
        out[:, f] = jnp.swapaxes(keep[f], 0, 1)


def local(prior_replicas, wind_field, obs_index, obs_count, obs_value, obs_weight):
    cols = prior_replicas.shape[3]
    strips = lax.axis_size("space")
    here = lax.axis_index("space")
    group = lax.axis_index("mem")
    pos = jnp.stack([here, jnp.int32(strips), group]).astype(jnp.int32)
    shape = jax.ShapeDtypeStruct

    turned, pay_a, pay_b = pl.pallas_call(
        pack_kernel,
        name="pack",
        in_specs=[smem(), vmem(), vmem()],
        out_specs=[vmem()] * 3,
        out_shape=[shape((2, 8, 16, cols), F32), shape((136, cols), BF), shape((136, cols), BF)],
        compiler_params=params(),
    )(pos, prior_replicas, wind_field)

    pairs_a = [(i, i ^ 1) for i in range(strips) if (i ^ 1) < strips]
    pairs_b = [(i, i + 1) for i in range(1, strips - 1, 2)]
    pairs_b = pairs_b + [(j, i) for i, j in pairs_b]
    recv_a = lax.ppermute(pay_a, "space", pairs_a)
    recv_b = lax.ppermute(pay_b, "space", pairs_b)

    slots = obs_index.shape[0]
    root_map, value_map = pl.pallas_call(
        maps_kernel,
        name="maps",
        in_specs=[smem(), vmem(), smem(), vmem(), vmem()],
        out_specs=[vmem()] * 2,
        out_shape=[shape((64, 128), F32)] * 2,
        compiler_params=params(),
    )(
        pos,
        obs_index.reshape(1, slots),
        obs_count,
        obs_weight.reshape(1, slots),
        obs_value.reshape(1, slots),
    )

    near, far, diag = pl.pallas_call(
        stencil_kernel,
        name="stencil",
        in_specs=[smem()] + [vmem()] * 4,
        out_specs=[vmem()] * 3,
        out_shape=[shape((8, 16, cols), BF), shape((4, 16, cols), BF), shape((4, 16, cols), BF)],
        scratch_shapes=[
            pltpu.VMEM((2, 16, 16, cols + PAD), F32),
            pltpu.VMEM((2, 12, 16, cols + PAD), F32),
            pltpu.VMEM((2, 12, 8, cols), F32),
            pltpu.VMEM((2, 8, 8, cols), F32),
        ],
        compiler_params=params(),
    )(pos, turned, recv_a, recv_b, wind_field)

    def swap(value, bits):
        return lax.ppermute(value, "mem", [(i, i ^ bits) for i in range(4)])

    got_far = swap(far, 2)
    got_diag = swap(diag, 3)
    mate_near = swap(near, 1)
    got_far, got_diag, mate_near, near_late, far_late, diag_late = lax.optimization_barrier(
        (got_far, got_diag, mate_near, near, far, diag)
    )
    far_near = swap(near_late, 2)
    mate_far = swap(far_late, 1)
    mate_diag = swap(diag_late, 1)
    diag_mate = swap(got_far, 1)
    far_mate = swap(got_diag, 1)
    diag_near = swap(far_near, 1)

    part = pl.pallas_call(
        gram_kernel,
        name="gram",
        in_specs=[smem()] + [vmem()] * 6,
        out_specs=vmem(),
        out_shape=shape((80, 64), F32),
        scratch_shapes=[pltpu.VMEM((5, 16, 4 * cols), BF)],
        compiler_params=params(),
    )(pos, near, mate_near, got_far, got_diag, root_map, value_map)

    rounds = [("mem", 1), ("mem", 2)]
    bit = 1
    while bit < strips:
        rounds.append(("space", bit))
        bit *= 2
    other = None
    for axis, bits in rounds:
        if other is not None:
            part = part + other
        size = lax.axis_size(axis)
        other = lax.ppermute(part, axis, [(i, i ^ bits) for i in range(size)])

    weights = pl.pallas_call(
        weights_kernel,
        name="weights",
        in_specs=[smem(), vmem(), vmem()],
        out_specs=vmem(),
        out_shape=shape((32, 64), BF),
        scratch_shapes=[pltpu.VMEM((64, 64), F32)],
        compiler_params=params(),
    )(pos, part, other)

    return pl.pallas_call(
        final_kernel,
        name="final",
        in_specs=[smem()] + [vmem()] * 13,
        out_specs=vmem(),
        out_shape=shape(prior_replicas.shape, F32),
        scratch_shapes=[pltpu.VMEM((2, 8, 16, cols), F32)],
        compiler_params=params(),
    )(
        pos, weights, near, far, diag, mate_near, mate_far, mate_diag,
        got_far, far_mate, far_near, got_diag, diag_mate, diag_near,
    )


def solution(mesh):
    in_specs = (
        P(("parts", "mem"), None, "space", None),
        P("parts", None, "space", None),
        P(("parts", "space")),
        P(("parts", "space")),
        P(("parts", "space")),
        P(("parts", "space")),
    )
    out_specs = P(("parts", "mem"), None, "space", None)
    strips = mesh.shape["space"]
    fast = mesh.shape["mem"] == 4 and strips > 1 and strips & (strips - 1) == 0
    body = local if fast else local_generic
    return jax.shard_map(body, mesh=mesh, in_specs=in_specs, out_specs=out_specs, check_vma=False)
```

```python
import jax
import jax.numpy as jnp
from jax import lax
from jax.experimental import pallas as pl
from jax.experimental.pallas import tpu as pltpu
from jax.sharding import PartitionSpec as P

REPLICA_COUNT = 64
NS_ITERS = 5


DIFFUSION = (0.05, 0.15)


def padded(value, sides, width):
    for axis, dim in sides:
        peers, length = (lax.axis_size(axis), value.shape[dim])
        up = [(i, (i + 1) % peers) for i in range(peers - 1)]
        down = [(j, i) for i, j in up]
        last = lax.slice_in_dim(value, length - width, length, axis=dim)
        initial = lax.slice_in_dim(value, 0, width, axis=dim)
        before = lax.ppermute(last, axis, up)
        after = lax.ppermute(initial, axis, down)
        value = jnp.concatenate([before, value, after], axis=dim)
    return value


def shift_columns(field, offset):
    width = field.shape[-1]
    blank = jnp.zeros(field.shape[:-1] + (abs(offset),), field.dtype)
    if offset > 0:
        return jnp.concatenate([field[..., offset:], blank], -1)
    return jnp.concatenate([blank, field[..., : width + offset]], -1)


def advance(extended, wind_rows):
    center = extended[:, :, 2:-2]
    north_one = extended[:, :, 3:-1]
    south_one = extended[:, :, 1:-3]
    north_two = extended[:, :, 4:]
    south_two = extended[:, :, :-4]
    east_one = shift_columns(center, 1)
    west_one = shift_columns(center, -1)
    east_two = shift_columns(center, 2)
    west_two = shift_columns(center, -2)
    grad_row = (8.0 * (north_one - south_one) - (north_two - south_two)) / 12.0
    grad_col = (8.0 * (east_one - west_one) - (east_two - west_two)) / 12.0
    laplace = north_one + south_one + east_one + west_one - 4.0 * center
    diffusion = jnp.array(DIFFUSION, jnp.float32).reshape(2, 1, 1)
    return center - wind_rows[0] * grad_row - wind_rows[1] * grad_col + diffusion * laplace


def shard_terms(observed, slot_weight, obs_value):
    obs_mean = jnp.sum(observed, 0) / REPLICA_COUNT
    obs_anomaly = observed - obs_mean
    weighted = obs_anomaly * slot_weight
    gram = jnp.dot(
        weighted, obs_anomaly.T, precision=lax.Precision.HIGHEST, preferred_element_type=jnp.float32
    )
    drive = jnp.dot(
        weighted,
        obs_value - obs_mean,
        precision=lax.Precision.HIGHEST,
        preferred_element_type=jnp.float32,
    )
    return (gram, drive)


def ensemble_weights(gram, drive):
    ident = jnp.eye(REPLICA_COUNT, dtype=jnp.float32)
    system = (REPLICA_COUNT - 1.0) * ident + gram
    scale = jnp.sqrt(jnp.sum(system * system))

    def newton_turn(turn, carry):
        root, inverse_root = carry
        middle_term = 0.5 * (
            3.0 * ident
            - jnp.dot(
                inverse_root,
                root,
                precision=lax.Precision.HIGHEST,
                preferred_element_type=jnp.float32,
            )
        )
        root = jnp.dot(
            root, middle_term, precision=lax.Precision.HIGHEST, preferred_element_type=jnp.float32
        )
        inverse_root = jnp.dot(
            middle_term,
            inverse_root,
            precision=lax.Precision.HIGHEST,
            preferred_element_type=jnp.float32,
        )
        return (root, inverse_root)

    root, inverse_root = lax.fori_loop(0, NS_ITERS, newton_turn, (system / scale, ident))
    half = inverse_root / jnp.sqrt(scale)
    precision_matrix = jnp.dot(
        half, half, precision=lax.Precision.HIGHEST, preferred_element_type=jnp.float32
    )
    mean_weight = jnp.dot(
        precision_matrix, drive, precision=lax.Precision.HIGHEST, preferred_element_type=jnp.float32
    )
    spread = jnp.sqrt(REPLICA_COUNT - 1.0) * half
    return (mean_weight[:, None] + spread).astype(jnp.bfloat16)


def local_generic(prior_replicas, wind_field, obs_index, obs_count, obs_value, obs_weight):
    member_count, field_count, row_count, col_count = prior_replicas.shape
    state = prior_replicas
    for step_index in range(2):
        extended = padded(state, (("space", 2),), 2)
        state = advance(extended, wind_field[step_index])
    capacity = obs_index.shape[0]
    raveled_vector = state.reshape(member_count, -1)
    local_obs = jnp.take(raveled_vector, obs_index, axis=1)
    slot_number = jnp.arange(capacity, dtype=jnp.int32)
    slot_weight = obs_weight * (slot_number < obs_count[0]).astype(jnp.float32)
    gathered = lax.all_gather(local_obs, "mem", axis=0, tiled=True)
    gram, drive = shard_terms(gathered, slot_weight, obs_value)
    gram, drive = lax.psum((gram, drive), "space")
    transform = ensemble_weights(gram, drive)
    transform_rows = transform.T
    block = lax.all_to_all(state, "mem", split_axis=3, concat_axis=0, tiled=True)
    replica_centroid = jnp.sum(block, 0) / REPLICA_COUNT
    replica_departure = (block - replica_centroid).astype(jnp.bfloat16)
    posterior_correction = jnp.dot(
        transform_rows,
        replica_departure.reshape(REPLICA_COUNT, -1),
        preferred_element_type=jnp.float32,
    )
    analysed = posterior_correction.reshape(block.shape) + replica_centroid
    return lax.all_to_all(analysed, "mem", split_axis=0, concat_axis=3, tiled=True)


BF = jnp.bfloat16
F32 = jnp.float32
PAD = 128


def vmem():
    return pl.BlockSpec(memory_space=pltpu.VMEM)


def smem():
    return pl.BlockSpec(memory_space=pltpu.SMEM)


def params():
    return pltpu.CompilerParams(vmem_limit_bytes=44 * 1024 * 1024)


def pack_kernel(pos, prior, wind, turned, pay_a, pay_b):
    for f in range(2):
        turned[f] = jnp.swapaxes(prior[:, f], 0, 1)
    even = (pos[0] % 2) == 0
    start_a = jnp.where(even, 4, 0)
    start_b = 4 - start_a
    for f in range(2):
        for r in range(4):
            at = (f * 4 + r) * 16
            pay_a[at : at + 16, :] = turned[f, start_a + r].astype(BF)
            pay_b[at : at + 16, :] = turned[f, start_b + r].astype(BF)
    first = jnp.concatenate([wind[0, 0, 0:2], wind[0, 1, 0:2]], 0)
    last = jnp.concatenate([wind[0, 0, 6:8], wind[0, 1, 6:8]], 0)
    first_high = first.astype(BF).astype(F32)
    last_high = last.astype(BF).astype(F32)
    first = jnp.concatenate([first_high, first - first_high], 0)
    last = jnp.concatenate([last_high, last - last_high], 0)
    pay_a[128:136, :] = jnp.where(even, last, first).astype(BF)
    pay_b[128:136, :] = jnp.where(even, first, last).astype(BF)


def maps_kernel(pos, index, count, weight, value, root_map, value_map):
    slots = index.shape[1]
    n = index[...]
    used = lax.broadcasted_iota(jnp.int32, (1, slots), 1) < count[0]
    root = jnp.where(used, jnp.sqrt(weight[...]), 0.0)
    rooted = root * value[...]
    block = n // 128 - pos[2] * 64
    lane = n % 128
    hit = lax.broadcasted_iota(jnp.int32, (64, slots), 0) == block
    hit = jnp.where(hit, 1.0, 0.0).astype(BF)
    lane_hit = lax.broadcasted_iota(jnp.int32, (128, slots), 0) == lane
    pieces = []
    for v in (root, rooted):
        high = v.astype(BF).astype(F32)
        for part in (high, v - high):
            pieces.append(jnp.where(lane_hit, part, 0.0).astype(BF))
    spread = jnp.concatenate(pieces, 0)
    out = lax.dot_general(
        hit, spread, (((1,), (1,)), ((), ())), preferred_element_type=F32
    )
    root_map[...] = out[:, 0:128] + out[:, 128:256]
    value_map[...] = out[:, 256:384] + out[:, 384:512]


def stencil_row(rows, wind_r, wind_c, nu):
    south_two, south_one, center, north_one, north_two = rows
    width = center.shape[1]
    east_one = pltpu.roll(center, width - 1, 1)
    west_one = pltpu.roll(center, 1, 1)
    east_two = pltpu.roll(center, width - 2, 1)
    west_two = pltpu.roll(center, 2, 1)
    grad_r = 8.0 * (north_one - south_one) - (north_two - south_two)
    grad_c = 8.0 * (east_one - west_one) - (east_two - west_two)
    ring = (north_one + south_one) + (east_one + west_one)
    out = (1.0 - 4.0 * nu) * center + nu * ring
    cut = width - PAD
    return out[:, :cut] - wind_r * grad_r[:, :cut] - wind_c * grad_c[:, :cut]


def stencil_kernel(
    pos, turned, recv_a, recv_b, wind, out_near, out_far, out_diag, ext, mid, wide, wide2
):
    cols = turned.shape[3]
    even = (pos[0] % 2) == 0
    start_a = jnp.where(even, 12, 0)
    start_b = 12 - start_a
    zeros = jnp.zeros((16, PAD), F32)
    for f in range(2):
        for r in range(16):
            ext[f, r, :, cols:] = zeros
        for r in range(12):
            mid[f, r, :, cols:] = zeros
        for r in range(8):
            ext[f, r + 4, :, :cols] = turned[f, r]
        for r in range(4):
            at = (f * 4 + r) * 16
            ext[f, start_a + r, :, :cols] = recv_a[at : at + 16, :].astype(F32)
            ext[f, start_b + r, :, :cols] = recv_b[at : at + 16, :].astype(F32)
    got_a = recv_a[128:136, :].astype(F32)
    got_a = got_a[0:4] + got_a[4:8]
    got_b = recv_b[128:136, :].astype(F32)
    got_b = got_b[0:4] + got_b[4:8]
    before = jnp.where(even, got_b, got_a)
    after = jnp.where(even, got_a, got_b)
    twelfth = 1.0 / 12.0
    for c in range(2):
        for r in range(12):
            if r < 2:
                row = before[2 * c + r : 2 * c + r + 1]
            elif r < 10:
                row = wind[0, c, r - 2 : r - 1]
            else:
                row = after[2 * c + r - 10 : 2 * c + r - 9]
            wide[c, r] = jnp.broadcast_to(row * twelfth, (8, cols))
        for r in range(8):
            row = wind[1, c, r : r + 1]
            wide2[c, r] = jnp.broadcast_to(row * twelfth, (8, cols))

    for f in range(2):

        def first_step(r, carry, f=f):
            for g in range(2):
                span = pl.ds(g * 8, 8)
                rows = [ext[f, r + i, span, :] for i in range(5)]
                mid[f, r, span, :cols] = stencil_row(
                    rows, wide[0, r], wide[1, r], DIFFUSION[f]
                )
            return carry

        lax.fori_loop(0, 12, first_step, 0)

    @pl.when(pos[0] == 0)
    def _():
        mid[:, 0:2] = jnp.zeros((2, 2) + mid.shape[2:], F32)

    @pl.when(pos[0] == pos[1] - 1)
    def _():
        mid[:, 10:12] = jnp.zeros((2, 2) + mid.shape[2:], F32)

    for slot, out, place in ((2, out_far, 0), (3, out_diag, 0), (0, out_near, 0), (1, out_near, 1)):
        quarter = jnp.bitwise_xor(pos[2], slot)
        f = quarter // 2
        base = (quarter % 2) * 4
        nu = jnp.where(f == 0, DIFFUSION[0], DIFFUSION[1])

        def second_step(r, carry, f=f, base=base, nu=nu, out=out, place=place):
            row = base + r
            both = []
            for g in range(2):
                span = pl.ds(g * 8, 8)
                rows = [mid[f, row + i, span, :] for i in range(5)]
                both.append(stencil_row(rows, wide2[0, row], wide2[1, row], nu))
            value = jnp.concatenate(both, 0).astype(BF)
            if place is None:
                out[r] = value
            else:
                out[place * 4 + r] = value
            return carry

        lax.fori_loop(0, 4, second_step, 0)


def gram_kernel(pos, own, mate, far, diag, root_map, value_map, out, spread):
    tiles = own.shape[2] // 128
    spread[4] = jnp.zeros(spread.shape[1:], BF)
    for r in range(4):
        for t in range(tiles):
            cut = slice(t * 128, (t + 1) * 128)
            at = r * tiles + t
            into = slice(at * 128, (at + 1) * 128)
            parts = [
                own[r, :, cut].astype(F32),
                mate[4 + r, :, cut].astype(F32),
                far[r, :, cut].astype(F32),
                diag[r, :, cut].astype(F32),
            ]
            total = (parts[0] + parts[1]) + (parts[2] + parts[3])
            mean = jnp.sum(total, 0, keepdims=True) * (1.0 / REPLICA_COUNT)
            root = root_map[at : at + 1, :]
            gap = value_map[at : at + 1, :] - root * mean
            for g in range(4):
                spread[jnp.bitwise_xor(pos[2], g), :, into] = ((parts[g] - mean) * root).astype(BF)
            high = gap.astype(BF).astype(F32)
            pair = jnp.concatenate([high, gap - high, jnp.zeros((14, 128), F32)], 0)
            spread[4, :, into] = pair.astype(BF)
    cells = spread.shape[2]
    left = spread[...].reshape(80, cells)
    right = spread[0:4].reshape(64, cells)
    out[...] = lax.dot_general(
        left, right, (((1,), (1,)), ((), ())), preferred_element_type=F32
    )


def exact(a, b):
    return jnp.dot(a, b, precision=lax.Precision.HIGHEST, preferred_element_type=F32)


def weights_kernel(pos, one, two, out, keep):
    total = one[...] + two[...]
    gram = total[0:64]
    drive = total[64:65] + total[65:66]
    row = lax.broadcasted_iota(jnp.int32, (64, 64), 0)
    col = lax.broadcasted_iota(jnp.int32, (64, 64), 1)
    ident = jnp.where(row == col, 1.0, 0.0)
    system = (REPLICA_COUNT - 1.0) * ident + gram
    square = jnp.sum(jnp.sum(system * system, 1, keepdims=True), 0, keepdims=True)
    scale = jnp.sqrt(square)
    root = system / scale
    inverse_root = ident
    for turn in range(NS_ITERS):
        if turn == 0:
            middle = 0.5 * (3.0 * ident - root)
            inverse_next = middle
        else:
            middle = 0.5 * (3.0 * ident - exact(inverse_root, root))
            inverse_next = exact(middle, inverse_root)
        if turn < NS_ITERS - 1:
            root = exact(root, middle)
        inverse_root = inverse_next
    half = inverse_root / jnp.sqrt(scale)
    drive8 = jnp.broadcast_to(drive, (8, 64))
    mean_weight = exact(exact(drive8, half), half)[0:1]
    transform_t = (mean_weight + (REPLICA_COUNT - 1.0) ** 0.5 * half).astype(BF).astype(F32)
    total_t = jnp.sum(transform_t, 1, keepdims=True)
    keep[...] = transform_t + (1.0 - total_t) * (1.0 / REPLICA_COUNT)
    mine = keep[pl.ds(pl.multiple_of(pos[2] * 16, 16), 16), :]
    swap1 = jnp.concatenate([mine[:, 16:32], mine[:, 0:16], mine[:, 48:64], mine[:, 32:48]], 1)
    mine = jnp.where((pos[2] % 2) == 1, swap1, mine)
    swap2 = jnp.concatenate([mine[:, 32:64], mine[:, 0:32]], 1)
    mine = jnp.where(pos[2] >= 2, swap2, mine)
    high = mine.astype(BF).astype(F32)
    out[...] = jnp.concatenate([high, mine - high], 0).astype(BF)


def final_kernel(
    pos, weights, own_near, own_far, own_diag, mate_near, mate_far, mate_diag,
    far, far_mate, far_near, diag, diag_mate, diag_near, out, keep
):
    m = weights[...]
    for t in range(4):
        quarter = jnp.bitwise_xor(pos[2], t)
        f = quarter // 2
        base = (quarter % 2) * 4
        for r in range(4):
            if t == 0:
                parts = [own_near[r], mate_near[4 + r], far[r], diag[r]]
            elif t == 1:
                parts = [own_near[4 + r], mate_near[r], far_mate[r], diag_mate[r]]
            elif t == 2:
                parts = [own_far[r], mate_diag[r], far_near[r], diag_near[4 + r]]
            else:
                parts = [own_diag[r], mate_far[r], far_near[4 + r], diag_near[r]]
            state = jnp.concatenate(parts, 0)
            both = jnp.dot(m, state, preferred_element_type=F32)
            keep[f, base + r] = both[0:16] + both[16:32]
    for f in range(2):
        out[:, f] = jnp.swapaxes(keep[f], 0, 1)


def local(prior_replicas, wind_field, obs_index, obs_count, obs_value, obs_weight):
    cols = prior_replicas.shape[3]
    strips = lax.axis_size("space")
    here = lax.axis_index("space")
    group = lax.axis_index("mem")
    pos = jnp.stack([here, jnp.int32(strips), group]).astype(jnp.int32)
    shape = jax.ShapeDtypeStruct

    turned, pay_a, pay_b = pl.pallas_call(
        pack_kernel,
        name="pack",
        in_specs=[smem(), vmem(), vmem()],
        out_specs=[vmem()] * 3,
        out_shape=[shape((2, 8, 16, cols), F32), shape((136, cols), BF), shape((136, cols), BF)],
        compiler_params=params(),
    )(pos, prior_replicas, wind_field)

    pairs_a = [(i, i ^ 1) for i in range(strips) if (i ^ 1) < strips]
    pairs_b = [(i, i + 1) for i in range(1, strips - 1, 2)]
    pairs_b = pairs_b + [(j, i) for i, j in pairs_b]
    recv_a = lax.ppermute(pay_a, "space", pairs_a)
    recv_b = lax.ppermute(pay_b, "space", pairs_b)

    slots = obs_index.shape[0]
    root_map, value_map = pl.pallas_call(
        maps_kernel,
        name="maps",
        in_specs=[smem(), vmem(), smem(), vmem(), vmem()],
        out_specs=[vmem()] * 2,
        out_shape=[shape((64, 128), F32)] * 2,
        compiler_params=params(),
    )(
        pos,
        obs_index.reshape(1, slots),
        obs_count,
        obs_weight.reshape(1, slots),
        obs_value.reshape(1, slots),
    )

    recv_b, root_map, value_map = lax.optimization_barrier((recv_b, root_map, value_map))
    near, far, diag = pl.pallas_call(
        stencil_kernel,
        name="stencil",
        in_specs=[smem()] + [vmem()] * 4,
        out_specs=[vmem()] * 3,
        out_shape=[shape((8, 16, cols), BF), shape((4, 16, cols), BF), shape((4, 16, cols), BF)],
        scratch_shapes=[
            pltpu.VMEM((2, 16, 16, cols + PAD), F32),
            pltpu.VMEM((2, 12, 16, cols + PAD), F32),
            pltpu.VMEM((2, 12, 8, cols), F32),
            pltpu.VMEM((2, 8, 8, cols), F32),
        ],
        compiler_params=params(),
    )(pos, turned, recv_a, recv_b, wind_field)

    def swap(value, bits):
        return lax.ppermute(value, "mem", [(i, i ^ bits) for i in range(4)])

    got_far = swap(far, 2)
    got_diag = swap(diag, 3)
    mate_near = swap(near, 1)
    got_far, got_diag, mate_near, near_late, far_late, diag_late = lax.optimization_barrier(
        (got_far, got_diag, mate_near, near, far, diag)
    )
    far_near = swap(near_late, 2)

    part = pl.pallas_call(
        gram_kernel,
        name="gram",
        in_specs=[smem()] + [vmem()] * 6,
        out_specs=vmem(),
        out_shape=shape((80, 64), F32),
        scratch_shapes=[pltpu.VMEM((5, 16, 4 * cols), BF)],
        compiler_params=params(),
    )(pos, near, mate_near, got_far, got_diag, root_map, value_map)

    rounds = [("mem", 1), ("mem", 2)]
    bit = 1
    while bit < strips:
        rounds.append(("space", bit))
        bit *= 2
    other = None
    for axis, bits in rounds:
        if other is not None:
            part = part + other
        if (axis, bits) == ("mem", 2):
            late = lax.optimization_barrier((far_late, diag_late, got_far, got_diag, part))
            mate_far, mate_diag, diag_mate, far_mate = [swap(v, 1) for v in late[:4]]
        size = lax.axis_size(axis)
        other = lax.ppermute(part, axis, [(i, i ^ bits) for i in range(size)])

    far_near_late, _ = lax.optimization_barrier((far_near, other))
    diag_near = swap(far_near_late, 1)

    weights = pl.pallas_call(
        weights_kernel,
        name="weights",
        in_specs=[smem(), vmem(), vmem()],
        out_specs=vmem(),
        out_shape=shape((32, 64), BF),
        scratch_shapes=[pltpu.VMEM((64, 64), F32)],
        compiler_params=params(),
    )(pos, part, other)

    return pl.pallas_call(
        final_kernel,
        name="final",
        in_specs=[smem()] + [vmem()] * 13,
        out_specs=vmem(),
        out_shape=shape(prior_replicas.shape, F32),
        scratch_shapes=[pltpu.VMEM((2, 8, 16, cols), F32)],
        compiler_params=params(),
    )(
        pos, weights, near, far, diag, mate_near, mate_far, mate_diag,
        got_far, far_mate, far_near, got_diag, diag_mate, diag_near,
    )


def solution(mesh):
    in_specs = (
        P(("parts", "mem"), None, "space", None),
        P("parts", None, "space", None),
        P(("parts", "space")),
        P(("parts", "space")),
        P(("parts", "space")),
        P(("parts", "space")),
    )
    out_specs = P(("parts", "mem"), None, "space", None)
    strips = mesh.shape["space"]
    fast = mesh.shape["mem"] == 4 and strips > 1 and strips & (strips - 1) == 0
    body = local if fast else local_generic
    return jax.shard_map(body, mesh=mesh, in_specs=in_specs, out_specs=out_specs, check_vma=False)
```

```python
import functools

import jax
import jax.numpy as jnp
from jax import lax
from jax.experimental import pallas as pl
from jax.experimental.pallas import tpu as pltpu
from jax.sharding import PartitionSpec as P

REPLICA_COUNT = 64
NS_ITERS = 5


DIFFUSION = (0.05, 0.15)


def padded(value, sides, width):
    for axis, dim in sides:
        peers, length = (lax.axis_size(axis), value.shape[dim])
        up = [(i, (i + 1) % peers) for i in range(peers - 1)]
        down = [(j, i) for i, j in up]
        last = lax.slice_in_dim(value, length - width, length, axis=dim)
        initial = lax.slice_in_dim(value, 0, width, axis=dim)
        before = lax.ppermute(last, axis, up)
        after = lax.ppermute(initial, axis, down)
        value = jnp.concatenate([before, value, after], axis=dim)
    return value


def shift_columns(field, offset):
    width = field.shape[-1]
    blank = jnp.zeros(field.shape[:-1] + (abs(offset),), field.dtype)
    if offset > 0:
        return jnp.concatenate([field[..., offset:], blank], -1)
    return jnp.concatenate([blank, field[..., : width + offset]], -1)


def advance(extended, wind_rows):
    center = extended[:, :, 2:-2]
    north_one = extended[:, :, 3:-1]
    south_one = extended[:, :, 1:-3]
    north_two = extended[:, :, 4:]
    south_two = extended[:, :, :-4]
    east_one = shift_columns(center, 1)
    west_one = shift_columns(center, -1)
    east_two = shift_columns(center, 2)
    west_two = shift_columns(center, -2)
    grad_row = (8.0 * (north_one - south_one) - (north_two - south_two)) / 12.0
    grad_col = (8.0 * (east_one - west_one) - (east_two - west_two)) / 12.0
    laplace = north_one + south_one + east_one + west_one - 4.0 * center
    diffusion = jnp.array(DIFFUSION, jnp.float32).reshape(2, 1, 1)
    return center - wind_rows[0] * grad_row - wind_rows[1] * grad_col + diffusion * laplace


def shard_terms(observed, slot_weight, obs_value):
    obs_mean = jnp.sum(observed, 0) / REPLICA_COUNT
    obs_anomaly = observed - obs_mean
    weighted = obs_anomaly * slot_weight
    gram = jnp.dot(
        weighted, obs_anomaly.T, precision=lax.Precision.HIGHEST, preferred_element_type=jnp.float32
    )
    drive = jnp.dot(
        weighted,
        obs_value - obs_mean,
        precision=lax.Precision.HIGHEST,
        preferred_element_type=jnp.float32,
    )
    return (gram, drive)


def ensemble_weights(gram, drive):
    ident = jnp.eye(REPLICA_COUNT, dtype=jnp.float32)
    system = (REPLICA_COUNT - 1.0) * ident + gram
    scale = jnp.sqrt(jnp.sum(system * system))

    def newton_turn(turn, carry):
        root, inverse_root = carry
        middle_term = 0.5 * (
            3.0 * ident
            - jnp.dot(
                inverse_root,
                root,
                precision=lax.Precision.HIGHEST,
                preferred_element_type=jnp.float32,
            )
        )
        root = jnp.dot(
            root, middle_term, precision=lax.Precision.HIGHEST, preferred_element_type=jnp.float32
        )
        inverse_root = jnp.dot(
            middle_term,
            inverse_root,
            precision=lax.Precision.HIGHEST,
            preferred_element_type=jnp.float32,
        )
        return (root, inverse_root)

    root, inverse_root = lax.fori_loop(0, NS_ITERS, newton_turn, (system / scale, ident))
    half = inverse_root / jnp.sqrt(scale)
    precision_matrix = jnp.dot(
        half, half, precision=lax.Precision.HIGHEST, preferred_element_type=jnp.float32
    )
    mean_weight = jnp.dot(
        precision_matrix, drive, precision=lax.Precision.HIGHEST, preferred_element_type=jnp.float32
    )
    spread = jnp.sqrt(REPLICA_COUNT - 1.0) * half
    return (mean_weight[:, None] + spread).astype(jnp.bfloat16)


def local_generic(prior_replicas, wind_field, obs_index, obs_count, obs_value, obs_weight):
    member_count, field_count, row_count, col_count = prior_replicas.shape
    state = prior_replicas
    for step_index in range(2):
        extended = padded(state, (("space", 2),), 2)
        state = advance(extended, wind_field[step_index])
    capacity = obs_index.shape[0]
    raveled_vector = state.reshape(member_count, -1)
    local_obs = jnp.take(raveled_vector, obs_index, axis=1)
    slot_number = jnp.arange(capacity, dtype=jnp.int32)
    slot_weight = obs_weight * (slot_number < obs_count[0]).astype(jnp.float32)
    gathered = lax.all_gather(local_obs, "mem", axis=0, tiled=True)
    gram, drive = shard_terms(gathered, slot_weight, obs_value)
    gram, drive = lax.psum((gram, drive), "space")
    transform = ensemble_weights(gram, drive)
    transform_rows = transform.T
    block = lax.all_to_all(state, "mem", split_axis=3, concat_axis=0, tiled=True)
    replica_centroid = jnp.sum(block, 0) / REPLICA_COUNT
    replica_departure = (block - replica_centroid).astype(jnp.bfloat16)
    posterior_correction = jnp.dot(
        transform_rows,
        replica_departure.reshape(REPLICA_COUNT, -1),
        preferred_element_type=jnp.float32,
    )
    analysed = posterior_correction.reshape(block.shape) + replica_centroid
    return lax.all_to_all(analysed, "mem", split_axis=0, concat_axis=3, tiled=True)


BF = jnp.bfloat16
F32 = jnp.float32
PAD = 128


def vmem():
    return pl.BlockSpec(memory_space=pltpu.VMEM)


def smem():
    return pl.BlockSpec(memory_space=pltpu.SMEM)


def hbm():
    return pl.BlockSpec(memory_space=pltpu.MemorySpace.HBM)


def params():
    return pltpu.CompilerParams(vmem_limit_bytes=44 * 1024 * 1024)


def cost(touched):
    return pl.CostEstimate(flops=touched, bytes_accessed=touched, transcendentals=0)


def pack_kernel(field, pos, prior, wind, turned, pay_a, pay_b, state, edge, sems):
    load = pltpu.make_async_copy(prior.at[:, field], state, sems.at[0])
    load.start()
    if field == 0:
        winds = pltpu.make_async_copy(wind.at[0], edge, sems.at[1])
        winds.start()
    even = (pos[0] % 2) == 0
    start_a = jnp.where(even, 4, 0)
    start_b = 4 - start_a
    if field == 0:
        winds.wait()
        first = jnp.concatenate([edge[0, 0:2], edge[1, 0:2]], 0)
        last = jnp.concatenate([edge[0, 6:8], edge[1, 6:8]], 0)
        first_high = first.astype(BF).astype(F32)
        last_high = last.astype(BF).astype(F32)
        first = jnp.concatenate([first_high, first - first_high], 0)
        last = jnp.concatenate([last_high, last - last_high], 0)
        pay_a[64:72, :] = jnp.where(even, last, first).astype(BF)
        pay_b[64:72, :] = jnp.where(even, first, last).astype(BF)
    load.wait()
    turned[...] = jnp.swapaxes(state[...], 0, 1)
    for r in range(4):
        pay_a[r * 16 : r * 16 + 16, :] = turned[start_a + r].astype(BF)
        pay_b[r * 16 : r * 16 + 16, :] = turned[start_b + r].astype(BF)


def maps_kernel(tiles, pos, index, count, weight, value, root_map, value_map):
    slots = index.shape[1]
    n = index[...]
    used = lax.broadcasted_iota(jnp.int32, (1, slots), 1) < count[0]
    root = jnp.where(used, jnp.sqrt(weight[...]), 0.0)
    rooted = root * value[...]
    block = n // 128
    row = (block // tiles) % 8
    cell = (block // (tiles * 8)) * (2 * tiles) + (row % 2) * tiles + block % tiles
    cell = jnp.where(row // 2 == pos[2], cell, -1)
    lane = n % 128
    hit = lax.broadcasted_iota(jnp.int32, (4 * tiles, slots), 0) == cell
    hit = jnp.where(hit, 1.0, 0.0).astype(BF)
    lane_hit = lax.broadcasted_iota(jnp.int32, (128, slots), 0) == lane
    pieces = []
    for v in (root, rooted):
        high = v.astype(BF).astype(F32)
        for part in (high, v - high):
            pieces.append(jnp.where(lane_hit, part, 0.0).astype(BF))
    spread = jnp.concatenate(pieces, 0)
    out = lax.dot_general(
        hit, spread, (((1,), (1,)), ((), ())), preferred_element_type=F32
    )
    root_map[...] = out[:, 0:128] + out[:, 128:256]
    value_map[...] = out[:, 256:384] + out[:, 384:512]


def stencil_row(rows, wind_r, wind_c, nu):
    south_two, south_one, center, north_one, north_two = rows
    width = center.shape[1]
    east_one = pltpu.roll(center, width - 1, 1)
    west_one = pltpu.roll(center, 1, 1)
    east_two = pltpu.roll(center, width - 2, 1)
    west_two = pltpu.roll(center, 2, 1)
    grad_r = 8.0 * (north_one - south_one) - (north_two - south_two)
    grad_c = 8.0 * (east_one - west_one) - (east_two - west_two)
    ring = (north_one + south_one) + (east_one + west_one)
    out = (1.0 - 4.0 * nu) * center + nu * ring
    cut = width - PAD
    return out[:, :cut] - wind_r * grad_r[:, :cut] - wind_c * grad_c[:, :cut]


def stencil_kernel(
    nu, pos, turned, recv_a, recv_b, wind_a, wind_b, wind, out_all, out_near, out_far, out_diag,
    ext, mid, wide, wide2
):
    cols = turned.shape[2]
    even = (pos[0] % 2) == 0
    start_a = jnp.where(even, 12, 0)
    start_b = 12 - start_a
    zeros = jnp.zeros((16, PAD), F32)
    for r in range(16):
        ext[r, :, cols:] = zeros
    for r in range(12):
        mid[r, :, cols:] = zeros
    for r in range(8):
        ext[r + 4, :, :cols] = turned[r]
    for r in range(4):
        ext[start_a + r, :, :cols] = recv_a[r * 16 : r * 16 + 16, :].astype(F32)
        ext[start_b + r, :, :cols] = recv_b[r * 16 : r * 16 + 16, :].astype(F32)
    got_a = wind_a[64:72, :].astype(F32)
    got_a = got_a[0:4] + got_a[4:8]
    got_b = wind_b[64:72, :].astype(F32)
    got_b = got_b[0:4] + got_b[4:8]
    before = jnp.where(even, got_b, got_a)
    after = jnp.where(even, got_a, got_b)
    twelfth = 1.0 / 12.0
    for c in range(2):
        for r in range(12):
            if r < 2:
                row = before[2 * c + r : 2 * c + r + 1]
            elif r < 10:
                row = wind[0, c, r - 2 : r - 1]
            else:
                row = after[2 * c + r - 10 : 2 * c + r - 9]
            wide[c, r] = jnp.broadcast_to(row * twelfth, (8, cols))
        for r in range(8):
            row = wind[1, c, r : r + 1]
            wide2[c, r] = jnp.broadcast_to(row * twelfth, (8, cols))

    def first_step(r, carry):
        for g in range(2):
            span = pl.ds(g * 8, 8)
            rows = [ext[r + i, span, :] for i in range(5)]
            mid[r, span, :cols] = stencil_row(rows, wide[0, r], wide[1, r], nu)
        return carry

    lax.fori_loop(0, 12, first_step, 0)

    @pl.when(pos[0] == 0)
    def _():
        mid[0:2] = jnp.zeros((2,) + mid.shape[1:], F32)

    @pl.when(pos[0] == pos[1] - 1)
    def _():
        mid[10:12] = jnp.zeros((2,) + mid.shape[1:], F32)

    def second_step(r, carry):
        both = []
        for g in range(2):
            span = pl.ds(g * 8, 8)
            rows = [mid[r + i, span, :] for i in range(5)]
            both.append(stencil_row(rows, wide2[0, r], wide2[1, r], nu))
        out_all[r] = jnp.concatenate(both, 0).astype(BF)
        return carry

    lax.fori_loop(0, 8, second_step, 0)
    for r in range(2):
        out_far[r] = out_all[2 * jnp.bitwise_xor(pos[2], 2) + r]
        out_diag[r] = out_all[2 * jnp.bitwise_xor(pos[2], 3) + r]
        out_near[r] = out_all[2 * pos[2] + r]
        out_near[2 + r] = out_all[2 * jnp.bitwise_xor(pos[2], 1) + r]


def gram_sum(field, pos, own, mate, far, diag, root_map, value_map, spread):
    tiles = own.shape[2] // 128
    spread[4] = jnp.zeros(spread.shape[1:], BF)
    for r in range(2):
        row = 2 * pos[2] + r
        for t in range(tiles):
            cut = slice(t * 128, (t + 1) * 128)
            at = (field * 2 + r) * tiles + t
            into = slice((r * tiles + t) * 128, (r * tiles + t + 1) * 128)
            parts = [
                own[row, :, cut].astype(F32),
                mate[row, :, cut].astype(F32),
                far[r, :, cut].astype(F32),
                diag[r, :, cut].astype(F32),
            ]
            total = (parts[0] + parts[1]) + (parts[2] + parts[3])
            mean = jnp.sum(total, 0, keepdims=True) * (1.0 / REPLICA_COUNT)
            root = root_map[at : at + 1, :]
            gap = value_map[at : at + 1, :] - root * mean
            for g in range(4):
                spread[jnp.bitwise_xor(pos[2], g), :, into] = ((parts[g] - mean) * root).astype(BF)
            high = gap.astype(BF).astype(F32)
            pair = jnp.concatenate([high, gap - high, jnp.zeros((14, 128), F32)], 0)
            spread[4, :, into] = pair.astype(BF)
    cells = spread.shape[2]
    left = spread[...].reshape(80, cells)
    right = spread[0:4].reshape(64, cells)
    return lax.dot_general(
        left, right, (((1,), (1,)), ((), ())), preferred_element_type=F32
    )


def gram_first(pos, own, mate, far, diag, root_map, value_map, out, spread):
    out[...] = gram_sum(0, pos, own, mate, far, diag, root_map, value_map, spread)


def gram_second(
    pos, own, mate, far, diag, root_map, value_map, part, far_zero, diag_zero, out, pass_on, spread
):
    out[...] = part[...] + gram_sum(1, pos, own, mate, far, diag, root_map, value_map, spread)
    pass_on[0:2] = far_zero[...]
    pass_on[2:4] = diag_zero[...]
    pass_on[4:6] = far[...]
    pass_on[6:8] = diag[...]


def exact(a, b):
    return jnp.dot(a, b, precision=lax.Precision.HIGHEST, preferred_element_type=F32)


def weights_kernel(pos, one, two, out, keep):
    total = one[...] + two[...]
    gram = total[0:64]
    drive = total[64:65] + total[65:66]
    row = lax.broadcasted_iota(jnp.int32, (64, 64), 0)
    col = lax.broadcasted_iota(jnp.int32, (64, 64), 1)
    ident = jnp.where(row == col, 1.0, 0.0)
    system = (REPLICA_COUNT - 1.0) * ident + gram
    square = jnp.sum(jnp.sum(system * system, 1, keepdims=True), 0, keepdims=True)
    scale = jnp.sqrt(square)
    root = system / scale
    inverse_root = ident
    for turn in range(NS_ITERS):
        if turn == 0:
            middle = 0.5 * (3.0 * ident - root)
            inverse_next = middle
        else:
            middle = 0.5 * (3.0 * ident - exact(inverse_root, root))
            inverse_next = exact(middle, inverse_root)
        if turn < NS_ITERS - 1:
            root = exact(root, middle)
        inverse_root = inverse_next
    half = inverse_root / jnp.sqrt(scale)
    drive8 = jnp.broadcast_to(drive, (8, 64))
    mean_weight = exact(exact(drive8, half), half)[0:1]
    transform_t = (mean_weight + (REPLICA_COUNT - 1.0) ** 0.5 * half).astype(BF).astype(F32)
    total_t = jnp.sum(transform_t, 1, keepdims=True)
    keep[...] = transform_t + (1.0 - total_t) * (1.0 / REPLICA_COUNT)
    mine = keep[pl.ds(pl.multiple_of(pos[2] * 16, 16), 16), :]
    swap1 = jnp.concatenate([mine[:, 16:32], mine[:, 0:16], mine[:, 48:64], mine[:, 32:48]], 1)
    mine = jnp.where((pos[2] % 2) == 1, swap1, mine)
    swap2 = jnp.concatenate([mine[:, 32:64], mine[:, 0:32]], 1)
    mine = jnp.where(pos[2] >= 2, swap2, mine)
    high = mine.astype(BF).astype(F32)
    out[...] = jnp.concatenate([high, mine - high], 0).astype(BF)


def final_kernel(
    pos, weights, own_0, own_1, mate_0, mate_1, far_0, far_1, diag_0, diag_1, passed,
    near_0, near_1, mate_near_0, mate_near_1, out, keep, ready, sems
):
    m = weights[...]
    fields = (
        (own_0, mate_0, far_0, diag_0, near_0, mate_near_0),
        (own_1, mate_1, far_1, diag_1, near_1, mate_near_1),
    )
    copies = []
    for f in range(2):
        own, mate, far, diag, near, mate_near = fields[f]
        for t in range(4):
            quarter = jnp.bitwise_xor(pos[2], t)
            for r in range(2):
                row = 2 * quarter + r
                if t == 0:
                    parts = [far[r], diag[r]]
                elif t == 1:
                    parts = [passed[4 * f + 2 + r], passed[4 * f + r]]
                elif t == 2:
                    parts = [near[r], mate_near[2 + r]]
                else:
                    parts = [near[2 + r], mate_near[r]]
                state = jnp.concatenate([own[row], mate[row]] + parts, 0)
                both = jnp.dot(m, state, preferred_element_type=F32)
                keep[row] = both[0:16] + both[16:32]
        ready[f] = jnp.swapaxes(keep[...], 0, 1)
        copies.append(pltpu.make_async_copy(ready.at[f], out.at[:, f], sems.at[f]))
        copies[f].start()
    for f in range(2):
        copies[f].wait()


def local(prior_replicas, wind_field, obs_index, obs_count, obs_value, obs_weight):
    cols = prior_replicas.shape[3]
    tiles = cols // 128
    strips = lax.axis_size("space")
    here = lax.axis_index("space")
    group = lax.axis_index("mem")
    pos = jnp.stack([here, jnp.int32(strips), group]).astype(jnp.int32)
    shape = jax.ShapeDtypeStruct
    pairs_a = [(i, i ^ 1) for i in range(strips)]
    pairs_b = [(i, i + 1) for i in range(1, strips - 1, 2)]
    pairs_b = pairs_b + [(j, i) for i, j in pairs_b]

    def swap(value, bits):
        return lax.ppermute(value, "mem", [(i, i ^ bits) for i in range(4)])

    turned = []
    recv = []
    for f in range(2):
        height = 72 if f == 0 else 64
        rows, pay_a, pay_b = pl.pallas_call(
            functools.partial(pack_kernel, f),
            name="pack",
            cost_estimate=cost(40 * 16 * cols * 4),
            in_specs=[smem(), hbm(), hbm()],
            out_specs=[vmem()] * 3,
            out_shape=[shape((8, 16, cols), F32)] + [shape((height, cols), BF)] * 2,
            scratch_shapes=[
                pltpu.VMEM((16, 8, cols), F32),
                pltpu.VMEM((2, 8, cols), F32),
                pltpu.SemaphoreType.DMA((2,)),
            ],
            compiler_params=params(),
        )(pos, prior_replicas, wind_field)
        turned.append(rows)
        recv.append([lax.ppermute(pay_a, "space", pairs_a), lax.ppermute(pay_b, "space", pairs_b)])

    slots = obs_index.shape[0]
    root_map, value_map = pl.pallas_call(
        functools.partial(maps_kernel, tiles),
        name="maps",
        cost_estimate=cost(slots * 1024 * 4),
        in_specs=[smem(), vmem(), smem(), vmem(), vmem()],
        out_specs=[vmem()] * 2,
        out_shape=[shape((4 * tiles, 128), F32)] * 2,
        compiler_params=params(),
    )(
        pos,
        obs_index.reshape(1, slots),
        obs_count,
        obs_weight.reshape(1, slots),
        obs_value.reshape(1, slots),
    )
    recv[0][1], root_map, value_map = lax.optimization_barrier((recv[0][1], root_map, value_map))

    state = []
    got = []
    for f in range(2):
        every, near, far, diag = pl.pallas_call(
            functools.partial(stencil_kernel, DIFFUSION[f]),
            name="stencil",
            cost_estimate=cost(180 * 16 * cols * 4),
            in_specs=[smem()] + [vmem()] * 6,
            out_specs=[vmem()] * 4,
            out_shape=[
                shape((8, 16, cols), BF),
                shape((4, 16, cols), BF),
                shape((2, 16, cols), BF),
                shape((2, 16, cols), BF),
            ],
            scratch_shapes=[
                pltpu.VMEM((16, 16, cols + PAD), F32),
                pltpu.VMEM((12, 16, cols + PAD), F32),
                pltpu.VMEM((2, 12, 8, cols), F32),
                pltpu.VMEM((2, 8, 8, cols), F32),
            ],
            compiler_params=params(),
        )(pos, turned[f], recv[f][0], recv[f][1], recv[0][0], recv[0][1], wind_field)
        if f == 1:
            got[0][0], got[0][1], every, far, diag = lax.optimization_barrier(
                (got[0][0], got[0][1], every, far, diag)
            )
        state.append((every, near))
        got.append([swap(far, 2), swap(diag, 3), swap(every, 1)])

    def gram(kernel, f, extra, more):
        return pl.pallas_call(
            kernel,
            name="gram",
            cost_estimate=cost(24 * 64 * cols * 2),
            in_specs=[smem()] + [vmem()] * (6 + len(extra)),
            out_specs=[vmem()] * (1 + len(more)),
            out_shape=[shape((80, 64), F32)] + more,
            scratch_shapes=[pltpu.VMEM((5, 16, 2 * cols), BF)],
            compiler_params=params(),
        )(pos, state[f][0], got[f][2], got[f][0], got[f][1], root_map, value_map, *extra)

    part = gram(gram_first, 0, [], [])[0]
    got[1][0], got[1][1], near_0, part = lax.optimization_barrier(
        (got[1][0], got[1][1], state[0][1], part)
    )
    near_0 = swap(near_0, 2)
    part, pass_on = gram(
        gram_second, 1, [part, got[0][0], got[0][1]], [shape((8, 16, cols), BF)]
    )

    rounds = [("mem", 1), ("space", 1), ("mem", 2)]
    bit = 2
    while bit < strips:
        rounds.append(("space", bit))
        bit *= 2
    other = None
    for axis, bits in rounds:
        if other is not None:
            part = part + other
        if (axis, bits) == ("mem", 2):
            part, near_0 = lax.optimization_barrier((part, near_0))
        size = lax.axis_size(axis)
        other = lax.ppermute(part, axis, [(i, i ^ bits) for i in range(size)])
        if (axis, bits) == ("mem", 2):
            near_1, pass_on, other = lax.optimization_barrier((state[1][1], pass_on, other))
            near_1 = swap(near_1, 2)
            passed = swap(pass_on, 1)

    weights = pl.pallas_call(
        weights_kernel,
        name="weights",
        cost_estimate=cost(400 * 64 * 128 * 4),
        in_specs=[smem(), vmem(), vmem()],
        out_specs=vmem(),
        out_shape=shape((32, 64), BF),
        scratch_shapes=[pltpu.VMEM((64, 64), F32)],
        compiler_params=params(),
    )(pos, part, other)

    near_0_late, _ = lax.optimization_barrier((near_0, other))
    mate_near_0 = swap(near_0_late, 1)
    mate_near_1 = swap(near_1, 1)

    return pl.pallas_call(
        final_kernel,
        name="final",
        cost_estimate=cost(100 * 16 * cols * 4),
        in_specs=[smem()] + [vmem()] * 14,
        out_specs=hbm(),
        out_shape=shape(prior_replicas.shape, F32),
        scratch_shapes=[
            pltpu.VMEM((8, 16, cols), F32),
            pltpu.VMEM((2, 16, 8, cols), F32),
            pltpu.SemaphoreType.DMA((2,)),
        ],
        compiler_params=params(),
    )(
        pos, weights, state[0][0], state[1][0], got[0][2], got[1][2], got[0][0], got[1][0],
        got[0][1], got[1][1], passed, near_0, near_1, mate_near_0, mate_near_1,
    )


def solution(mesh):
    in_specs = (
        P(("parts", "mem"), None, "space", None),
        P("parts", None, "space", None),
        P(("parts", "space")),
        P(("parts", "space")),
        P(("parts", "space")),
        P(("parts", "space")),
    )
    out_specs = P(("parts", "mem"), None, "space", None)
    strips = mesh.shape["space"]
    fast = mesh.shape["mem"] == 4 and strips > 1 and strips & (strips - 1) == 0
    body = local if fast else local_generic
    return jax.shard_map(body, mesh=mesh, in_specs=in_specs, out_specs=out_specs, check_vma=False)
```

```python
import functools

import jax
import jax.numpy as jnp
from jax import lax
from jax.experimental import pallas as pl
from jax.experimental.pallas import tpu as pltpu
from jax.sharding import PartitionSpec as P

REPLICA_COUNT = 64
NS_ITERS = 5


DIFFUSION = (0.05, 0.15)


def padded(value, sides, width):
    for axis, dim in sides:
        peers, length = (lax.axis_size(axis), value.shape[dim])
        up = [(i, (i + 1) % peers) for i in range(peers - 1)]
        down = [(j, i) for i, j in up]
        last = lax.slice_in_dim(value, length - width, length, axis=dim)
        initial = lax.slice_in_dim(value, 0, width, axis=dim)
        before = lax.ppermute(last, axis, up)
        after = lax.ppermute(initial, axis, down)
        value = jnp.concatenate([before, value, after], axis=dim)
    return value


def shift_columns(field, offset):
    width = field.shape[-1]
    blank = jnp.zeros(field.shape[:-1] + (abs(offset),), field.dtype)
    if offset > 0:
        return jnp.concatenate([field[..., offset:], blank], -1)
    return jnp.concatenate([blank, field[..., : width + offset]], -1)


def advance(extended, wind_rows):
    center = extended[:, :, 2:-2]
    north_one = extended[:, :, 3:-1]
    south_one = extended[:, :, 1:-3]
    north_two = extended[:, :, 4:]
    south_two = extended[:, :, :-4]
    east_one = shift_columns(center, 1)
    west_one = shift_columns(center, -1)
    east_two = shift_columns(center, 2)
    west_two = shift_columns(center, -2)
    grad_row = (8.0 * (north_one - south_one) - (north_two - south_two)) / 12.0
    grad_col = (8.0 * (east_one - west_one) - (east_two - west_two)) / 12.0
    laplace = north_one + south_one + east_one + west_one - 4.0 * center
    diffusion = jnp.array(DIFFUSION, jnp.float32).reshape(2, 1, 1)
    return center - wind_rows[0] * grad_row - wind_rows[1] * grad_col + diffusion * laplace


def shard_terms(observed, slot_weight, obs_value):
    obs_mean = jnp.sum(observed, 0) / REPLICA_COUNT
    obs_anomaly = observed - obs_mean
    weighted = obs_anomaly * slot_weight
    gram = jnp.dot(
        weighted, obs_anomaly.T, precision=lax.Precision.HIGHEST, preferred_element_type=jnp.float32
    )
    drive = jnp.dot(
        weighted,
        obs_value - obs_mean,
        precision=lax.Precision.HIGHEST,
        preferred_element_type=jnp.float32,
    )
    return (gram, drive)


def ensemble_weights(gram, drive):
    ident = jnp.eye(REPLICA_COUNT, dtype=jnp.float32)
    system = (REPLICA_COUNT - 1.0) * ident + gram
    scale = jnp.sqrt(jnp.sum(system * system))

    def newton_turn(turn, carry):
        root, inverse_root = carry
        middle_term = 0.5 * (
            3.0 * ident
            - jnp.dot(
                inverse_root,
                root,
                precision=lax.Precision.HIGHEST,
                preferred_element_type=jnp.float32,
            )
        )
        root = jnp.dot(
            root, middle_term, precision=lax.Precision.HIGHEST, preferred_element_type=jnp.float32
        )
        inverse_root = jnp.dot(
            middle_term,
            inverse_root,
            precision=lax.Precision.HIGHEST,
            preferred_element_type=jnp.float32,
        )
        return (root, inverse_root)

    root, inverse_root = lax.fori_loop(0, NS_ITERS, newton_turn, (system / scale, ident))
    half = inverse_root / jnp.sqrt(scale)
    precision_matrix = jnp.dot(
        half, half, precision=lax.Precision.HIGHEST, preferred_element_type=jnp.float32
    )
    mean_weight = jnp.dot(
        precision_matrix, drive, precision=lax.Precision.HIGHEST, preferred_element_type=jnp.float32
    )
    spread = jnp.sqrt(REPLICA_COUNT - 1.0) * half
    return (mean_weight[:, None] + spread).astype(jnp.bfloat16)


def local_generic(prior_replicas, wind_field, obs_index, obs_count, obs_value, obs_weight):
    member_count, field_count, row_count, col_count = prior_replicas.shape
    state = prior_replicas
    for step_index in range(2):
        extended = padded(state, (("space", 2),), 2)
        state = advance(extended, wind_field[step_index])
    capacity = obs_index.shape[0]
    raveled_vector = state.reshape(member_count, -1)
    local_obs = jnp.take(raveled_vector, obs_index, axis=1)
    slot_number = jnp.arange(capacity, dtype=jnp.int32)
    slot_weight = obs_weight * (slot_number < obs_count[0]).astype(jnp.float32)
    gathered = lax.all_gather(local_obs, "mem", axis=0, tiled=True)
    gram, drive = shard_terms(gathered, slot_weight, obs_value)
    gram, drive = lax.psum((gram, drive), "space")
    transform = ensemble_weights(gram, drive)
    transform_rows = transform.T
    block = lax.all_to_all(state, "mem", split_axis=3, concat_axis=0, tiled=True)
    replica_centroid = jnp.sum(block, 0) / REPLICA_COUNT
    replica_departure = (block - replica_centroid).astype(jnp.bfloat16)
    posterior_correction = jnp.dot(
        transform_rows,
        replica_departure.reshape(REPLICA_COUNT, -1),
        preferred_element_type=jnp.float32,
    )
    analysed = posterior_correction.reshape(block.shape) + replica_centroid
    return lax.all_to_all(analysed, "mem", split_axis=0, concat_axis=3, tiled=True)


BF = jnp.bfloat16
F32 = jnp.float32
PAD = 128


def vmem():
    return pl.BlockSpec(memory_space=pltpu.VMEM)


def smem():
    return pl.BlockSpec(memory_space=pltpu.SMEM)


def hbm():
    return pl.BlockSpec(memory_space=pltpu.MemorySpace.HBM)


def params():
    return pltpu.CompilerParams(vmem_limit_bytes=44 * 1024 * 1024)


def cost(touched):
    return pl.CostEstimate(flops=touched, bytes_accessed=touched, transcendentals=0)


def blank_edges(rows):
    width = rows.shape[2]
    for r in (0, 1, 10, 11):
        rows[r] = jnp.zeros((16, width), F32)
    for r in range(2, 10):
        rows[r, :, width - PAD :] = jnp.zeros((16, PAD), F32)


def pack_kernel(field, pos, prior, wind, turned, pay_a, pay_b, state, edge, sems):
    load = pltpu.make_async_copy(prior.at[:, field], state, sems.at[0])
    load.start()
    if field == 0:
        winds = pltpu.make_async_copy(wind.at[0], edge, sems.at[1])
        winds.start()
    even = (pos[0] % 2) == 0
    start_a = jnp.where(even, 4, 0)
    start_b = 4 - start_a
    if field == 0:
        winds.wait()
        first = jnp.concatenate([edge[0, 0:2], edge[1, 0:2]], 0)
        last = jnp.concatenate([edge[0, 6:8], edge[1, 6:8]], 0)
        first_high = first.astype(BF).astype(F32)
        last_high = last.astype(BF).astype(F32)
        first = jnp.concatenate([first_high, first - first_high], 0)
        last = jnp.concatenate([last_high, last - last_high], 0)
        pay_a[64:72, :] = jnp.where(even, last, first).astype(BF)
        pay_b[64:72, :] = jnp.where(even, first, last).astype(BF)
    load.wait()
    cols = state.shape[2]
    turned[2:10, :, :cols] = jnp.swapaxes(state[...], 0, 1)
    for r in range(4):
        pay_a[r * 16 : r * 16 + 16, :] = turned[2 + start_a + r, :, :cols].astype(BF)
        pay_b[r * 16 : r * 16 + 16, :] = turned[2 + start_b + r, :, :cols].astype(BF)
    blank_edges(turned)


def maps_kernel(tiles, pos, index, count, weight, value, root_map, value_map):
    slots = index.shape[1]
    n = index[...]
    used = lax.broadcasted_iota(jnp.int32, (1, slots), 1) < count[0]
    root = jnp.where(used, jnp.sqrt(weight[...]), 0.0)
    rooted = root * value[...]
    block = n // 128
    row = (block // tiles) % 8
    cell = (block // (tiles * 8)) * (2 * tiles) + (row % 2) * tiles + block % tiles
    cell = jnp.where(row // 2 == pos[2], cell, -1)
    lane = n % 128
    hit = lax.broadcasted_iota(jnp.int32, (4 * tiles, slots), 0) == cell
    hit = jnp.where(hit, 1.0, 0.0).astype(BF)
    lane_hit = lax.broadcasted_iota(jnp.int32, (128, slots), 0) == lane
    pieces = []
    for v in (root, rooted):
        high = v.astype(BF).astype(F32)
        for part in (high, v - high):
            pieces.append(jnp.where(lane_hit, part, 0.0).astype(BF))
    spread = jnp.concatenate(pieces, 0)
    out = lax.dot_general(
        hit, spread, (((1,), (1,)), ((), ())), preferred_element_type=F32
    )
    root_map[...] = out[:, 0:128] + out[:, 128:256]
    value_map[...] = out[:, 256:384] + out[:, 384:512]


def stencil_row(rows, wind_r, wind_c, nu):
    south_two, south_one, center, north_one, north_two = rows
    width = [v for v in rows if v is not None][0].shape[1]
    keep = width - PAD

    def less(a, b):
        if a is None:
            return None if b is None else -b
        return a if b is None else a - b

    def more(a, b):
        if a is None or b is None:
            return b if a is None else a
        return a + b

    rows = [None if v is None else v[:, :keep] for v in rows]
    one = less(rows[3], rows[1])
    grad_r = less(None if one is None else 8.0 * one, less(rows[4], rows[0]))
    ring = more(rows[3], rows[1])
    out = -(wind_r * grad_r)
    if center is not None:
        east_one = pltpu.roll(center, width - 1, 1)
        west_one = pltpu.roll(center, 1, 1)
        east_two = pltpu.roll(center, width - 2, 1)
        west_two = pltpu.roll(center, 2, 1)
        grad_c = 8.0 * (east_one - west_one) - (east_two - west_two)
        ring = more(ring, (east_one + west_one)[:, :keep])
        out = (1.0 - 4.0 * nu) * rows[2] + out - wind_c * grad_c[:, :keep]
    return out if ring is None else out + nu * ring


TWELFTH = 1.0 / 12.0


def pre_kernel(nu, turned, wind, out, mid, wide):
    cols = out.shape[2]
    blank_edges(mid)
    for step in range(2):
        for c in range(2):
            for r in range(8):
                wide[step, c, r] = jnp.broadcast_to(wind[step, c, r : r + 1] * TWELFTH, (8, cols))

    def first_step(r, carry):
        for g in range(2):
            span = pl.ds(g * 8, 8)
            rows = [turned[r + i, span, :] for i in range(5)]
            mid[r + 2, span, :cols] = stencil_row(rows, wide[0, 0, r], wide[0, 1, r], nu)
        return carry

    lax.fori_loop(0, 8, first_step, 0)

    def second_step(r, carry):
        for g in range(2):
            span = pl.ds(g * 8, 8)
            rows = [mid[r + i, span, :] for i in range(5)]
            out[r, span, :] = stencil_row(rows, wide[1, 0, r], wide[1, 1, r], nu)
        return carry

    lax.fori_loop(0, 8, second_step, 0)


def post_kernel(
    nu, pos, turned, begun, recv_a, recv_b, wind_a, wind_b, wind, out_all, out_near, out_far,
    halo, delta
):
    cols = begun.shape[2]
    even = (pos[0] % 2) == 0
    start_a = jnp.where(even, 4, 0)
    start_b = 4 - start_a
    blank = jnp.zeros((16, PAD), F32)
    for r in range(8):
        halo[r, :, cols:] = blank
        delta[r, :, cols:] = blank
    for r in range(4):
        halo[start_a + r, :, :cols] = recv_a[r * 16 : r * 16 + 16, :].astype(F32)
        halo[start_b + r, :, :cols] = recv_b[r * 16 : r * 16 + 16, :].astype(F32)
    got_a = wind_a[64:72, :].astype(F32)
    got_a = got_a[0:4] + got_a[4:8]
    got_b = wind_b[64:72, :].astype(F32)
    got_b = got_b[0:4] + got_b[4:8]
    top = jnp.where(pos[0] == 0, 0.0, 1.0)
    bottom = jnp.where(pos[0] == pos[1] - 1, 0.0, 1.0)
    before = jnp.where(even, got_b, got_a) * TWELFTH
    after = jnp.where(even, got_a, got_b) * TWELFTH

    def broad(row):
        return jnp.broadcast_to(row, (8, cols))

    def own_wind(step, c, r):
        return broad(wind[step, c, r : r + 1] * TWELFTH)

    for g in range(2):
        span = slice(g * 8, g * 8 + 8)
        h = lambda i: halo[i, span, :]
        x = lambda r: turned[2 + r, span, :]
        for i in range(2):
            rows = [h(0), h(1), h(2), h(3), x(0)] if i == 0 else [h(1), h(2), h(3), x(0), x(1)]
            value = stencil_row(rows, broad(before[i : i + 1]), broad(before[2 + i : 3 + i]), nu)
            delta[i, span, :cols] = value * top
            rows = [x(6), x(7), h(4), h(5), h(6)] if i == 0 else [x(7), h(4), h(5), h(6), h(7)]
            value = stencil_row(rows, broad(after[i : i + 1]), broad(after[2 + i : 3 + i]), nu)
            delta[6 + i, span, :cols] = value * bottom
        near = (
            (2, 0, [h(2), h(3), None, None, None]),
            (3, 1, [h(3), None, None, None, None]),
            (4, 6, [None, None, None, None, h(4)]),
            (5, 7, [None, None, None, h(4), h(5)]),
        )
        for at, r, rows in near:
            delta[at, span, :cols] = stencil_row(rows, own_wind(0, 0, r), None, nu)

    for r in range(8):
        both = []
        for g in range(2):
            span = slice(g * 8, g * 8 + 8)
            rows = []
            for i in range(r - 2, r + 3):
                if i <= 1 and r <= 3:
                    rows.append(delta[i + 2, span, :])
                elif i >= 6 and r >= 4:
                    rows.append(delta[i - 2, span, :])
                else:
                    rows.append(None)
            center = rows[2] is not None
            value = stencil_row(
                rows, own_wind(1, 0, r), own_wind(1, 1, r) if center else None, nu
            )
            both.append(begun[r, span, :] + value)
        out_all[r] = jnp.concatenate(both, 0).astype(BF)
    base = (pos[2] // 2) * 4
    for r in range(4):
        out_near[r] = out_all[base + r]
        out_far[r] = out_all[4 - base + r]


def gram_sum(field, pos, own, mate, far, diag, root_map, value_map, spread):
    tiles = own.shape[2] // 128
    spread[4] = jnp.zeros(spread.shape[1:], BF)
    half = 2 * (pos[2] % 2)
    for r in range(2):
        row = 2 * pos[2] + r
        for t in range(tiles):
            cut = slice(t * 128, (t + 1) * 128)
            at = (field * 2 + r) * tiles + t
            into = slice((r * tiles + t) * 128, (r * tiles + t + 1) * 128)
            parts = [
                own[row, :, cut].astype(F32),
                mate[row, :, cut].astype(F32),
                far[half + r, :, cut].astype(F32),
                diag[half + r, :, cut].astype(F32),
            ]
            total = (parts[0] + parts[1]) + (parts[2] + parts[3])
            mean = jnp.sum(total, 0, keepdims=True) * (1.0 / REPLICA_COUNT)
            root = root_map[at : at + 1, :]
            gap = value_map[at : at + 1, :] - root * mean
            for g in range(4):
                spread[jnp.bitwise_xor(pos[2], g), :, into] = ((parts[g] - mean) * root).astype(BF)
            high = gap.astype(BF).astype(F32)
            pair = jnp.concatenate([high, gap - high, jnp.zeros((14, 128), F32)], 0)
            spread[4, :, into] = pair.astype(BF)
    cells = spread.shape[2]
    left = spread[...].reshape(80, cells)
    right = spread[0:4].reshape(64, cells)
    return lax.dot_general(
        left, right, (((1,), (1,)), ((), ())), preferred_element_type=F32
    )


def gram_first(pos, own, mate, far, diag, root_map, value_map, out, spread):
    out[...] = gram_sum(0, pos, own, mate, far, diag, root_map, value_map, spread)


def gram_second(pos, own, mate, far, diag, root_map, value_map, part, out, spread):
    out[...] = part[...] + gram_sum(1, pos, own, mate, far, diag, root_map, value_map, spread)


def exact(a, b):
    return jnp.dot(a, b, precision=lax.Precision.HIGHEST, preferred_element_type=F32)


def weights_kernel(pos, one, two, out, keep):
    total = one[...] + two[...]
    gram = total[0:64]
    drive = total[64:65] + total[65:66]
    row = lax.broadcasted_iota(jnp.int32, (64, 64), 0)
    col = lax.broadcasted_iota(jnp.int32, (64, 64), 1)
    ident = jnp.where(row == col, 1.0, 0.0)
    system = (REPLICA_COUNT - 1.0) * ident + gram
    square = jnp.sum(jnp.sum(system * system, 1, keepdims=True), 0, keepdims=True)
    scale = jnp.sqrt(square)
    root = system / scale
    inverse_root = ident
    for turn in range(NS_ITERS):
        if turn == 0:
            middle = 0.5 * (3.0 * ident - root)
            inverse_next = middle
        else:
            middle = 0.5 * (3.0 * ident - exact(inverse_root, root))
            inverse_next = exact(middle, inverse_root)
        if turn < NS_ITERS - 1:
            root = exact(root, middle)
        inverse_root = inverse_next
    half = inverse_root / jnp.sqrt(scale)
    drive8 = jnp.broadcast_to(drive, (8, 64))
    mean_weight = exact(exact(drive8, half), half)[0:1]
    transform_t = (mean_weight + (REPLICA_COUNT - 1.0) ** 0.5 * half).astype(BF).astype(F32)
    total_t = jnp.sum(transform_t, 1, keepdims=True)
    keep[...] = transform_t + (1.0 - total_t) * (1.0 / REPLICA_COUNT)
    mine = keep[pl.ds(pl.multiple_of(pos[2] * 16, 16), 16), :]
    swap1 = jnp.concatenate([mine[:, 16:32], mine[:, 0:16], mine[:, 48:64], mine[:, 32:48]], 1)
    mine = jnp.where((pos[2] % 2) == 1, swap1, mine)
    swap2 = jnp.concatenate([mine[:, 32:64], mine[:, 0:32]], 1)
    mine = jnp.where(pos[2] >= 2, swap2, mine)
    high = mine.astype(BF).astype(F32)
    out[...] = jnp.concatenate([high, mine - high], 0).astype(BF)


def final_kernel(
    pos, weights, own_0, own_1, mate_0, mate_1, far_0, far_1, diag_0, diag_1,
    near_0, near_1, mate_near_0, mate_near_1, out, keep, ready, sems
):
    m = weights[...]
    fields = (
        (own_0, mate_0, far_0, diag_0, near_0, mate_near_0),
        (own_1, mate_1, far_1, diag_1, near_1, mate_near_1),
    )
    base = (pos[2] // 2) * 4
    copies = []
    for f in range(2):
        own, mate, far, diag, near, mate_near = fields[f]
        for r in range(8):
            row = base + r if r < 4 else 4 - base + r - 4
            other = [far[r], diag[r]] if r < 4 else [near[r - 4], mate_near[r - 4]]
            state = jnp.concatenate([own[row], mate[row]] + other, 0)
            both = jnp.dot(m, state, preferred_element_type=F32)
            keep[row] = both[0:16] + both[16:32]
        ready[f] = jnp.swapaxes(keep[...], 0, 1)
        copies.append(pltpu.make_async_copy(ready.at[f], out.at[:, f], sems.at[f]))
        copies[f].start()
    for f in range(2):
        copies[f].wait()


def local(prior_replicas, wind_field, obs_index, obs_count, obs_value, obs_weight):
    cols = prior_replicas.shape[3]
    tiles = cols // 128
    strips = lax.axis_size("space")
    here = lax.axis_index("space")
    group = lax.axis_index("mem")
    pos = jnp.stack([here, jnp.int32(strips), group]).astype(jnp.int32)
    shape = jax.ShapeDtypeStruct
    pairs_a = [(i, i ^ 1) for i in range(strips)]
    pairs_b = [(i, i + 1) for i in range(1, strips - 1, 2)]
    pairs_b = pairs_b + [(j, i) for i, j in pairs_b]

    def swap(value, bits):
        return lax.ppermute(value, "mem", [(i, i ^ bits) for i in range(4)])

    prior_here = pltpu.with_memory_space_constraint(prior_replicas, pltpu.MemorySpace.HBM)
    wind_here = pltpu.with_memory_space_constraint(wind_field, pltpu.MemorySpace.HBM)
    turned = []
    recv = []
    for f in range(2):
        height = 72 if f == 0 else 64
        rows, pay_a, pay_b = pl.pallas_call(
            functools.partial(pack_kernel, f),
            name="pack",
            cost_estimate=cost(40 * 16 * cols * 4),
            in_specs=[smem(), hbm(), hbm()],
            out_specs=[vmem()] * 3,
            out_shape=[shape((12, 16, cols + PAD), F32)] + [shape((height, cols), BF)] * 2,
            scratch_shapes=[
                pltpu.VMEM((16, 8, cols), F32),
                pltpu.VMEM((2, 8, cols), F32),
                pltpu.SemaphoreType.DMA((2,)),
            ],
            compiler_params=params(),
        )(pos, prior_here, wind_here)
        turned.append(rows)
        recv.append([lax.ppermute(pay_a, "space", pairs_a), lax.ppermute(pay_b, "space", pairs_b)])

    slots = obs_index.shape[0]
    root_map, value_map = pl.pallas_call(
        functools.partial(maps_kernel, tiles),
        name="maps",
        cost_estimate=cost(slots * 1024 * 4),
        in_specs=[smem(), vmem(), smem(), vmem(), vmem()],
        out_specs=[vmem()] * 2,
        out_shape=[shape((4 * tiles, 128), F32)] * 2,
        compiler_params=params(),
    )(
        pos,
        obs_index.reshape(1, slots),
        obs_count,
        obs_weight.reshape(1, slots),
        obs_value.reshape(1, slots),
    )
    begun = [
        pl.pallas_call(
            functools.partial(pre_kernel, DIFFUSION[f]),
            name="pre",
            cost_estimate=cost(150 * 16 * cols * 4),
            in_specs=[vmem()] * 2,
            out_specs=vmem(),
            out_shape=shape((8, 16, cols), F32),
            scratch_shapes=[
                pltpu.VMEM((12, 16, cols + PAD), F32),
                pltpu.VMEM((2, 2, 8, 8, cols), F32),
            ],
            compiler_params=params(),
        )(turned[f], wind_field)
        for f in range(2)
    ]

    state = []
    got = []
    for f in range(2):
        every, near, far = pl.pallas_call(
            functools.partial(post_kernel, DIFFUSION[f]),
            name="post",
            cost_estimate=cost(100 * 16 * cols * 4),
            in_specs=[smem()] + [vmem()] * 7,
            out_specs=[vmem()] * 3,
            out_shape=[
                shape((8, 16, cols), BF),
                shape((4, 16, cols), BF),
                shape((4, 16, cols), BF),
            ],
            scratch_shapes=[
                pltpu.VMEM((8, 16, cols + PAD), F32),
                pltpu.VMEM((8, 16, cols + PAD), F32),
            ],
            compiler_params=params(),
        )(pos, turned[f], begun[f], recv[f][0], recv[f][1], recv[0][0], recv[0][1], wind_field)
        if f == 1:
            got[0][0], every, far = lax.optimization_barrier((got[0][0], every, far))
        state.append((every, near))
        got.append([swap(far, 2), swap(every, 1)])
    got[0].append(swap(got[0][0], 1))

    def gram(kernel, f, extra):
        return pl.pallas_call(
            kernel,
            name="gram",
            cost_estimate=cost(24 * 64 * cols * 2),
            in_specs=[smem()] + [vmem()] * (6 + len(extra)),
            out_specs=vmem(),
            out_shape=shape((80, 64), F32),
            scratch_shapes=[pltpu.VMEM((5, 16, 2 * cols), BF)],
            compiler_params=params(),
        )(pos, state[f][0], got[f][1], got[f][0], got[f][2], root_map, value_map, *extra)

    part = gram(gram_first, 0, [])
    got[1][0], part, near_0, near_1 = lax.optimization_barrier(
        (got[1][0], part, state[0][1], state[1][1])
    )
    near_0 = swap(near_0, 2)
    near_1 = swap(near_1, 2)
    got[1].append(swap(got[1][0], 1))
    part = gram(gram_second, 1, [part])

    rounds = [("mem", 1)]
    bit = 1
    while bit < strips:
        rounds.append(("space", bit))
        bit *= 2
    rounds.append(("mem", 2))
    other = None
    for axis, bits in rounds:
        if other is not None:
            part = part + other
        size = lax.axis_size(axis)
        other = lax.ppermute(part, axis, [(i, i ^ bits) for i in range(size)])
    near_0_late, near_1_late, _ = lax.optimization_barrier((near_0, near_1, other))
    mate_near_0 = swap(near_0_late, 1)
    mate_near_1 = swap(near_1_late, 1)

    weights = pl.pallas_call(
        weights_kernel,
        name="weights",
        cost_estimate=cost(400 * 64 * 128 * 4),
        in_specs=[smem(), vmem(), vmem()],
        out_specs=vmem(),
        out_shape=shape((32, 64), BF),
        scratch_shapes=[pltpu.VMEM((64, 64), F32)],
        compiler_params=params(),
    )(pos, part, other)

    return pl.pallas_call(
        final_kernel,
        name="final",
        cost_estimate=cost(100 * 16 * cols * 4),
        in_specs=[smem()] + [vmem()] * 13,
        out_specs=hbm(),
        out_shape=shape(prior_replicas.shape, F32),
        scratch_shapes=[
            pltpu.VMEM((8, 16, cols), F32),
            pltpu.VMEM((2, 16, 8, cols), F32),
            pltpu.SemaphoreType.DMA((2,)),
        ],
        compiler_params=params(),
    )(
        pos, weights, state[0][0], state[1][0], got[0][1], got[1][1], got[0][0], got[1][0],
        got[0][2], got[1][2], near_0, near_1, mate_near_0, mate_near_1,
    )


def solution(mesh):
    in_specs = (
        P(("parts", "mem"), None, "space", None),
        P("parts", None, "space", None),
        P(("parts", "space")),
        P(("parts", "space")),
        P(("parts", "space")),
        P(("parts", "space")),
    )
    out_specs = P(("parts", "mem"), None, "space", None)
    strips = mesh.shape["space"]
    fast = mesh.shape["mem"] == 4 and strips > 1 and strips & (strips - 1) == 0
    body = local if fast else local_generic
    return jax.shard_map(body, mesh=mesh, in_specs=in_specs, out_specs=out_specs, check_vma=False)
```

```python
import functools

import jax
import jax.numpy as jnp
from jax import lax
from jax.experimental import pallas as pl
from jax.experimental.pallas import tpu as pltpu
from jax.sharding import PartitionSpec as P

REPLICA_COUNT = 64
NS_ITERS = 5


DIFFUSION = (0.05, 0.15)


def padded(value, sides, width):
    for axis, dim in sides:
        peers, length = (lax.axis_size(axis), value.shape[dim])
        up = [(i, (i + 1) % peers) for i in range(peers - 1)]
        down = [(j, i) for i, j in up]
        last = lax.slice_in_dim(value, length - width, length, axis=dim)
        initial = lax.slice_in_dim(value, 0, width, axis=dim)
        before = lax.ppermute(last, axis, up)
        after = lax.ppermute(initial, axis, down)
        value = jnp.concatenate([before, value, after], axis=dim)
    return value


def shift_columns(field, offset):
    width = field.shape[-1]
    blank = jnp.zeros(field.shape[:-1] + (abs(offset),), field.dtype)
    if offset > 0:
        return jnp.concatenate([field[..., offset:], blank], -1)
    return jnp.concatenate([blank, field[..., : width + offset]], -1)


def advance(extended, wind_rows):
    center = extended[:, :, 2:-2]
    north_one = extended[:, :, 3:-1]
    south_one = extended[:, :, 1:-3]
    north_two = extended[:, :, 4:]
    south_two = extended[:, :, :-4]
    east_one = shift_columns(center, 1)
    west_one = shift_columns(center, -1)
    east_two = shift_columns(center, 2)
    west_two = shift_columns(center, -2)
    grad_row = (8.0 * (north_one - south_one) - (north_two - south_two)) / 12.0
    grad_col = (8.0 * (east_one - west_one) - (east_two - west_two)) / 12.0
    laplace = north_one + south_one + east_one + west_one - 4.0 * center
    diffusion = jnp.array(DIFFUSION, jnp.float32).reshape(2, 1, 1)
    return center - wind_rows[0] * grad_row - wind_rows[1] * grad_col + diffusion * laplace


def shard_terms(observed, slot_weight, obs_value):
    obs_mean = jnp.sum(observed, 0) / REPLICA_COUNT
    obs_anomaly = observed - obs_mean
    weighted = obs_anomaly * slot_weight
    gram = jnp.dot(
        weighted, obs_anomaly.T, precision=lax.Precision.HIGHEST, preferred_element_type=jnp.float32
    )
    drive = jnp.dot(
        weighted,
        obs_value - obs_mean,
        precision=lax.Precision.HIGHEST,
        preferred_element_type=jnp.float32,
    )
    return (gram, drive)


def ensemble_weights(gram, drive):
    ident = jnp.eye(REPLICA_COUNT, dtype=jnp.float32)
    system = (REPLICA_COUNT - 1.0) * ident + gram
    scale = jnp.sqrt(jnp.sum(system * system))

    def newton_turn(turn, carry):
        root, inverse_root = carry
        middle_term = 0.5 * (
            3.0 * ident
            - jnp.dot(
                inverse_root,
                root,
                precision=lax.Precision.HIGHEST,
                preferred_element_type=jnp.float32,
            )
        )
        root = jnp.dot(
            root, middle_term, precision=lax.Precision.HIGHEST, preferred_element_type=jnp.float32
        )
        inverse_root = jnp.dot(
            middle_term,
            inverse_root,
            precision=lax.Precision.HIGHEST,
            preferred_element_type=jnp.float32,
        )
        return (root, inverse_root)

    root, inverse_root = lax.fori_loop(0, NS_ITERS, newton_turn, (system / scale, ident))
    half = inverse_root / jnp.sqrt(scale)
    precision_matrix = jnp.dot(
        half, half, precision=lax.Precision.HIGHEST, preferred_element_type=jnp.float32
    )
    mean_weight = jnp.dot(
        precision_matrix, drive, precision=lax.Precision.HIGHEST, preferred_element_type=jnp.float32
    )
    spread = jnp.sqrt(REPLICA_COUNT - 1.0) * half
    return (mean_weight[:, None] + spread).astype(jnp.bfloat16)


def local_generic(prior_replicas, wind_field, obs_index, obs_count, obs_value, obs_weight):
    member_count, field_count, row_count, col_count = prior_replicas.shape
    state = prior_replicas
    for step_index in range(2):
        extended = padded(state, (("space", 2),), 2)
        state = advance(extended, wind_field[step_index])
    capacity = obs_index.shape[0]
    raveled_vector = state.reshape(member_count, -1)
    local_obs = jnp.take(raveled_vector, obs_index, axis=1)
    slot_number = jnp.arange(capacity, dtype=jnp.int32)
    slot_weight = obs_weight * (slot_number < obs_count[0]).astype(jnp.float32)
    gathered = lax.all_gather(local_obs, "mem", axis=0, tiled=True)
    gram, drive = shard_terms(gathered, slot_weight, obs_value)
    gram, drive = lax.psum((gram, drive), "space")
    transform = ensemble_weights(gram, drive)
    transform_rows = transform.T
    block = lax.all_to_all(state, "mem", split_axis=3, concat_axis=0, tiled=True)
    replica_centroid = jnp.sum(block, 0) / REPLICA_COUNT
    replica_departure = (block - replica_centroid).astype(jnp.bfloat16)
    posterior_correction = jnp.dot(
        transform_rows,
        replica_departure.reshape(REPLICA_COUNT, -1),
        preferred_element_type=jnp.float32,
    )
    analysed = posterior_correction.reshape(block.shape) + replica_centroid
    return lax.all_to_all(analysed, "mem", split_axis=0, concat_axis=3, tiled=True)


BF = jnp.bfloat16
F32 = jnp.float32
PAD = 128


def vmem():
    return pl.BlockSpec(memory_space=pltpu.VMEM)


def smem():
    return pl.BlockSpec(memory_space=pltpu.SMEM)


def hbm():
    return pl.BlockSpec(memory_space=pltpu.MemorySpace.HBM)


def params():
    return pltpu.CompilerParams(vmem_limit_bytes=44 * 1024 * 1024)


def cost(touched):
    return pl.CostEstimate(flops=touched, bytes_accessed=touched, transcendentals=0)


def blank_edges(rows):
    width = rows.shape[2]
    for r in (0, 1, 10, 11):
        rows[r] = jnp.zeros((16, width), F32)
    for r in range(2, 10):
        rows[r, :, width - PAD :] = jnp.zeros((16, PAD), F32)


def pack_kernel(field, pos, prior, wind, turned, pay_a, pay_b, state, edge, sems):
    load = pltpu.make_async_copy(prior.at[:, field], state, sems.at[0])
    load.start()
    if field == 0:
        winds = pltpu.make_async_copy(wind.at[0], edge, sems.at[1])
        winds.start()
    even = (pos[0] % 2) == 0
    start_a = jnp.where(even, 4, 0)
    start_b = 4 - start_a
    if field == 0:
        winds.wait()
        first = jnp.concatenate([edge[0, 0:2], edge[1, 0:2]], 0)
        last = jnp.concatenate([edge[0, 6:8], edge[1, 6:8]], 0)
        first_high = first.astype(BF).astype(F32)
        last_high = last.astype(BF).astype(F32)
        first = jnp.concatenate([first_high, first - first_high], 0)
        last = jnp.concatenate([last_high, last - last_high], 0)
        pay_a[64:72, :] = jnp.where(even, last, first).astype(BF)
        pay_b[64:72, :] = jnp.where(even, first, last).astype(BF)
    load.wait()
    cols = state.shape[2]
    turned[2:10, :, :cols] = jnp.swapaxes(state[...], 0, 1)
    for r in range(4):
        pay_a[r * 16 : r * 16 + 16, :] = turned[2 + start_a + r, :, :cols].astype(BF)
        pay_b[r * 16 : r * 16 + 16, :] = turned[2 + start_b + r, :, :cols].astype(BF)
    blank_edges(turned)


def maps_kernel(tiles, pos, index, count, weight, value, root_map, value_map):
    slots = index.shape[1]
    n = index[...]
    used = lax.broadcasted_iota(jnp.int32, (1, slots), 1) < count[0]
    root = jnp.where(used, jnp.sqrt(weight[...]), 0.0)
    rooted = root * value[...]
    block = n // 128
    row = (block // tiles) % 8
    cell = (block // (tiles * 8)) * (2 * tiles) + (row % 2) * tiles + block % tiles
    cell = jnp.where(row // 2 == pos[2], cell, -1)
    lane = n % 128
    hit = lax.broadcasted_iota(jnp.int32, (4 * tiles, slots), 0) == cell
    hit = jnp.where(hit, 1.0, 0.0).astype(BF)
    lane_hit = lax.broadcasted_iota(jnp.int32, (128, slots), 0) == lane
    pieces = []
    for v in (root, rooted):
        high = v.astype(BF).astype(F32)
        for part in (high, v - high):
            pieces.append(jnp.where(lane_hit, part, 0.0).astype(BF))
    spread = jnp.concatenate(pieces, 0)
    out = lax.dot_general(
        hit, spread, (((1,), (1,)), ((), ())), preferred_element_type=F32
    )
    root_map[...] = out[:, 0:128] + out[:, 128:256]
    value_map[...] = out[:, 256:384] + out[:, 384:512]


def stencil_row(rows, wind_r, wind_c, nu):
    south_two, south_one, center, north_one, north_two = rows
    width = [v for v in rows if v is not None][0].shape[1]
    keep = width - PAD

    def less(a, b):
        if a is None:
            return None if b is None else -b
        return a if b is None else a - b

    def more(a, b):
        if a is None or b is None:
            return b if a is None else a
        return a + b

    rows = [None if v is None else v[:, :keep] for v in rows]
    one = less(rows[3], rows[1])
    grad_r = less(None if one is None else 8.0 * one, less(rows[4], rows[0]))
    ring = more(rows[3], rows[1])
    out = -(wind_r * grad_r)
    if center is not None:
        east_one = pltpu.roll(center, width - 1, 1)
        west_one = pltpu.roll(center, 1, 1)
        east_two = pltpu.roll(center, width - 2, 1)
        west_two = pltpu.roll(center, 2, 1)
        grad_c = 8.0 * (east_one - west_one) - (east_two - west_two)
        ring = more(ring, (east_one + west_one)[:, :keep])
        out = (1.0 - 4.0 * nu) * rows[2] + out - wind_c * grad_c[:, :keep]
    return out if ring is None else out + nu * ring


TWELFTH = 1.0 / 12.0


def pre_kernel(nu, turned, wind, out, mid, wide):
    cols = out.shape[2]
    blank_edges(mid)
    for step in range(2):
        for c in range(2):
            for r in range(8):
                wide[step, c, r] = jnp.broadcast_to(wind[step, c, r : r + 1] * TWELFTH, (8, cols))

    def first_step(r, carry):
        for g in range(2):
            span = pl.ds(g * 8, 8)
            rows = [turned[r + i, span, :] for i in range(5)]
            mid[r + 2, span, :cols] = stencil_row(rows, wide[0, 0, r], wide[0, 1, r], nu)
        return carry

    lax.fori_loop(0, 8, first_step, 0)

    def second_step(r, carry):
        for g in range(2):
            span = pl.ds(g * 8, 8)
            rows = [mid[r + i, span, :] for i in range(5)]
            out[r, span, :] = stencil_row(rows, wide[1, 0, r], wide[1, 1, r], nu)
        return carry

    lax.fori_loop(0, 8, second_step, 0)


def post_kernel(nu, pos, turned, begun, recv_a, recv_b, wind_a, wind_b, wind, *refs):
    out_all, out_near, out_far, halo, delta = refs[-5:]
    cols = begun.shape[2]
    even = (pos[0] % 2) == 0
    start_a = jnp.where(even, 4, 0)
    start_b = 4 - start_a
    blank = jnp.zeros((16, PAD), F32)
    for r in range(8):
        halo[r, :, cols:] = blank
        delta[r, :, cols:] = blank
    for r in range(4):
        halo[start_a + r, :, :cols] = recv_a[r * 16 : r * 16 + 16, :].astype(F32)
        halo[start_b + r, :, :cols] = recv_b[r * 16 : r * 16 + 16, :].astype(F32)
    got_a = wind_a[64:72, :].astype(F32)
    got_a = got_a[0:4] + got_a[4:8]
    got_b = wind_b[64:72, :].astype(F32)
    got_b = got_b[0:4] + got_b[4:8]
    top = jnp.where(pos[0] == 0, 0.0, 1.0)
    bottom = jnp.where(pos[0] == pos[1] - 1, 0.0, 1.0)
    before = jnp.where(even, got_b, got_a) * TWELFTH
    after = jnp.where(even, got_a, got_b) * TWELFTH

    def broad(row):
        return jnp.broadcast_to(row, (8, cols))

    def own_wind(step, c, r):
        return broad(wind[step, c, r : r + 1] * TWELFTH)

    for g in range(2):
        span = slice(g * 8, g * 8 + 8)
        h = lambda i: halo[i, span, :]
        x = lambda r: turned[2 + r, span, :]
        for i in range(2):
            rows = [h(0), h(1), h(2), h(3), x(0)] if i == 0 else [h(1), h(2), h(3), x(0), x(1)]
            value = stencil_row(rows, broad(before[i : i + 1]), broad(before[2 + i : 3 + i]), nu)
            delta[i, span, :cols] = value * top
            rows = [x(6), x(7), h(4), h(5), h(6)] if i == 0 else [x(7), h(4), h(5), h(6), h(7)]
            value = stencil_row(rows, broad(after[i : i + 1]), broad(after[2 + i : 3 + i]), nu)
            delta[6 + i, span, :cols] = value * bottom
        near = (
            (2, 0, [h(2), h(3), None, None, None]),
            (3, 1, [h(3), None, None, None, None]),
            (4, 6, [None, None, None, None, h(4)]),
            (5, 7, [None, None, None, h(4), h(5)]),
        )
        for at, r, rows in near:
            delta[at, span, :cols] = stencil_row(rows, own_wind(0, 0, r), None, nu)

    for r in range(8):
        both = []
        for g in range(2):
            span = slice(g * 8, g * 8 + 8)
            rows = []
            for i in range(r - 2, r + 3):
                if i <= 1 and r <= 3:
                    rows.append(delta[i + 2, span, :])
                elif i >= 6 and r >= 4:
                    rows.append(delta[i - 2, span, :])
                else:
                    rows.append(None)
            center = rows[2] is not None
            value = stencil_row(
                rows, own_wind(1, 0, r), own_wind(1, 1, r) if center else None, nu
            )
            both.append(begun[r, span, :] + value)
        out_all[r] = jnp.concatenate(both, 0).astype(BF)
    base = (pos[2] // 2) * 4
    if len(refs) == 6:
        out_near[0:4] = refs[0][...]
    for r in range(4):
        out_near[out_near.shape[0] - 4 + r] = out_all[base + r]
        out_far[r] = out_all[4 - base + r]


def gram_sum(field, pos, own, mate, far, diag, root_map, value_map, spread):
    tiles = own.shape[2] // 128
    spread[4] = jnp.zeros(spread.shape[1:], BF)
    half = 2 * (pos[2] % 2)
    for r in range(2):
        row = 2 * pos[2] + r
        for t in range(tiles):
            cut = slice(t * 128, (t + 1) * 128)
            at = (field * 2 + r) * tiles + t
            into = slice((r * tiles + t) * 128, (r * tiles + t + 1) * 128)
            parts = [
                own[row, :, cut].astype(F32),
                mate[row, :, cut].astype(F32),
                far[half + r, :, cut].astype(F32),
                diag[half + r, :, cut].astype(F32),
            ]
            total = (parts[0] + parts[1]) + (parts[2] + parts[3])
            mean = jnp.sum(total, 0, keepdims=True) * (1.0 / REPLICA_COUNT)
            root = root_map[at : at + 1, :]
            gap = value_map[at : at + 1, :] - root * mean
            for g in range(4):
                spread[jnp.bitwise_xor(pos[2], g), :, into] = ((parts[g] - mean) * root).astype(BF)
            high = gap.astype(BF).astype(F32)
            pair = jnp.concatenate([high, gap - high, jnp.zeros((14, 128), F32)], 0)
            spread[4, :, into] = pair.astype(BF)
    cells = spread.shape[2]
    left = spread[...].reshape(80, cells)
    right = spread[0:4].reshape(64, cells)
    return lax.dot_general(
        left, right, (((1,), (1,)), ((), ())), preferred_element_type=F32
    )


def gram_first(pos, own, mate, far, diag, root_map, value_map, out, spread):
    out[...] = gram_sum(0, pos, own, mate, far, diag, root_map, value_map, spread)


def gram_second(pos, own, mate, far, diag, root_map, value_map, part, out, spread):
    out[...] = part[...] + gram_sum(1, pos, own, mate, far, diag, root_map, value_map, spread)


def exact(a, b):
    return jnp.dot(a, b, precision=lax.Precision.HIGHEST, preferred_element_type=F32)


def weights_kernel(pos, one, two, out, keep):
    total = one[...] + two[...]
    gram = total[0:64]
    drive = total[64:65] + total[65:66]
    row = lax.broadcasted_iota(jnp.int32, (64, 64), 0)
    col = lax.broadcasted_iota(jnp.int32, (64, 64), 1)
    ident = jnp.where(row == col, 1.0, 0.0)
    system = (REPLICA_COUNT - 1.0) * ident + gram
    square = jnp.sum(jnp.sum(system * system, 1, keepdims=True), 0, keepdims=True)
    scale = jnp.sqrt(square)
    root = system / scale
    inverse_root = ident
    for turn in range(NS_ITERS):
        if turn == 0:
            middle = 0.5 * (3.0 * ident - root)
            inverse_next = middle
        else:
            middle = 0.5 * (3.0 * ident - exact(inverse_root, root))
            inverse_next = exact(middle, inverse_root)
        if turn < NS_ITERS - 1:
            root = exact(root, middle)
        inverse_root = inverse_next
    half = inverse_root / jnp.sqrt(scale)
    drive8 = jnp.broadcast_to(drive, (8, 64))
    mean_weight = exact(exact(drive8, half), half)[0:1]
    transform_t = (mean_weight + (REPLICA_COUNT - 1.0) ** 0.5 * half).astype(BF).astype(F32)
    total_t = jnp.sum(transform_t, 1, keepdims=True)
    keep[...] = transform_t + (1.0 - total_t) * (1.0 / REPLICA_COUNT)
    mine = keep[pl.ds(pl.multiple_of(pos[2] * 16, 16), 16), :]
    swap1 = jnp.concatenate([mine[:, 16:32], mine[:, 0:16], mine[:, 48:64], mine[:, 32:48]], 1)
    mine = jnp.where((pos[2] % 2) == 1, swap1, mine)
    swap2 = jnp.concatenate([mine[:, 32:64], mine[:, 0:32]], 1)
    mine = jnp.where(pos[2] >= 2, swap2, mine)
    high = mine.astype(BF).astype(F32)
    out[...] = jnp.concatenate([high, mine - high], 0).astype(BF)


def final_kernel(
    pos, weights, own_0, own_1, mate_0, mate_1, far_0, far_1, diag_0, diag_1,
    near, mate_near, out, keep, ready, sems
):
    m = weights[...]
    fields = ((own_0, mate_0, far_0, diag_0), (own_1, mate_1, far_1, diag_1))
    base = (pos[2] // 2) * 4
    copies = []
    for f in range(2):
        own, mate, far, diag = fields[f]
        for r in range(8):
            row = base + r if r < 4 else 4 - base + r - 4
            other = [far[r], diag[r]] if r < 4 else [near[4 * f + r - 4], mate_near[4 * f + r - 4]]
            state = jnp.concatenate([own[row], mate[row]] + other, 0)
            both = jnp.dot(m, state, preferred_element_type=F32)
            keep[row] = both[0:16] + both[16:32]
        ready[f] = jnp.swapaxes(keep[...], 0, 1)
        copies.append(pltpu.make_async_copy(ready.at[f], out.at[:, f], sems.at[f]))
        copies[f].start()
    for f in range(2):
        copies[f].wait()


def local(prior_replicas, wind_field, obs_index, obs_count, obs_value, obs_weight):
    cols = prior_replicas.shape[3]
    tiles = cols // 128
    strips = lax.axis_size("space")
    here = lax.axis_index("space")
    group = lax.axis_index("mem")
    pos = jnp.stack([here, jnp.int32(strips), group]).astype(jnp.int32)
    shape = jax.ShapeDtypeStruct
    pairs_a = [(i, i ^ 1) for i in range(strips)]
    pairs_b = [(i, i + 1) for i in range(1, strips - 1, 2)]
    pairs_b = pairs_b + [(j, i) for i, j in pairs_b]

    def swap(value, bits):
        return lax.ppermute(value, "mem", [(i, i ^ bits) for i in range(4)])

    prior_here = pltpu.with_memory_space_constraint(prior_replicas, pltpu.MemorySpace.HBM)
    wind_here = pltpu.with_memory_space_constraint(wind_field, pltpu.MemorySpace.HBM)

    def pack(f, when, prior, wind):
        height = 72 if f == 0 else 64
        rows, pay_a, pay_b = pl.pallas_call(
            functools.partial(pack_kernel, f),
            name="pack",
            cost_estimate=cost(40 * 16 * cols * 4),
            in_specs=[smem(), hbm(), hbm()],
            out_specs=[vmem()] * 3,
            out_shape=[shape((12, 16, cols + PAD), F32)] + [shape((height, cols), BF)] * 2,
            scratch_shapes=[
                pltpu.VMEM((16, 8, cols), F32),
                pltpu.VMEM((2, 8, cols), F32),
                pltpu.SemaphoreType.DMA((2,)),
            ],
            compiler_params=params(),
        )(when, prior, wind)
        return rows, lax.ppermute(pay_a, "space", pairs_a), lax.ppermute(pay_b, "space", pairs_b)

    def pre(f, rows):
        return pl.pallas_call(
            functools.partial(pre_kernel, DIFFUSION[f]),
            name="pre",
            cost_estimate=cost(150 * 16 * cols * 4),
            in_specs=[vmem()] * 2,
            out_specs=vmem(),
            out_shape=shape((8, 16, cols), F32),
            scratch_shapes=[
                pltpu.VMEM((12, 16, cols + PAD), F32),
                pltpu.VMEM((2, 2, 8, 8, cols), F32),
            ],
            compiler_params=params(),
        )(rows, wind_field)

    packed = [pack(0, pos, prior_here, wind_here)]
    begun = [pre(0, packed[0][0])]
    later, begun[0] = lax.optimization_barrier((pos, begun[0]))
    packed.append(pack(1, later, prior_here, wind_here))
    begun.append(pre(1, packed[1][0]))
    turned = [v[0] for v in packed]
    recv = [[v[1], v[2]] for v in packed]

    slots = obs_index.shape[0]

    def maps(when):
        return pl.pallas_call(
            functools.partial(maps_kernel, tiles),
            name="maps",
            cost_estimate=cost(slots * 1024 * 4),
            in_specs=[smem(), vmem(), smem(), vmem(), vmem()],
            out_specs=[vmem()] * 2,
            out_shape=[shape((4 * tiles, 128), F32)] * 2,
            compiler_params=params(),
        )(
            when,
            obs_index.reshape(1, slots),
            obs_count,
            obs_weight.reshape(1, slots),
            obs_value.reshape(1, slots),
        )

    root_map, value_map = maps(pos)
    state = []
    got = []
    for f in range(2):
        every, near, far = pl.pallas_call(
            functools.partial(post_kernel, DIFFUSION[f]),
            name="post",
            cost_estimate=cost(100 * 16 * cols * 4),
            in_specs=[smem()] + [vmem()] * (7 + f),
            out_specs=[vmem()] * 3,
            out_shape=[
                shape((8, 16, cols), BF),
                shape((4 + 4 * f, 16, cols), BF),
                shape((4, 16, cols), BF),
            ],
            scratch_shapes=[
                pltpu.VMEM((8, 16, cols + PAD), F32),
                pltpu.VMEM((8, 16, cols + PAD), F32),
            ],
            compiler_params=params(),
        )(
            pos, turned[f], begun[f], recv[f][0], recv[f][1], recv[0][0], recv[0][1], wind_field,
            *[v[1] for v in state]
        )
        if f == 1:
            got[0][0], every, far = lax.optimization_barrier((got[0][0], every, far))
        state.append((every, near))
        got.append([swap(far, 2), swap(every, 1)])
    got[0].append(swap(got[0][0], 1))

    def gram(kernel, f, extra):
        return pl.pallas_call(
            kernel,
            name="gram",
            cost_estimate=cost(24 * 64 * cols * 2),
            in_specs=[smem()] + [vmem()] * (6 + len(extra)),
            out_specs=vmem(),
            out_shape=shape((80, 64), F32),
            scratch_shapes=[pltpu.VMEM((5, 16, 2 * cols), BF)],
            compiler_params=params(),
        )(pos, state[f][0], got[f][1], got[f][0], got[f][2], root_map, value_map, *extra)

    part = gram(gram_first, 0, [])
    part, near = lax.optimization_barrier((part, state[1][1]))
    near = swap(near, 2)
    got[1][0], _ = lax.optimization_barrier((got[1][0], part))
    got[1].append(swap(got[1][0], 1))
    part = gram(gram_second, 1, [part])

    rounds = [("mem", 1)]
    bit = 1
    while bit < strips:
        rounds.append(("space", bit))
        bit *= 2
    rounds.append(("mem", 2))
    other = None
    for axis, bits in rounds:
        if other is not None:
            part = part + other
        size = lax.axis_size(axis)
        other = lax.ppermute(part, axis, [(i, i ^ bits) for i in range(size)])
    near_late, _ = lax.optimization_barrier((near, other))
    mate_near = swap(near_late, 1)

    weights = pl.pallas_call(
        weights_kernel,
        name="weights",
        cost_estimate=cost(400 * 64 * 128 * 4),
        in_specs=[smem(), vmem(), vmem()],
        out_specs=vmem(),
        out_shape=shape((32, 64), BF),
        scratch_shapes=[pltpu.VMEM((64, 64), F32)],
        compiler_params=params(),
    )(pos, part, other)

    return pl.pallas_call(
        final_kernel,
        name="final",
        cost_estimate=cost(100 * 16 * cols * 4),
        in_specs=[smem()] + [vmem()] * 11,
        out_specs=hbm(),
        out_shape=shape(prior_replicas.shape, F32),
        scratch_shapes=[
            pltpu.VMEM((8, 16, cols), F32),
            pltpu.VMEM((2, 16, 8, cols), F32),
            pltpu.SemaphoreType.DMA((2,)),
        ],
        compiler_params=params(),
    )(
        pos, weights, state[0][0], state[1][0], got[0][1], got[1][1], got[0][0], got[1][0],
        got[0][2], got[1][2], near, mate_near,
    )


def solution(mesh):
    in_specs = (
        P(("parts", "mem"), None, "space", None),
        P("parts", None, "space", None),
        P(("parts", "space")),
        P(("parts", "space")),
        P(("parts", "space")),
        P(("parts", "space")),
    )
    out_specs = P(("parts", "mem"), None, "space", None)
    strips = mesh.shape["space"]
    fast = mesh.shape["mem"] == 4 and strips > 1 and strips & (strips - 1) == 0
    body = local if fast else local_generic
    return jax.shard_map(body, mesh=mesh, in_specs=in_specs, out_specs=out_specs, check_vma=False)
```

```python
import functools

import jax
import jax.numpy as jnp
from jax import lax
from jax.experimental import pallas as pl
from jax.experimental.pallas import tpu as pltpu
from jax.sharding import PartitionSpec as P

REPLICA_COUNT = 64
NS_ITERS = 5


DIFFUSION = (0.05, 0.15)


def padded(value, sides, width):
    for axis, dim in sides:
        peers, length = (lax.axis_size(axis), value.shape[dim])
        up = [(i, (i + 1) % peers) for i in range(peers - 1)]
        down = [(j, i) for i, j in up]
        last = lax.slice_in_dim(value, length - width, length, axis=dim)
        initial = lax.slice_in_dim(value, 0, width, axis=dim)
        before = lax.ppermute(last, axis, up)
        after = lax.ppermute(initial, axis, down)
        value = jnp.concatenate([before, value, after], axis=dim)
    return value


def shift_columns(field, offset):
    width = field.shape[-1]
    blank = jnp.zeros(field.shape[:-1] + (abs(offset),), field.dtype)
    if offset > 0:
        return jnp.concatenate([field[..., offset:], blank], -1)
    return jnp.concatenate([blank, field[..., : width + offset]], -1)


def advance(extended, wind_rows):
    center = extended[:, :, 2:-2]
    north_one = extended[:, :, 3:-1]
    south_one = extended[:, :, 1:-3]
    north_two = extended[:, :, 4:]
    south_two = extended[:, :, :-4]
    east_one = shift_columns(center, 1)
    west_one = shift_columns(center, -1)
    east_two = shift_columns(center, 2)
    west_two = shift_columns(center, -2)
    grad_row = (8.0 * (north_one - south_one) - (north_two - south_two)) / 12.0
    grad_col = (8.0 * (east_one - west_one) - (east_two - west_two)) / 12.0
    laplace = north_one + south_one + east_one + west_one - 4.0 * center
    diffusion = jnp.array(DIFFUSION, jnp.float32).reshape(2, 1, 1)
    return center - wind_rows[0] * grad_row - wind_rows[1] * grad_col + diffusion * laplace


def shard_terms(observed, slot_weight, obs_value):
    obs_mean = jnp.sum(observed, 0) / REPLICA_COUNT
    obs_anomaly = observed - obs_mean
    weighted = obs_anomaly * slot_weight
    gram = jnp.dot(
        weighted, obs_anomaly.T, precision=lax.Precision.HIGHEST, preferred_element_type=jnp.float32
    )
    drive = jnp.dot(
        weighted,
        obs_value - obs_mean,
        precision=lax.Precision.HIGHEST,
        preferred_element_type=jnp.float32,
    )
    return (gram, drive)


def ensemble_weights(gram, drive):
    ident = jnp.eye(REPLICA_COUNT, dtype=jnp.float32)
    system = (REPLICA_COUNT - 1.0) * ident + gram
    scale = jnp.sqrt(jnp.sum(system * system))

    def newton_turn(turn, carry):
        root, inverse_root = carry
        middle_term = 0.5 * (
            3.0 * ident
            - jnp.dot(
                inverse_root,
                root,
                precision=lax.Precision.HIGHEST,
                preferred_element_type=jnp.float32,
            )
        )
        root = jnp.dot(
            root, middle_term, precision=lax.Precision.HIGHEST, preferred_element_type=jnp.float32
        )
        inverse_root = jnp.dot(
            middle_term,
            inverse_root,
            precision=lax.Precision.HIGHEST,
            preferred_element_type=jnp.float32,
        )
        return (root, inverse_root)

    root, inverse_root = lax.fori_loop(0, NS_ITERS, newton_turn, (system / scale, ident))
    half = inverse_root / jnp.sqrt(scale)
    precision_matrix = jnp.dot(
        half, half, precision=lax.Precision.HIGHEST, preferred_element_type=jnp.float32
    )
    mean_weight = jnp.dot(
        precision_matrix, drive, precision=lax.Precision.HIGHEST, preferred_element_type=jnp.float32
    )
    spread = jnp.sqrt(REPLICA_COUNT - 1.0) * half
    return (mean_weight[:, None] + spread).astype(jnp.bfloat16)


def local_generic(prior_replicas, wind_field, obs_index, obs_count, obs_value, obs_weight):
    member_count, field_count, row_count, col_count = prior_replicas.shape
    state = prior_replicas
    for step_index in range(2):
        extended = padded(state, (("space", 2),), 2)
        state = advance(extended, wind_field[step_index])
    capacity = obs_index.shape[0]
    raveled_vector = state.reshape(member_count, -1)
    local_obs = jnp.take(raveled_vector, obs_index, axis=1)
    slot_number = jnp.arange(capacity, dtype=jnp.int32)
    slot_weight = obs_weight * (slot_number < obs_count[0]).astype(jnp.float32)
    gathered = lax.all_gather(local_obs, "mem", axis=0, tiled=True)
    gram, drive = shard_terms(gathered, slot_weight, obs_value)
    gram, drive = lax.psum((gram, drive), "space")
    transform = ensemble_weights(gram, drive)
    transform_rows = transform.T
    block = lax.all_to_all(state, "mem", split_axis=3, concat_axis=0, tiled=True)
    replica_centroid = jnp.sum(block, 0) / REPLICA_COUNT
    replica_departure = (block - replica_centroid).astype(jnp.bfloat16)
    posterior_correction = jnp.dot(
        transform_rows,
        replica_departure.reshape(REPLICA_COUNT, -1),
        preferred_element_type=jnp.float32,
    )
    analysed = posterior_correction.reshape(block.shape) + replica_centroid
    return lax.all_to_all(analysed, "mem", split_axis=0, concat_axis=3, tiled=True)


BF = jnp.bfloat16
F32 = jnp.float32
PAD = 128


def vmem():
    return pl.BlockSpec(memory_space=pltpu.VMEM)


def smem():
    return pl.BlockSpec(memory_space=pltpu.SMEM)


def hbm():
    return pl.BlockSpec(memory_space=pltpu.MemorySpace.HBM)


def params():
    return pltpu.CompilerParams(vmem_limit_bytes=44 * 1024 * 1024)


def cost(touched):
    return pl.CostEstimate(flops=touched, bytes_accessed=touched, transcendentals=0)


def blank_edges(rows):
    width = rows.shape[2]
    for r in (0, 1, 10, 11):
        rows[r] = jnp.zeros((16, width), F32)
    for r in range(2, 10):
        rows[r, :, width - PAD :] = jnp.zeros((16, PAD), F32)


def pack_kernel(
    pos, prior, wind, turned_0, turned_1, pay_a, pay_b, state, edge, sems
):
    winds = pltpu.make_async_copy(wind.at[0], edge, sems.at[2])
    loads = [pltpu.make_async_copy(prior.at[:, f], state.at[f], sems.at[f]) for f in range(2)]
    loads[0].start()
    winds.start()
    loads[1].start()
    even = (pos[0] % 2) == 0
    start_a = jnp.where(even, 4, 0)
    start_b = 4 - start_a
    cols = state.shape[3]
    for f in range(2):
        turned = (turned_0, turned_1)[f]
        blank_edges(turned)
        loads[f].wait()
        turned[2:10, :, :cols] = jnp.swapaxes(state[f], 0, 1)
        for r in range(4):
            at = (f * 4 + r) * 16
            pay_a[at : at + 16, :] = turned[2 + start_a + r, :, :cols].astype(BF)
            pay_b[at : at + 16, :] = turned[2 + start_b + r, :, :cols].astype(BF)
    winds.wait()
    first = jnp.concatenate([edge[0, 0:2], edge[1, 0:2]], 0)
    last = jnp.concatenate([edge[0, 6:8], edge[1, 6:8]], 0)
    first_high = first.astype(BF).astype(F32)
    last_high = last.astype(BF).astype(F32)
    first = jnp.concatenate([first_high, first - first_high], 0)
    last = jnp.concatenate([last_high, last - last_high], 0)
    pay_a[128:136, :] = jnp.where(even, last, first).astype(BF)
    pay_b[128:136, :] = jnp.where(even, first, last).astype(BF)


def slots_kernel(index, count, weight, value, place, chunk, root_out, rooted_out):
    slots = index.shape[1]
    width = place.shape[0]
    n = index[...]
    used = lax.broadcasted_iota(jnp.int32, (1, slots), 1) < count[0]
    root = jnp.where(used, jnp.sqrt(weight[...]), 0.0)
    root_out[...] = root
    rooted_out[...] = root * value[...]
    chunk[...] = jnp.broadcast_to(n // width, (16, slots))
    column = n % width
    step = 64
    for r in range(0, width, step):
        hit = lax.broadcasted_iota(jnp.int32, (step, slots), 0) == column - r
        place[r : r + step, :] = jnp.where(hit, 1.0, 0.0).astype(BF)


def pick_kernel(place, chunk, one, more, out, tall):
    width, slots = place.shape
    parts = one.shape[2] // width
    at = 0
    for ref in (one, more):
        for r in range(ref.shape[0]):
            for p in range(parts):
                tall[at * 16 : at * 16 + 16, :] = ref[r, :, p * width : (p + 1) * width]
                at += 1
    count = at
    step = 256
    for o in range(0, slots, step):
        cut = slice(o, o + step)
        seen = jnp.dot(tall[...], place[:, cut], preferred_element_type=F32)
        number = chunk[:, cut]
        total = jnp.zeros((16, step), F32)
        for at in range(count):
            total = total + jnp.where(number == at, seen[at * 16 : at * 16 + 16], 0.0)
        out[:, cut] = total.astype(BF)


def stencil_row(rows, wind_r, wind_c, nu):
    south_two, south_one, center, north_one, north_two = rows
    width = [v for v in rows if v is not None][0].shape[1]
    keep = width - PAD

    def less(a, b):
        if a is None:
            return None if b is None else -b
        return a if b is None else a - b

    def more(a, b):
        if a is None or b is None:
            return b if a is None else a
        return a + b

    rows = [None if v is None else v[:, :keep] for v in rows]
    one = less(rows[3], rows[1])
    grad_r = less(None if one is None else 8.0 * one, less(rows[4], rows[0]))
    ring = more(rows[3], rows[1])
    out = -(wind_r * grad_r)
    if center is not None:
        east_one = pltpu.roll(center, width - 1, 1)
        west_one = pltpu.roll(center, 1, 1)
        east_two = pltpu.roll(center, width - 2, 1)
        west_two = pltpu.roll(center, 2, 1)
        grad_c = 8.0 * (east_one - west_one) - (east_two - west_two)
        ring = more(ring, (east_one + west_one)[:, :keep])
        out = (1.0 - 4.0 * nu) * rows[2] + out - wind_c * grad_c[:, :keep]
    return out if ring is None else out + nu * ring


TWELFTH = 1.0 / 12.0


def pre_kernel(nu, turned, wind, out, mid, wide):
    cols = out.shape[2]
    blank_edges(mid)
    for step in range(2):
        for c in range(2):
            for r in range(8):
                wide[step, c, r] = jnp.broadcast_to(wind[step, c, r : r + 1] * TWELFTH, (8, cols))

    def first_step(r, carry):
        for g in range(2):
            span = pl.ds(g * 8, 8)
            rows = [turned[r + i, span, :] for i in range(5)]
            mid[r + 2, span, :cols] = stencil_row(rows, wide[0, 0, r], wide[0, 1, r], nu)
        return carry

    lax.fori_loop(0, 8, first_step, 0)

    def second_step(r, carry):
        for g in range(2):
            span = pl.ds(g * 8, 8)
            rows = [mid[r + i, span, :] for i in range(5)]
            out[r, span, :] = stencil_row(rows, wide[1, 0, r], wide[1, 1, r], nu)
        return carry

    lax.fori_loop(0, 8, second_step, 0)


def post_kernel(field, pos, turned, begun, recv_a, recv_b, wind, *refs):
    outs = refs[-4:-2] if field == 0 else refs[-3:-2]
    halo, delta = refs[-2:]
    nu = DIFFUSION[field]
    cols = begun.shape[2]
    even = (pos[0] % 2) == 0
    start_a = jnp.where(even, 4, 0)
    start_b = 4 - start_a
    blank = jnp.zeros((16, PAD), F32)
    for r in range(8):
        halo[r, :, cols:] = blank
        delta[r, :, cols:] = blank
    for r in range(4):
        at = (field * 4 + r) * 16
        halo[start_a + r, :, :cols] = recv_a[at : at + 16, :].astype(F32)
        halo[start_b + r, :, :cols] = recv_b[at : at + 16, :].astype(F32)
    got_a = recv_a[128:136, :].astype(F32)
    got_a = got_a[0:4] + got_a[4:8]
    got_b = recv_b[128:136, :].astype(F32)
    got_b = got_b[0:4] + got_b[4:8]
    top = jnp.where(pos[0] == 0, 0.0, 1.0)
    bottom = jnp.where(pos[0] == pos[1] - 1, 0.0, 1.0)
    before = jnp.where(even, got_b, got_a) * TWELFTH
    after = jnp.where(even, got_a, got_b) * TWELFTH

    def broad(row):
        return jnp.broadcast_to(row, (8, cols))

    def own_wind(step, c, r):
        return broad(wind[step, c, r : r + 1] * TWELFTH)

    for g in range(2):
        span = slice(g * 8, g * 8 + 8)
        h = lambda i: halo[i, span, :]
        x = lambda r: turned[2 + r, span, :]
        for i in range(2):
            rows = [h(0), h(1), h(2), h(3), x(0)] if i == 0 else [h(1), h(2), h(3), x(0), x(1)]
            value = stencil_row(rows, broad(before[i : i + 1]), broad(before[2 + i : 3 + i]), nu)
            delta[i, span, :cols] = value * top
            rows = [x(6), x(7), h(4), h(5), h(6)] if i == 0 else [x(7), h(4), h(5), h(6), h(7)]
            value = stencil_row(rows, broad(after[i : i + 1]), broad(after[2 + i : 3 + i]), nu)
            delta[6 + i, span, :cols] = value * bottom
        near = (
            (2, 0, [h(2), h(3), None, None, None]),
            (3, 1, [h(3), None, None, None, None]),
            (4, 6, [None, None, None, None, h(4)]),
            (5, 7, [None, None, None, h(4), h(5)]),
        )
        for at, r, rows in near:
            delta[at, span, :cols] = stencil_row(rows, own_wind(0, 0, r), None, nu)

    for r in range(8):
        both = []
        for g in range(2):
            span = slice(g * 8, g * 8 + 8)
            rows = []
            for i in range(r - 2, r + 3):
                if i <= 1 and r <= 3:
                    rows.append(delta[i + 2, span, :])
                elif i >= 6 and r >= 4:
                    rows.append(delta[i - 2, span, :])
                else:
                    rows.append(None)
            center = rows[2] is not None
            value = stencil_row(
                rows, own_wind(1, 0, r), own_wind(1, 1, r) if center else None, nu
            )
            both.append(begun[r, span, :] + value)
        whole = jnp.concatenate(both, 0).astype(BF)
        if field == 0:
            outs[r // 4][r % 4] = whole
        else:
            outs[0][4 + r] = whole
    if field == 1:
        outs[0][0:4] = refs[0][...]


def gram_kernel(pos, own, mate, far, diag, root, rooted, out, spread):
    parts = [v[...].astype(F32) for v in (own, mate, far, diag)]
    total = (parts[0] + parts[1]) + (parts[2] + parts[3])
    mean = jnp.sum(total, 0, keepdims=True) * (1.0 / REPLICA_COUNT)
    weight = root[...]
    gap = rooted[...] - weight * mean
    for g in range(4):
        spread[jnp.bitwise_xor(pos[2], g)] = ((parts[g] - mean) * weight).astype(BF)
    high = gap.astype(BF).astype(F32)
    slots = root.shape[1]
    pair = jnp.concatenate([high, gap - high, jnp.zeros((14, slots), F32)], 0)
    spread[4] = pair.astype(BF)
    left = spread[...].reshape(80, slots)
    right = spread[0:4].reshape(64, slots)
    out[...] = lax.dot_general(
        left, right, (((1,), (1,)), ((), ())), preferred_element_type=F32
    )


def exact(a, b):
    return jnp.dot(a, b, precision=lax.Precision.HIGHEST, preferred_element_type=F32)


def weights_kernel(pos, one, two, out, keep):
    total = one[...] + two[...]
    gram = total[0:64]
    drive = total[64:65] + total[65:66]
    row = lax.broadcasted_iota(jnp.int32, (64, 64), 0)
    col = lax.broadcasted_iota(jnp.int32, (64, 64), 1)
    ident = jnp.where(row == col, 1.0, 0.0)
    system = (REPLICA_COUNT - 1.0) * ident + gram
    square = jnp.sum(jnp.sum(system * system, 1, keepdims=True), 0, keepdims=True)
    scale = jnp.sqrt(square)
    root = system / scale
    inverse_root = ident
    for turn in range(NS_ITERS):
        if turn == 0:
            middle = 0.5 * (3.0 * ident - root)
            inverse_next = middle
        else:
            middle = 0.5 * (3.0 * ident - exact(inverse_root, root))
            inverse_next = exact(middle, inverse_root)
        if turn < NS_ITERS - 1:
            root = exact(root, middle)
        inverse_root = inverse_next
    half = inverse_root / jnp.sqrt(scale)
    drive8 = jnp.broadcast_to(drive, (8, 64))
    mean_weight = exact(exact(drive8, half), half)[0:1]
    transform_t = (mean_weight + (REPLICA_COUNT - 1.0) ** 0.5 * half).astype(BF).astype(F32)
    total_t = jnp.sum(transform_t, 1, keepdims=True)
    keep[...] = transform_t + (1.0 - total_t) * (1.0 / REPLICA_COUNT)
    mine = keep[pl.ds(pl.multiple_of(pos[2] * 16, 16), 16), :]
    swap1 = jnp.concatenate([mine[:, 16:32], mine[:, 0:16], mine[:, 48:64], mine[:, 32:48]], 1)
    mine = jnp.where((pos[2] % 2) == 1, swap1, mine)
    swap2 = jnp.concatenate([mine[:, 32:64], mine[:, 0:32]], 1)
    mine = jnp.where(pos[2] >= 2, swap2, mine)
    high = mine.astype(BF).astype(F32)
    out[...] = jnp.concatenate([high, mine - high], 0).astype(BF)


def final_kernel(
    weights, own, mate, far, diag, own_more, mate_more, far_more, diag_more, out, keep, ready, sems
):
    m = weights[...]
    copies = []
    for f in range(2):
        for r in range(8):
            first = f == 0 and r < 4
            refs = (own, mate, far, diag) if first else (own_more, mate_more, far_more, diag_more)
            at = r if first else f * 8 + r - 4
            state = jnp.concatenate([v[at] for v in refs], 0)
            both = jnp.dot(m, state, preferred_element_type=F32)
            keep[r] = both[0:16] + both[16:32]
        ready[f] = jnp.swapaxes(keep[...], 0, 1)
        copies.append(pltpu.make_async_copy(ready.at[f], out.at[:, f], sems.at[f]))
        copies[f].start()
    for f in range(2):
        copies[f].wait()


def local(prior_replicas, wind_field, obs_index, obs_count, obs_value, obs_weight):
    cols = prior_replicas.shape[3]
    strips = lax.axis_size("space")
    here = lax.axis_index("space")
    group = lax.axis_index("mem")
    pos = jnp.stack([here, jnp.int32(strips), group]).astype(jnp.int32)
    shape = jax.ShapeDtypeStruct
    pairs_a = [(i, i ^ 1) for i in range(strips)]
    pairs_b = [(i, i + 1) for i in range(1, strips - 1, 2)]
    pairs_b = pairs_b + [(j, i) for i, j in pairs_b]

    def swap(value, bits):
        return lax.ppermute(value, "mem", [(i, i ^ bits) for i in range(4)])

    prior_here = pltpu.with_memory_space_constraint(prior_replicas, pltpu.MemorySpace.HBM)
    wind_here = pltpu.with_memory_space_constraint(wind_field, pltpu.MemorySpace.HBM)

    packed = pl.pallas_call(
        pack_kernel,
        name="pack",
        cost_estimate=cost(80 * 16 * cols * 4),
        in_specs=[smem(), hbm(), hbm()],
        out_specs=[vmem()] * 4,
        out_shape=[shape((12, 16, cols + PAD), F32)] * 2
        + [shape((136, cols), BF)] * 2,
        scratch_shapes=[
            pltpu.VMEM((2, 16, 8, cols), F32),
            pltpu.VMEM((2, 8, cols), F32),
            pltpu.SemaphoreType.DMA((3,)),
        ],
        compiler_params=params(),
    )(pos, prior_here, wind_here)
    turned = packed[0:2]
    recv_a = lax.ppermute(packed[2], "space", pairs_a)
    recv_b = lax.ppermute(packed[3], "space", pairs_b)

    def pre(f, rows):
        return pl.pallas_call(
            functools.partial(pre_kernel, DIFFUSION[f]),
            name="pre",
            cost_estimate=cost(150 * 16 * cols * 4),
            in_specs=[vmem()] * 2,
            out_specs=vmem(),
            out_shape=shape((8, 16, cols), F32),
            scratch_shapes=[
                pltpu.VMEM((12, 16, cols + PAD), F32),
                pltpu.VMEM((2, 2, 8, 8, cols), F32),
            ],
            compiler_params=params(),
        )(rows, wind_field)

    begun = [pre(f, turned[f]) for f in range(2)]

    slots = obs_index.shape[0]
    width = 512
    place, chunk, root, rooted = pl.pallas_call(
        slots_kernel,
        name="slots",
        cost_estimate=cost(width * slots * 2),
        in_specs=[vmem(), smem(), vmem(), vmem()],
        out_specs=[vmem()] * 4,
        out_shape=[
            shape((width, slots), BF),
            shape((16, slots), jnp.int32),
            shape((1, slots), F32),
            shape((1, slots), F32),
        ],
        compiler_params=params(),
    )(
        obs_index.reshape(1, slots),
        obs_count,
        obs_weight.reshape(1, slots),
        obs_value.reshape(1, slots),
    )
    recv_a, begun[0], begun[1], place = lax.optimization_barrier(
        (recv_a, begun[0], begun[1], place)
    )

    def post(f, extra):
        heights = (4, 4) if f == 0 else (12,)
        return pl.pallas_call(
            functools.partial(post_kernel, f),
            name="post",
            cost_estimate=cost(8),
            in_specs=[smem()] + [vmem()] * (5 + f),
            out_specs=[vmem()] * len(heights),
            out_shape=[shape((v, 16, cols), BF) for v in heights],
            scratch_shapes=[
                pltpu.VMEM((8, 16, cols + PAD), F32),
                pltpu.VMEM((8, 16, cols + PAD), F32),
            ],
            compiler_params=params(),
        )(pos, turned[f], begun[f], recv_a, recv_b, wind_field, *extra)

    one, two = post(0, [])
    far_one = swap(one, 2)
    more = post(1, [two])[0]
    seen = pl.pallas_call(
        pick_kernel,
        name="pick",
        cost_estimate=cost(8),
        in_specs=[vmem()] * 4,
        out_specs=vmem(),
        out_shape=shape((16, slots), BF),
        scratch_shapes=[pltpu.VMEM((16 * 16 * cols // width, width), BF)],
        compiler_params=params(),
    )(place, chunk, one, more)

    seen_far = swap(seen, 2)
    seen_mate = swap(seen, 1)
    seen_far, far_one, late = lax.optimization_barrier((seen_far, far_one, more))
    far_more = swap(late, 2)
    seen_diag = swap(seen_far, 1)

    part = pl.pallas_call(
        gram_kernel,
        name="gram",
        cost_estimate=cost(24 * 64 * slots),
        in_specs=[smem()] + [vmem()] * 6,
        out_specs=vmem(),
        out_shape=shape((80, 64), F32),
        scratch_shapes=[pltpu.VMEM((5, 16, slots), BF)],
        compiler_params=params(),
    )(pos, seen, seen_mate, seen_far, seen_diag, root, rooted)

    bits = 1
    other = None
    while bits < strips:
        if other is not None:
            part = part + other
        other = lax.ppermute(part, "space", [(i, i ^ bits) for i in range(strips)])
        bits *= 2

    late = lax.optimization_barrier((one, more, far_one, part))
    mate_one, mate_more, diag_one = [swap(v, 1) for v in late[:3]]
    late, _ = lax.optimization_barrier((far_more, other))
    diag_more = swap(late, 1)

    weights = pl.pallas_call(
        weights_kernel,
        name="weights",
        cost_estimate=cost(400 * 64 * 128 * 4),
        in_specs=[smem(), vmem(), vmem()],
        out_specs=vmem(),
        out_shape=shape((32, 64), BF),
        scratch_shapes=[pltpu.VMEM((64, 64), F32)],
        compiler_params=params(),
    )(pos, part, other)

    return pl.pallas_call(
        final_kernel,
        name="final",
        cost_estimate=cost(100 * 16 * cols * 4),
        in_specs=[vmem()] * 9,
        out_specs=hbm(),
        out_shape=shape(prior_replicas.shape, F32),
        scratch_shapes=[
            pltpu.VMEM((8, 16, cols), F32),
            pltpu.VMEM((2, 16, 8, cols), F32),
            pltpu.SemaphoreType.DMA((2,)),
        ],
        compiler_params=params(),
    )(
        weights, one, mate_one, far_one, diag_one, more, mate_more, far_more, diag_more
    )


def solution(mesh):
    in_specs = (
        P(("parts", "mem"), None, "space", None),
        P("parts", None, "space", None),
        P(("parts", "space")),
        P(("parts", "space")),
        P(("parts", "space")),
        P(("parts", "space")),
    )
    out_specs = P(("parts", "mem"), None, "space", None)
    strips = mesh.shape["space"]
    fast = mesh.shape["mem"] == 4 and strips > 1 and strips & (strips - 1) == 0
    body = local if fast else local_generic
    return jax.shard_map(body, mesh=mesh, in_specs=in_specs, out_specs=out_specs, check_vma=False)
```

```python
import functools

import jax
import jax.numpy as jnp
from jax import lax
from jax.experimental import pallas as pl
from jax.experimental.pallas import tpu as pltpu
from jax.sharding import PartitionSpec as P

REPLICA_COUNT = 64
NS_ITERS = 5


DIFFUSION = (0.05, 0.15)


def padded(value, sides, width):
    for axis, dim in sides:
        peers, length = (lax.axis_size(axis), value.shape[dim])
        up = [(i, (i + 1) % peers) for i in range(peers - 1)]
        down = [(j, i) for i, j in up]
        last = lax.slice_in_dim(value, length - width, length, axis=dim)
        initial = lax.slice_in_dim(value, 0, width, axis=dim)
        before = lax.ppermute(last, axis, up)
        after = lax.ppermute(initial, axis, down)
        value = jnp.concatenate([before, value, after], axis=dim)
    return value


def shift_columns(field, offset):
    width = field.shape[-1]
    blank = jnp.zeros(field.shape[:-1] + (abs(offset),), field.dtype)
    if offset > 0:
        return jnp.concatenate([field[..., offset:], blank], -1)
    return jnp.concatenate([blank, field[..., : width + offset]], -1)


def advance(extended, wind_rows):
    center = extended[:, :, 2:-2]
    north_one = extended[:, :, 3:-1]
    south_one = extended[:, :, 1:-3]
    north_two = extended[:, :, 4:]
    south_two = extended[:, :, :-4]
    east_one = shift_columns(center, 1)
    west_one = shift_columns(center, -1)
    east_two = shift_columns(center, 2)
    west_two = shift_columns(center, -2)
    grad_row = (8.0 * (north_one - south_one) - (north_two - south_two)) / 12.0
    grad_col = (8.0 * (east_one - west_one) - (east_two - west_two)) / 12.0
    laplace = north_one + south_one + east_one + west_one - 4.0 * center
    diffusion = jnp.array(DIFFUSION, jnp.float32).reshape(2, 1, 1)
    return center - wind_rows[0] * grad_row - wind_rows[1] * grad_col + diffusion * laplace


def shard_terms(observed, slot_weight, obs_value):
    obs_mean = jnp.sum(observed, 0) / REPLICA_COUNT
    obs_anomaly = observed - obs_mean
    weighted = obs_anomaly * slot_weight
    gram = jnp.dot(
        weighted, obs_anomaly.T, precision=lax.Precision.HIGHEST, preferred_element_type=jnp.float32
    )
    drive = jnp.dot(
        weighted,
        obs_value - obs_mean,
        precision=lax.Precision.HIGHEST,
        preferred_element_type=jnp.float32,
    )
    return (gram, drive)


def ensemble_weights(gram, drive):
    ident = jnp.eye(REPLICA_COUNT, dtype=jnp.float32)
    system = (REPLICA_COUNT - 1.0) * ident + gram
    scale = jnp.sqrt(jnp.sum(system * system))

    def newton_turn(turn, carry):
        root, inverse_root = carry
        middle_term = 0.5 * (
            3.0 * ident
            - jnp.dot(
                inverse_root,
                root,
                precision=lax.Precision.HIGHEST,
                preferred_element_type=jnp.float32,
            )
        )
        root = jnp.dot(
            root, middle_term, precision=lax.Precision.HIGHEST, preferred_element_type=jnp.float32
        )
        inverse_root = jnp.dot(
            middle_term,
            inverse_root,
            precision=lax.Precision.HIGHEST,
            preferred_element_type=jnp.float32,
        )
        return (root, inverse_root)

    root, inverse_root = lax.fori_loop(0, NS_ITERS, newton_turn, (system / scale, ident))
    half = inverse_root / jnp.sqrt(scale)
    precision_matrix = jnp.dot(
        half, half, precision=lax.Precision.HIGHEST, preferred_element_type=jnp.float32
    )
    mean_weight = jnp.dot(
        precision_matrix, drive, precision=lax.Precision.HIGHEST, preferred_element_type=jnp.float32
    )
    spread = jnp.sqrt(REPLICA_COUNT - 1.0) * half
    return (mean_weight[:, None] + spread).astype(jnp.bfloat16)


def local_generic(prior_replicas, wind_field, obs_index, obs_count, obs_value, obs_weight):
    member_count, field_count, row_count, col_count = prior_replicas.shape
    state = prior_replicas
    for step_index in range(2):
        extended = padded(state, (("space", 2),), 2)
        state = advance(extended, wind_field[step_index])
    capacity = obs_index.shape[0]
    raveled_vector = state.reshape(member_count, -1)
    local_obs = jnp.take(raveled_vector, obs_index, axis=1)
    slot_number = jnp.arange(capacity, dtype=jnp.int32)
    slot_weight = obs_weight * (slot_number < obs_count[0]).astype(jnp.float32)
    gathered = lax.all_gather(local_obs, "mem", axis=0, tiled=True)
    gram, drive = shard_terms(gathered, slot_weight, obs_value)
    gram, drive = lax.psum((gram, drive), "space")
    transform = ensemble_weights(gram, drive)
    transform_rows = transform.T
    block = lax.all_to_all(state, "mem", split_axis=3, concat_axis=0, tiled=True)
    replica_centroid = jnp.sum(block, 0) / REPLICA_COUNT
    replica_departure = (block - replica_centroid).astype(jnp.bfloat16)
    posterior_correction = jnp.dot(
        transform_rows,
        replica_departure.reshape(REPLICA_COUNT, -1),
        preferred_element_type=jnp.float32,
    )
    analysed = posterior_correction.reshape(block.shape) + replica_centroid
    return lax.all_to_all(analysed, "mem", split_axis=0, concat_axis=3, tiled=True)


BF = jnp.bfloat16
F32 = jnp.float32
PAD = 128


def vmem():
    return pl.BlockSpec(memory_space=pltpu.VMEM)


def smem():
    return pl.BlockSpec(memory_space=pltpu.SMEM)


def hbm():
    return pl.BlockSpec(memory_space=pltpu.MemorySpace.HBM)


def params():
    return pltpu.CompilerParams(vmem_limit_bytes=44 * 1024 * 1024)


def cost(touched):
    return pl.CostEstimate(flops=touched, bytes_accessed=touched, transcendentals=0)


def blank_edges(rows):
    width = rows.shape[2]
    for r in (0, 1, 10, 11):
        rows[r] = jnp.zeros((16, width), F32)
    for r in range(2, 10):
        rows[r, :, width - PAD :] = jnp.zeros((16, PAD), F32)


def pack_kernel(
    pos, prior, wind, turned_0, turned_1, pay_a, pay_b, state, edge, sems
):
    winds = pltpu.make_async_copy(wind.at[0], edge, sems.at[2])
    loads = [pltpu.make_async_copy(prior.at[:, f], state.at[f], sems.at[f]) for f in range(2)]
    loads[0].start()
    winds.start()
    loads[1].start()
    even = (pos[0] % 2) == 0
    start_a = jnp.where(even, 4, 0)
    start_b = 4 - start_a
    cols = state.shape[3]
    for f in range(2):
        turned = (turned_0, turned_1)[f]
        blank_edges(turned)
        loads[f].wait()
        turned[2:10, :, :cols] = jnp.swapaxes(state[f], 0, 1)
        for r in range(4):
            at = (f * 4 + r) * 16
            pay_a[at : at + 16, :] = turned[2 + start_a + r, :, :cols].astype(BF)
            pay_b[at : at + 16, :] = turned[2 + start_b + r, :, :cols].astype(BF)
    winds.wait()
    first = jnp.concatenate([edge[0, 0:2], edge[1, 0:2]], 0)
    last = jnp.concatenate([edge[0, 6:8], edge[1, 6:8]], 0)
    first_high = first.astype(BF).astype(F32)
    last_high = last.astype(BF).astype(F32)
    first = jnp.concatenate([first_high, first - first_high], 0)
    last = jnp.concatenate([last_high, last - last_high], 0)
    pay_a[128:136, :] = jnp.where(even, last, first).astype(BF)
    pay_b[128:136, :] = jnp.where(even, first, last).astype(BF)


def slots_kernel(index, count, weight, value, place, chunk, root_out, rooted_out):
    slots = index.shape[1]
    width = place.shape[0]
    n = index[...]
    used = lax.broadcasted_iota(jnp.int32, (1, slots), 1) < count[0]
    root = jnp.where(used, jnp.sqrt(weight[...]), 0.0)
    root_out[...] = root
    rooted_out[...] = root * value[...]
    chunk[...] = jnp.broadcast_to(n // width, (16, slots))
    column = n % width
    step = 64
    for r in range(0, width, step):
        hit = lax.broadcasted_iota(jnp.int32, (step, slots), 0) == column - r
        place[r : r + step, :] = jnp.where(hit, 1.0, 0.0).astype(BF)


def pick_kernel(place, chunk, one, more, out, tall):
    width, slots = place.shape
    parts = one.shape[2] // width
    at = 0
    for ref in (one, more):
        for r in range(ref.shape[0]):
            for p in range(parts):
                tall[at * 16 : at * 16 + 16, :] = ref[r, :, p * width : (p + 1) * width]
                at += 1
    count = at
    step = 256
    for o in range(0, slots, step):
        cut = slice(o, o + step)
        seen = jnp.dot(tall[...], place[:, cut], preferred_element_type=F32)
        number = chunk[:, cut]
        total = jnp.zeros((16, step), F32)
        for at in range(count):
            total = total + jnp.where(number == at, seen[at * 16 : at * 16 + 16], 0.0)
        out[:, cut] = total.astype(BF)


def stencil_row(rows, wind_r, wind_c, nu):
    south_two, south_one, center, north_one, north_two = rows
    width = [v for v in rows if v is not None][0].shape[1]
    keep = width - PAD

    def less(a, b):
        if a is None:
            return None if b is None else -b
        return a if b is None else a - b

    def more(a, b):
        if a is None or b is None:
            return b if a is None else a
        return a + b

    rows = [None if v is None else v[:, :keep] for v in rows]
    one = less(rows[3], rows[1])
    grad_r = less(None if one is None else 8.0 * one, less(rows[4], rows[0]))
    ring = more(rows[3], rows[1])
    out = -(wind_r * grad_r)
    if center is not None:
        east_one = pltpu.roll(center, width - 1, 1)
        west_one = pltpu.roll(center, 1, 1)
        east_two = pltpu.roll(center, width - 2, 1)
        west_two = pltpu.roll(center, 2, 1)
        grad_c = 8.0 * (east_one - west_one) - (east_two - west_two)
        ring = more(ring, (east_one + west_one)[:, :keep])
        out = (1.0 - 4.0 * nu) * rows[2] + out - wind_c * grad_c[:, :keep]
    return out if ring is None else out + nu * ring


TWELFTH = 1.0 / 12.0


def pre_kernel(nu, turned, wind, out, mid, wide):
    cols = out.shape[2]
    blank_edges(mid)
    for step in range(2):
        for c in range(2):
            for r in range(8):
                wide[step, c, r] = jnp.broadcast_to(wind[step, c, r : r + 1] * TWELFTH, (8, cols))

    def first_step(r, carry):
        for g in range(2):
            span = pl.ds(g * 8, 8)
            rows = [turned[r + i, span, :] for i in range(5)]
            mid[r + 2, span, :cols] = stencil_row(rows, wide[0, 0, r], wide[0, 1, r], nu)
        return carry

    lax.fori_loop(0, 8, first_step, 0)

    def second_step(r, carry):
        for g in range(2):
            span = pl.ds(g * 8, 8)
            rows = [mid[r + i, span, :] for i in range(5)]
            out[r, span, :] = stencil_row(rows, wide[1, 0, r], wide[1, 1, r], nu)
        return carry

    lax.fori_loop(0, 8, second_step, 0)


def post_kernel(field, pos, turned, begun, recv_a, recv_b, wind, *refs):
    outs = refs[-4:-2] if field == 0 else refs[-3:-2]
    halo, delta = refs[-2:]
    nu = DIFFUSION[field]
    cols = begun.shape[2]
    even = (pos[0] % 2) == 0
    start_a = jnp.where(even, 4, 0)
    start_b = 4 - start_a
    blank = jnp.zeros((16, PAD), F32)
    for r in range(8):
        halo[r, :, cols:] = blank
        delta[r, :, cols:] = blank
    for r in range(4):
        at = (field * 4 + r) * 16
        halo[start_a + r, :, :cols] = recv_a[at : at + 16, :].astype(F32)
        halo[start_b + r, :, :cols] = recv_b[at : at + 16, :].astype(F32)
    got_a = recv_a[128:136, :].astype(F32)
    got_a = got_a[0:4] + got_a[4:8]
    got_b = recv_b[128:136, :].astype(F32)
    got_b = got_b[0:4] + got_b[4:8]
    top = jnp.where(pos[0] == 0, 0.0, 1.0)
    bottom = jnp.where(pos[0] == pos[1] - 1, 0.0, 1.0)
    before = jnp.where(even, got_b, got_a) * TWELFTH
    after = jnp.where(even, got_a, got_b) * TWELFTH

    def broad(row):
        return jnp.broadcast_to(row, (8, cols))

    def own_wind(step, c, r):
        return broad(wind[step, c, r : r + 1] * TWELFTH)

    for g in range(2):
        span = slice(g * 8, g * 8 + 8)
        h = lambda i: halo[i, span, :]
        x = lambda r: turned[2 + r, span, :]
        for i in range(2):
            rows = [h(0), h(1), h(2), h(3), x(0)] if i == 0 else [h(1), h(2), h(3), x(0), x(1)]
            value = stencil_row(rows, broad(before[i : i + 1]), broad(before[2 + i : 3 + i]), nu)
            delta[i, span, :cols] = value * top
            rows = [x(6), x(7), h(4), h(5), h(6)] if i == 0 else [x(7), h(4), h(5), h(6), h(7)]
            value = stencil_row(rows, broad(after[i : i + 1]), broad(after[2 + i : 3 + i]), nu)
            delta[6 + i, span, :cols] = value * bottom
        near = (
            (2, 0, [h(2), h(3), None, None, None]),
            (3, 1, [h(3), None, None, None, None]),
            (4, 6, [None, None, None, None, h(4)]),
            (5, 7, [None, None, None, h(4), h(5)]),
        )
        for at, r, rows in near:
            delta[at, span, :cols] = stencil_row(rows, own_wind(0, 0, r), None, nu)

    for r in range(8):
        both = []
        for g in range(2):
            span = slice(g * 8, g * 8 + 8)
            rows = []
            for i in range(r - 2, r + 3):
                if i <= 1 and r <= 3:
                    rows.append(delta[i + 2, span, :])
                elif i >= 6 and r >= 4:
                    rows.append(delta[i - 2, span, :])
                else:
                    rows.append(None)
            center = rows[2] is not None
            value = stencil_row(
                rows, own_wind(1, 0, r), own_wind(1, 1, r) if center else None, nu
            )
            both.append(begun[r, span, :] + value)
        whole = jnp.concatenate(both, 0).astype(BF)
        if field == 0:
            outs[r // 4][r % 4] = whole
        else:
            outs[0][4 + r] = whole
    if field == 1:
        outs[0][0:4] = refs[0][...]


def gram_kernel(pos, own, mate, far, diag, root, rooted, out, spread):
    parts = [v[...].astype(F32) for v in (own, mate, far, diag)]
    total = (parts[0] + parts[1]) + (parts[2] + parts[3])
    mean = jnp.sum(total, 0, keepdims=True) * (1.0 / REPLICA_COUNT)
    weight = root[...]
    gap = rooted[...] - weight * mean
    for g in range(4):
        spread[jnp.bitwise_xor(pos[2], g)] = ((parts[g] - mean) * weight).astype(BF)
    high = gap.astype(BF).astype(F32)
    slots = root.shape[1]
    pair = jnp.concatenate([high, gap - high, jnp.zeros((14, slots), F32)], 0)
    spread[4] = pair.astype(BF)
    left = spread[...].reshape(80, slots)
    right = spread[0:4].reshape(64, slots)
    out[...] = lax.dot_general(
        left, right, (((1,), (1,)), ((), ())), preferred_element_type=F32
    )


def exact(a, b):
    a_high = a.astype(BF)
    b_high = b.astype(BF)
    a_low = (a - a_high.astype(F32)).astype(BF)
    b_low = (b - b_high.astype(F32)).astype(BF)

    def product(x, y):
        return jnp.dot(x, y, preferred_element_type=F32)

    return product(a_high, b_high) + (product(a_high, b_low) + product(a_low, b_high))


def weights_kernel(pos, one, two, out, keep):
    total = one[...] + two[...]
    gram = total[0:64]
    drive = total[64:65] + total[65:66]
    row = lax.broadcasted_iota(jnp.int32, (64, 64), 0)
    col = lax.broadcasted_iota(jnp.int32, (64, 64), 1)
    ident = jnp.where(row == col, 1.0, 0.0)
    system = (REPLICA_COUNT - 1.0) * ident + gram
    square = jnp.sum(jnp.sum(system * system, 1, keepdims=True), 0, keepdims=True)
    scale = jnp.sqrt(square)
    root = system / scale
    inverse_root = ident
    for turn in range(NS_ITERS):
        if turn == 0:
            middle = 0.5 * (3.0 * ident - root)
            inverse_next = middle
        else:
            middle = 0.5 * (3.0 * ident - exact(inverse_root, root))
            inverse_next = exact(middle, inverse_root)
        if turn < NS_ITERS - 1:
            root = exact(root, middle)
        inverse_root = inverse_next
    half = inverse_root / jnp.sqrt(scale)
    drive8 = jnp.broadcast_to(drive, (8, 64))
    mean_weight = exact(exact(drive8, half), half)[0:1]
    transform_t = (mean_weight + (REPLICA_COUNT - 1.0) ** 0.5 * half).astype(BF).astype(F32)
    total_t = jnp.sum(transform_t, 1, keepdims=True)
    keep[...] = transform_t + (1.0 - total_t) * (1.0 / REPLICA_COUNT)
    mine = keep[pl.ds(pl.multiple_of(pos[2] * 16, 16), 16), :]
    swap1 = jnp.concatenate([mine[:, 16:32], mine[:, 0:16], mine[:, 48:64], mine[:, 32:48]], 1)
    mine = jnp.where((pos[2] % 2) == 1, swap1, mine)
    swap2 = jnp.concatenate([mine[:, 32:64], mine[:, 0:32]], 1)
    mine = jnp.where(pos[2] >= 2, swap2, mine)
    high = mine.astype(BF).astype(F32)
    out[...] = jnp.concatenate([high, mine - high], 0).astype(BF)


def final_kernel(
    weights, own, mate, far, diag, own_more, mate_more, far_more, diag_more, out, keep, ready, sems
):
    m = weights[...]
    copies = []
    for f in range(2):
        for r in range(8):
            first = f == 0 and r < 4
            refs = (own, mate, far, diag) if first else (own_more, mate_more, far_more, diag_more)
            at = r if first else f * 8 + r - 4
            state = jnp.concatenate([v[at] for v in refs], 0)
            both = jnp.dot(m, state, preferred_element_type=F32)
            keep[r] = both[0:16] + both[16:32]
        ready[f] = jnp.swapaxes(keep[...], 0, 1)
        copies.append(pltpu.make_async_copy(ready.at[f], out.at[:, f], sems.at[f]))
        copies[f].start()
    for f in range(2):
        copies[f].wait()


def local(prior_replicas, wind_field, obs_index, obs_count, obs_value, obs_weight):
    cols = prior_replicas.shape[3]
    strips = lax.axis_size("space")
    here = lax.axis_index("space")
    group = lax.axis_index("mem")
    pos = jnp.stack([here, jnp.int32(strips), group]).astype(jnp.int32)
    shape = jax.ShapeDtypeStruct
    pairs_a = [(i, i ^ 1) for i in range(strips)]
    pairs_b = [(i, i + 1) for i in range(1, strips - 1, 2)]
    pairs_b = pairs_b + [(j, i) for i, j in pairs_b]

    def swap(value, bits):
        return lax.ppermute(value, "mem", [(i, i ^ bits) for i in range(4)])

    prior_here = pltpu.with_memory_space_constraint(prior_replicas, pltpu.MemorySpace.HBM)
    wind_here = pltpu.with_memory_space_constraint(wind_field, pltpu.MemorySpace.HBM)

    packed = pl.pallas_call(
        pack_kernel,
        name="pack",
        cost_estimate=cost(80 * 16 * cols * 4),
        in_specs=[smem(), hbm(), hbm()],
        out_specs=[vmem()] * 4,
        out_shape=[shape((12, 16, cols + PAD), F32)] * 2
        + [shape((136, cols), BF)] * 2,
        scratch_shapes=[
            pltpu.VMEM((2, 16, 8, cols), F32),
            pltpu.VMEM((2, 8, cols), F32),
            pltpu.SemaphoreType.DMA((3,)),
        ],
        compiler_params=params(),
    )(pos, prior_here, wind_here)
    turned = packed[0:2]
    recv_a = lax.ppermute(packed[2], "space", pairs_a)
    recv_b = lax.ppermute(packed[3], "space", pairs_b)

    def pre(f, rows):
        return pl.pallas_call(
            functools.partial(pre_kernel, DIFFUSION[f]),
            name="pre",
            cost_estimate=cost(150 * 16 * cols * 4),
            in_specs=[vmem()] * 2,
            out_specs=vmem(),
            out_shape=shape((8, 16, cols), F32),
            scratch_shapes=[
                pltpu.VMEM((12, 16, cols + PAD), F32),
                pltpu.VMEM((2, 2, 8, 8, cols), F32),
            ],
            compiler_params=params(),
        )(rows, wind_field)

    begun = [pre(f, turned[f]) for f in range(2)]

    slots = obs_index.shape[0]
    width = 512
    place, chunk, root, rooted = pl.pallas_call(
        slots_kernel,
        name="slots",
        cost_estimate=cost(width * slots * 2),
        in_specs=[vmem(), smem(), vmem(), vmem()],
        out_specs=[vmem()] * 4,
        out_shape=[
            shape((width, slots), BF),
            shape((16, slots), jnp.int32),
            shape((1, slots), F32),
            shape((1, slots), F32),
        ],
        compiler_params=params(),
    )(
        obs_index.reshape(1, slots),
        obs_count,
        obs_weight.reshape(1, slots),
        obs_value.reshape(1, slots),
    )
    recv_a, begun[0], begun[1], place = lax.optimization_barrier(
        (recv_a, begun[0], begun[1], place)
    )

    def post(f, extra):
        heights = (4, 4) if f == 0 else (12,)
        return pl.pallas_call(
            functools.partial(post_kernel, f),
            name="post",
            cost_estimate=cost(8),
            in_specs=[smem()] + [vmem()] * (5 + f),
            out_specs=[vmem()] * len(heights),
            out_shape=[shape((v, 16, cols), BF) for v in heights],
            scratch_shapes=[
                pltpu.VMEM((8, 16, cols + PAD), F32),
                pltpu.VMEM((8, 16, cols + PAD), F32),
            ],
            compiler_params=params(),
        )(pos, turned[f], begun[f], recv_a, recv_b, wind_field, *extra)

    one, two = post(0, [])
    far_one = swap(one, 2)
    more = post(1, [two])[0]
    seen = pl.pallas_call(
        pick_kernel,
        name="pick",
        cost_estimate=cost(8),
        in_specs=[vmem()] * 4,
        out_specs=vmem(),
        out_shape=shape((16, slots), BF),
        scratch_shapes=[pltpu.VMEM((16 * 16 * cols // width, width), BF)],
        compiler_params=params(),
    )(place, chunk, one, more)

    seen_far = swap(seen, 2)
    seen_mate = swap(seen, 1)
    seen_far, far_one, late = lax.optimization_barrier((seen_far, far_one, more))
    far_more = swap(late, 2)
    seen_diag = swap(seen_far, 1)

    part = pl.pallas_call(
        gram_kernel,
        name="gram",
        cost_estimate=cost(24 * 64 * slots),
        in_specs=[smem()] + [vmem()] * 6,
        out_specs=vmem(),
        out_shape=shape((80, 64), F32),
        scratch_shapes=[pltpu.VMEM((5, 16, slots), BF)],
        compiler_params=params(),
    )(pos, seen, seen_mate, seen_far, seen_diag, root, rooted)

    mate_more = swap(more, 1)
    mate_one = swap(one, 1)
    diag_one = swap(far_one, 1)
    bits = 1
    other = None
    while bits < strips:
        if other is not None:
            part = part + other
            part, mate_one, diag_one = lax.optimization_barrier((part, mate_one, diag_one))
        other = lax.ppermute(part, "space", [(i, i ^ bits) for i in range(strips)])
        bits *= 2
    late, _ = lax.optimization_barrier((far_more, other))
    diag_more = swap(late, 1)

    weights = pl.pallas_call(
        weights_kernel,
        name="weights",
        cost_estimate=cost(400 * 64 * 128 * 4),
        in_specs=[smem(), vmem(), vmem()],
        out_specs=vmem(),
        out_shape=shape((32, 64), BF),
        scratch_shapes=[pltpu.VMEM((64, 64), F32)],
        compiler_params=params(),
    )(pos, part, other)

    return pl.pallas_call(
        final_kernel,
        name="final",
        cost_estimate=cost(100 * 16 * cols * 4),
        in_specs=[vmem()] * 9,
        out_specs=hbm(),
        out_shape=shape(prior_replicas.shape, F32),
        scratch_shapes=[
            pltpu.VMEM((8, 16, cols), F32),
            pltpu.VMEM((2, 16, 8, cols), F32),
            pltpu.SemaphoreType.DMA((2,)),
        ],
        compiler_params=params(),
    )(
        weights, one, mate_one, far_one, diag_one, more, mate_more, far_more, diag_more
    )


def solution(mesh):
    in_specs = (
        P(("parts", "mem"), None, "space", None),
        P("parts", None, "space", None),
        P(("parts", "space")),
        P(("parts", "space")),
        P(("parts", "space")),
        P(("parts", "space")),
    )
    out_specs = P(("parts", "mem"), None, "space", None)
    strips = mesh.shape["space"]
    fast = mesh.shape["mem"] == 4 and strips > 1 and strips & (strips - 1) == 0
    body = local if fast else local_generic
    return jax.shard_map(body, mesh=mesh, in_specs=in_specs, out_specs=out_specs, check_vma=False)
```

```python
import functools

import jax
import jax.numpy as jnp
from jax import lax
from jax.experimental import pallas as pl
from jax.experimental.pallas import tpu as pltpu
from jax.sharding import PartitionSpec as P

REPLICA_COUNT = 64
NS_ITERS = 5


DIFFUSION = (0.05, 0.15)


def padded(value, sides, width):
    for axis, dim in sides:
        peers, length = (lax.axis_size(axis), value.shape[dim])
        up = [(i, (i + 1) % peers) for i in range(peers - 1)]
        down = [(j, i) for i, j in up]
        last = lax.slice_in_dim(value, length - width, length, axis=dim)
        initial = lax.slice_in_dim(value, 0, width, axis=dim)
        before = lax.ppermute(last, axis, up)
        after = lax.ppermute(initial, axis, down)
        value = jnp.concatenate([before, value, after], axis=dim)
    return value


def shift_columns(field, offset):
    width = field.shape[-1]
    blank = jnp.zeros(field.shape[:-1] + (abs(offset),), field.dtype)
    if offset > 0:
        return jnp.concatenate([field[..., offset:], blank], -1)
    return jnp.concatenate([blank, field[..., : width + offset]], -1)


def advance(extended, wind_rows):
    center = extended[:, :, 2:-2]
    north_one = extended[:, :, 3:-1]
    south_one = extended[:, :, 1:-3]
    north_two = extended[:, :, 4:]
    south_two = extended[:, :, :-4]
    east_one = shift_columns(center, 1)
    west_one = shift_columns(center, -1)
    east_two = shift_columns(center, 2)
    west_two = shift_columns(center, -2)
    grad_row = (8.0 * (north_one - south_one) - (north_two - south_two)) / 12.0
    grad_col = (8.0 * (east_one - west_one) - (east_two - west_two)) / 12.0
    laplace = north_one + south_one + east_one + west_one - 4.0 * center
    diffusion = jnp.array(DIFFUSION, jnp.float32).reshape(2, 1, 1)
    return center - wind_rows[0] * grad_row - wind_rows[1] * grad_col + diffusion * laplace


def shard_terms(observed, slot_weight, obs_value):
    obs_mean = jnp.sum(observed, 0) / REPLICA_COUNT
    obs_anomaly = observed - obs_mean
    weighted = obs_anomaly * slot_weight
    gram = jnp.dot(
        weighted, obs_anomaly.T, precision=lax.Precision.HIGHEST, preferred_element_type=jnp.float32
    )
    drive = jnp.dot(
        weighted,
        obs_value - obs_mean,
        precision=lax.Precision.HIGHEST,
        preferred_element_type=jnp.float32,
    )
    return (gram, drive)


def ensemble_weights(gram, drive):
    ident = jnp.eye(REPLICA_COUNT, dtype=jnp.float32)
    system = (REPLICA_COUNT - 1.0) * ident + gram
    scale = jnp.sqrt(jnp.sum(system * system))

    def newton_turn(turn, carry):
        root, inverse_root = carry
        middle_term = 0.5 * (
            3.0 * ident
            - jnp.dot(
                inverse_root,
                root,
                precision=lax.Precision.HIGHEST,
                preferred_element_type=jnp.float32,
            )
        )
        root = jnp.dot(
            root, middle_term, precision=lax.Precision.HIGHEST, preferred_element_type=jnp.float32
        )
        inverse_root = jnp.dot(
            middle_term,
            inverse_root,
            precision=lax.Precision.HIGHEST,
            preferred_element_type=jnp.float32,
        )
        return (root, inverse_root)

    root, inverse_root = lax.fori_loop(0, NS_ITERS, newton_turn, (system / scale, ident))
    half = inverse_root / jnp.sqrt(scale)
    precision_matrix = jnp.dot(
        half, half, precision=lax.Precision.HIGHEST, preferred_element_type=jnp.float32
    )
    mean_weight = jnp.dot(
        precision_matrix, drive, precision=lax.Precision.HIGHEST, preferred_element_type=jnp.float32
    )
    spread = jnp.sqrt(REPLICA_COUNT - 1.0) * half
    return (mean_weight[:, None] + spread).astype(jnp.bfloat16)


def local_generic(prior_replicas, wind_field, obs_index, obs_count, obs_value, obs_weight):
    member_count, field_count, row_count, col_count = prior_replicas.shape
    state = prior_replicas
    for step_index in range(2):
        extended = padded(state, (("space", 2),), 2)
        state = advance(extended, wind_field[step_index])
    capacity = obs_index.shape[0]
    raveled_vector = state.reshape(member_count, -1)
    local_obs = jnp.take(raveled_vector, obs_index, axis=1)
    slot_number = jnp.arange(capacity, dtype=jnp.int32)
    slot_weight = obs_weight * (slot_number < obs_count[0]).astype(jnp.float32)
    gathered = lax.all_gather(local_obs, "mem", axis=0, tiled=True)
    gram, drive = shard_terms(gathered, slot_weight, obs_value)
    gram, drive = lax.psum((gram, drive), "space")
    transform = ensemble_weights(gram, drive)
    transform_rows = transform.T
    block = lax.all_to_all(state, "mem", split_axis=3, concat_axis=0, tiled=True)
    replica_centroid = jnp.sum(block, 0) / REPLICA_COUNT
    replica_departure = (block - replica_centroid).astype(jnp.bfloat16)
    posterior_correction = jnp.dot(
        transform_rows,
        replica_departure.reshape(REPLICA_COUNT, -1),
        preferred_element_type=jnp.float32,
    )
    analysed = posterior_correction.reshape(block.shape) + replica_centroid
    return lax.all_to_all(analysed, "mem", split_axis=0, concat_axis=3, tiled=True)


BF = jnp.bfloat16
F32 = jnp.float32
PAD = 128


def vmem():
    return pl.BlockSpec(memory_space=pltpu.VMEM)


def smem():
    return pl.BlockSpec(memory_space=pltpu.SMEM)


def hbm():
    return pl.BlockSpec(memory_space=pltpu.MemorySpace.HBM)


def params():
    return pltpu.CompilerParams(vmem_limit_bytes=44 * 1024 * 1024)


def cost(touched):
    return pl.CostEstimate(flops=touched, bytes_accessed=touched, transcendentals=0)


def blank_edges(rows):
    width = rows.shape[2]
    for r in (0, 1, 10, 11):
        rows[r] = jnp.zeros((16, width), F32)
    for r in range(2, 10):
        rows[r, :, width - PAD :] = jnp.zeros((16, PAD), F32)


def pack_kernel(
    pos, prior, wind, turned_0, turned_1, pay_a, pay_b, state, edge, sems
):
    winds = pltpu.make_async_copy(wind.at[0], edge, sems.at[4])
    loads = {}
    for f in range(2):
        for g in range(2):
            span = slice(8 * g, 8 * g + 8)
            loads[f, g] = pltpu.make_async_copy(
                prior.at[span, f], state.at[f, span], sems.at[2 * f + g]
            )
            loads[f, g].start()
    winds.start()
    even = (pos[0] % 2) == 0
    start_a = jnp.where(even, 4, 0)
    start_b = 4 - start_a
    cols = state.shape[3]
    blank_edges(turned_0)
    blank_edges(turned_1)
    for f in range(2):
        turned = (turned_0, turned_1)[f]
        for g in range(2):
            span = slice(8 * g, 8 * g + 8)
            loads[f, g].wait()
            turned[2:10, span, :cols] = jnp.swapaxes(state[f, span], 0, 1)
        for r in range(4):
            at = (f * 4 + r) * 16
            pay_a[at : at + 16, :] = turned[2 + start_a + r, :, :cols].astype(BF)
            pay_b[at : at + 16, :] = turned[2 + start_b + r, :, :cols].astype(BF)
    winds.wait()
    first = jnp.concatenate([edge[0, 0:2], edge[1, 0:2]], 0)
    last = jnp.concatenate([edge[0, 6:8], edge[1, 6:8]], 0)
    first_high = first.astype(BF).astype(F32)
    last_high = last.astype(BF).astype(F32)
    first = jnp.concatenate([first_high, first - first_high], 0)
    last = jnp.concatenate([last_high, last - last_high], 0)
    pay_a[128:136, :] = jnp.where(even, last, first).astype(BF)
    pay_b[128:136, :] = jnp.where(even, first, last).astype(BF)


def slots_kernel(index, count, weight, value, place, chunk, root_out, rooted_out):
    slots = index.shape[1]
    width = place.shape[0]
    n = index[...]
    used = lax.broadcasted_iota(jnp.int32, (1, slots), 1) < count[0]
    root = jnp.where(used, jnp.sqrt(weight[...]), 0.0)
    root_out[...] = root
    rooted_out[...] = root * value[...]
    chunk[...] = jnp.broadcast_to(n // width, (16, slots))
    column = n % width
    step = 64
    for r in range(0, width, step):
        hit = lax.broadcasted_iota(jnp.int32, (step, slots), 0) == column - r
        place[r : r + step, :] = jnp.where(hit, 1.0, 0.0).astype(BF)


def pick_kernel(place, chunk, one, more, out, tall):
    width, slots = place.shape
    parts = one.shape[2] // width
    at = 0
    for ref in (one, more):
        for r in range(ref.shape[0]):
            for p in range(parts):
                tall[at * 16 : at * 16 + 16, :] = ref[r, :, p * width : (p + 1) * width]
                at += 1
    count = at
    step = 256
    for o in range(0, slots, step):
        cut = slice(o, o + step)
        seen = jnp.dot(tall[...], place[:, cut], preferred_element_type=F32)
        number = chunk[:, cut]
        total = jnp.zeros((16, step), F32)
        for at in range(count):
            total = total + jnp.where(number == at, seen[at * 16 : at * 16 + 16], 0.0)
        out[:, cut] = total.astype(BF)


def stencil_row(rows, wind_r, wind_c, nu):
    south_two, south_one, center, north_one, north_two = rows
    width = [v for v in rows if v is not None][0].shape[1]
    keep = width - PAD

    def less(a, b):
        if a is None:
            return None if b is None else -b
        return a if b is None else a - b

    def more(a, b):
        if a is None or b is None:
            return b if a is None else a
        return a + b

    rows = [None if v is None else v[:, :keep] for v in rows]
    one = less(rows[3], rows[1])
    grad_r = less(None if one is None else 8.0 * one, less(rows[4], rows[0]))
    ring = more(rows[3], rows[1])
    out = -(wind_r * grad_r)
    if center is not None:
        east_one = pltpu.roll(center, width - 1, 1)
        west_one = pltpu.roll(center, 1, 1)
        east_two = pltpu.roll(center, width - 2, 1)
        west_two = pltpu.roll(center, 2, 1)
        grad_c = 8.0 * (east_one - west_one) - (east_two - west_two)
        ring = more(ring, (east_one + west_one)[:, :keep])
        out = (1.0 - 4.0 * nu) * rows[2] + out - wind_c * grad_c[:, :keep]
    return out if ring is None else out + nu * ring


TWELFTH = 1.0 / 12.0


def pre_kernel(nu, turned, wind, out, mid, wide):
    cols = out.shape[2]
    blank_edges(mid)
    for step in range(2):
        for c in range(2):
            for r in range(8):
                wide[step, c, r] = jnp.broadcast_to(wind[step, c, r : r + 1] * TWELFTH, (8, cols))

    def first_step(r, carry):
        for g in range(2):
            span = pl.ds(g * 8, 8)
            rows = [turned[r + i, span, :] for i in range(5)]
            mid[r + 2, span, :cols] = stencil_row(rows, wide[0, 0, r], wide[0, 1, r], nu)
        return carry

    lax.fori_loop(0, 8, first_step, 0)

    def second_step(r, carry):
        for g in range(2):
            span = pl.ds(g * 8, 8)
            rows = [mid[r + i, span, :] for i in range(5)]
            out[r, span, :] = stencil_row(rows, wide[1, 0, r], wide[1, 1, r], nu)
        return carry

    lax.fori_loop(0, 8, second_step, 0)


def post_kernel(field, pos, turned, begun, recv_a, recv_b, wind, *refs):
    outs = refs[-4:-2] if field == 0 else refs[-3:-2]
    halo, delta = refs[-2:]
    nu = DIFFUSION[field]
    cols = begun.shape[2]
    even = (pos[0] % 2) == 0
    start_a = jnp.where(even, 4, 0)
    start_b = 4 - start_a
    blank = jnp.zeros((16, PAD), F32)
    for r in range(8):
        halo[r, :, cols:] = blank
        delta[r, :, cols:] = blank
    for r in range(4):
        at = (field * 4 + r) * 16
        halo[start_a + r, :, :cols] = recv_a[at : at + 16, :].astype(F32)
        halo[start_b + r, :, :cols] = recv_b[at : at + 16, :].astype(F32)
    got_a = recv_a[128:136, :].astype(F32)
    got_a = got_a[0:4] + got_a[4:8]
    got_b = recv_b[128:136, :].astype(F32)
    got_b = got_b[0:4] + got_b[4:8]
    top = jnp.where(pos[0] == 0, 0.0, 1.0)
    bottom = jnp.where(pos[0] == pos[1] - 1, 0.0, 1.0)
    before = jnp.where(even, got_b, got_a) * TWELFTH
    after = jnp.where(even, got_a, got_b) * TWELFTH

    def broad(row):
        return jnp.broadcast_to(row, (8, cols))

    def own_wind(step, c, r):
        return broad(wind[step, c, r : r + 1] * TWELFTH)

    for g in range(2):
        span = slice(g * 8, g * 8 + 8)
        h = lambda i: halo[i, span, :]
        x = lambda r: turned[2 + r, span, :]
        for i in range(2):
            rows = [h(0), h(1), h(2), h(3), x(0)] if i == 0 else [h(1), h(2), h(3), x(0), x(1)]
            value = stencil_row(rows, broad(before[i : i + 1]), broad(before[2 + i : 3 + i]), nu)
            delta[i, span, :cols] = value * top
            rows = [x(6), x(7), h(4), h(5), h(6)] if i == 0 else [x(7), h(4), h(5), h(6), h(7)]
            value = stencil_row(rows, broad(after[i : i + 1]), broad(after[2 + i : 3 + i]), nu)
            delta[6 + i, span, :cols] = value * bottom
        near = (
            (2, 0, [h(2), h(3), None, None, None]),
            (3, 1, [h(3), None, None, None, None]),
            (4, 6, [None, None, None, None, h(4)]),
            (5, 7, [None, None, None, h(4), h(5)]),
        )
        for at, r, rows in near:
            delta[at, span, :cols] = stencil_row(rows, own_wind(0, 0, r), None, nu)

    for r in range(8):
        both = []
        for g in range(2):
            span = slice(g * 8, g * 8 + 8)
            rows = []
            for i in range(r - 2, r + 3):
                if i <= 1 and r <= 3:
                    rows.append(delta[i + 2, span, :])
                elif i >= 6 and r >= 4:
                    rows.append(delta[i - 2, span, :])
                else:
                    rows.append(None)
            center = rows[2] is not None
            value = stencil_row(
                rows, own_wind(1, 0, r), own_wind(1, 1, r) if center else None, nu
            )
            both.append(begun[r, span, :] + value)
        whole = jnp.concatenate(both, 0).astype(BF)
        if field == 0:
            outs[r // 4][r % 4] = whole
        else:
            outs[0][4 + r] = whole
    if field == 1:
        outs[0][0:4] = refs[0][...]


def gram_kernel(pos, own, mate, far, diag, root, rooted, out, spread):
    parts = [v[...].astype(F32) for v in (own, mate, far, diag)]
    total = (parts[0] + parts[1]) + (parts[2] + parts[3])
    mean = jnp.sum(total, 0, keepdims=True) * (1.0 / REPLICA_COUNT)
    weight = root[...]
    gap = rooted[...] - weight * mean
    for g in range(4):
        spread[jnp.bitwise_xor(pos[2], g)] = ((parts[g] - mean) * weight).astype(BF)
    high = gap.astype(BF).astype(F32)
    slots = root.shape[1]
    pair = jnp.concatenate([high, gap - high, jnp.zeros((14, slots), F32)], 0)
    spread[4] = pair.astype(BF)
    left = spread[...].reshape(80, slots)
    right = spread[0:4].reshape(64, slots)
    out[...] = lax.dot_general(
        left, right, (((1,), (1,)), ((), ())), preferred_element_type=F32
    )


def exact(a, b):
    a_high = a.astype(BF)
    b_high = b.astype(BF)
    a_low = (a - a_high.astype(F32)).astype(BF)
    b_low = (b - b_high.astype(F32)).astype(BF)

    def product(x, y):
        return jnp.dot(x, y, preferred_element_type=F32)

    return product(a_high, b_high) + (product(a_high, b_low) + product(a_low, b_high))


def weights_kernel(pos, one, two, out, keep):
    total = one[...] + two[...]
    gram = total[0:64]
    drive = total[64:65] + total[65:66]
    row = lax.broadcasted_iota(jnp.int32, (64, 64), 0)
    col = lax.broadcasted_iota(jnp.int32, (64, 64), 1)
    ident = jnp.where(row == col, 1.0, 0.0)
    system = (REPLICA_COUNT - 1.0) * ident + gram
    square = jnp.sum(jnp.sum(system * system, 1, keepdims=True), 0, keepdims=True)
    scale = jnp.sqrt(square)
    root = system / scale
    inverse_root = ident
    for turn in range(NS_ITERS):
        if turn == 0:
            middle = 0.5 * (3.0 * ident - root)
            inverse_next = middle
        else:
            middle = 0.5 * (3.0 * ident - exact(inverse_root, root))
            inverse_next = exact(middle, inverse_root)
        if turn < NS_ITERS - 1:
            root = exact(root, middle)
        inverse_root = inverse_next
    half = inverse_root / jnp.sqrt(scale)
    drive8 = jnp.broadcast_to(drive, (8, 64))
    mean_weight = exact(exact(drive8, half), half)[0:1]
    transform_t = (mean_weight + (REPLICA_COUNT - 1.0) ** 0.5 * half).astype(BF).astype(F32)
    total_t = jnp.sum(transform_t, 1, keepdims=True)
    keep[...] = transform_t + (1.0 - total_t) * (1.0 / REPLICA_COUNT)
    mine = keep[pl.ds(pl.multiple_of(pos[2] * 16, 16), 16), :]
    swap1 = jnp.concatenate([mine[:, 16:32], mine[:, 0:16], mine[:, 48:64], mine[:, 32:48]], 1)
    mine = jnp.where((pos[2] % 2) == 1, swap1, mine)
    swap2 = jnp.concatenate([mine[:, 32:64], mine[:, 0:32]], 1)
    mine = jnp.where(pos[2] >= 2, swap2, mine)
    high = mine.astype(BF).astype(F32)
    pair = jnp.concatenate([high, mine - high], 0)
    blank = jnp.zeros((32, 64), F32)
    for r in range(4):
        line = [pair if k == r else blank for k in range(4)]
        out[r * 32 : r * 32 + 32, :] = jnp.concatenate(line, 1).astype(BF)


def final_kernel(
    weights, own, mate, far, diag, own_more, mate_more, far_more, diag_more, out, keep, ready, sems
):
    copies = []
    cols = own.shape[2]
    step = 512
    half = cols // 2
    for f in range(2):
        for part in range(2):
            span = slice(part * half, part * half + half)
            for base in (0, 4):
                first = f == 0 and base == 0
                refs = (own, mate, far, diag) if first else (own_more, mate_more, far_more, diag_more)
                at = 0 if first else f * 8 + base - 4
                for c in range(part * half, part * half + half, step):
                    cut = slice(c, c + step)
                    parts = [v[at + r, :, cut] for r in range(4) for v in refs]
                    both = jnp.dot(
                        weights[...], jnp.concatenate(parts, 0), preferred_element_type=F32
                    )
                    for r in range(4):
                        high = both[r * 32 : r * 32 + 16]
                        keep[base + r, :, cut] = high + both[r * 32 + 16 : r * 32 + 32]
            ready[f, :, :, span] = jnp.swapaxes(keep[:, :, span], 0, 1)
            copies.append(
                pltpu.make_async_copy(
                    ready.at[f, :, :, span], out.at[:, f, :, span], sems.at[2 * f + part]
                )
            )
            copies[-1].start()
    for copy in copies:
        copy.wait()


def local(prior_replicas, wind_field, obs_index, obs_count, obs_value, obs_weight):
    cols = prior_replicas.shape[3]
    strips = lax.axis_size("space")
    here = lax.axis_index("space")
    group = lax.axis_index("mem")
    pos = jnp.stack([here, jnp.int32(strips), group]).astype(jnp.int32)
    shape = jax.ShapeDtypeStruct
    pairs_a = [(i, i ^ 1) for i in range(strips)]
    pairs_b = [(i, i + 1) for i in range(1, strips - 1, 2)]
    pairs_b = pairs_b + [(j, i) for i, j in pairs_b]

    def swap(value, bits):
        return lax.ppermute(value, "mem", [(i, i ^ bits) for i in range(4)])

    prior_here = pltpu.with_memory_space_constraint(prior_replicas, pltpu.MemorySpace.HBM)
    wind_here = pltpu.with_memory_space_constraint(wind_field, pltpu.MemorySpace.HBM)

    packed = pl.pallas_call(
        pack_kernel,
        name="pack",
        cost_estimate=cost(80 * 16 * cols * 4),
        in_specs=[smem(), hbm(), hbm()],
        out_specs=[vmem()] * 4,
        out_shape=[shape((12, 16, cols + PAD), F32)] * 2
        + [shape((136, cols), BF)] * 2,
        scratch_shapes=[
            pltpu.VMEM((2, 16, 8, cols), F32),
            pltpu.VMEM((2, 8, cols), F32),
            pltpu.SemaphoreType.DMA((5,)),
        ],
        compiler_params=params(),
    )(pos, prior_here, wind_here)
    turned = packed[0:2]
    recv_a = lax.ppermute(packed[2], "space", pairs_a)
    recv_b = lax.ppermute(packed[3], "space", pairs_b)

    def pre(f, rows):
        return pl.pallas_call(
            functools.partial(pre_kernel, DIFFUSION[f]),
            name="pre",
            cost_estimate=cost(150 * 16 * cols * 4),
            in_specs=[vmem()] * 2,
            out_specs=vmem(),
            out_shape=shape((8, 16, cols), F32),
            scratch_shapes=[
                pltpu.VMEM((12, 16, cols + PAD), F32),
                pltpu.VMEM((2, 2, 8, 8, cols), F32),
            ],
            compiler_params=params(),
        )(rows, wind_field)

    begun = [pre(f, turned[f]) for f in range(2)]

    slots = obs_index.shape[0]
    width = 512
    place, chunk, root, rooted = pl.pallas_call(
        slots_kernel,
        name="slots",
        cost_estimate=cost(width * slots * 2),
        in_specs=[vmem(), smem(), vmem(), vmem()],
        out_specs=[vmem()] * 4,
        out_shape=[
            shape((width, slots), BF),
            shape((16, slots), jnp.int32),
            shape((1, slots), F32),
            shape((1, slots), F32),
        ],
        compiler_params=params(),
    )(
        obs_index.reshape(1, slots),
        obs_count,
        obs_weight.reshape(1, slots),
        obs_value.reshape(1, slots),
    )
    recv_a, begun[0], begun[1], place = lax.optimization_barrier(
        (recv_a, begun[0], begun[1], place)
    )

    def post(f, extra):
        heights = (4, 4) if f == 0 else (12,)
        return pl.pallas_call(
            functools.partial(post_kernel, f),
            name="post",
            cost_estimate=cost(8),
            in_specs=[smem()] + [vmem()] * (5 + f),
            out_specs=[vmem()] * len(heights),
            out_shape=[shape((v, 16, cols), BF) for v in heights],
            scratch_shapes=[
                pltpu.VMEM((8, 16, cols + PAD), F32),
                pltpu.VMEM((8, 16, cols + PAD), F32),
            ],
            compiler_params=params(),
        )(pos, turned[f], begun[f], recv_a, recv_b, wind_field, *extra)

    one, two = post(0, [])
    far_one = swap(one, 2)
    more = post(1, [two])[0]
    seen = pl.pallas_call(
        pick_kernel,
        name="pick",
        cost_estimate=cost(8),
        in_specs=[vmem()] * 4,
        out_specs=vmem(),
        out_shape=shape((16, slots), BF),
        scratch_shapes=[pltpu.VMEM((16 * 16 * cols // width, width), BF)],
        compiler_params=params(),
    )(place, chunk, one, more)

    seen_far = swap(seen, 2)
    seen_mate = swap(seen, 1)
    seen_far, far_one, late = lax.optimization_barrier((seen_far, far_one, more))
    far_more = swap(late, 2)
    seen_diag = swap(seen_far, 1)

    part = pl.pallas_call(
        gram_kernel,
        name="gram",
        cost_estimate=cost(24 * 64 * slots),
        in_specs=[smem()] + [vmem()] * 6,
        out_specs=vmem(),
        out_shape=shape((80, 64), F32),
        scratch_shapes=[pltpu.VMEM((5, 16, slots), BF)],
        compiler_params=params(),
    )(pos, seen, seen_mate, seen_far, seen_diag, root, rooted)

    mate_more = swap(more, 1)
    mate_one = swap(one, 1)
    diag_one = swap(far_one, 1)
    bits = 1
    other = None
    while bits < strips:
        if other is not None:
            part = part + other
            part, mate_one, diag_one = lax.optimization_barrier((part, mate_one, diag_one))
        other = lax.ppermute(part, "space", [(i, i ^ bits) for i in range(strips)])
        bits *= 2
    late, _ = lax.optimization_barrier((far_more, other))
    diag_more = swap(late, 1)

    weights = pl.pallas_call(
        weights_kernel,
        name="weights",
        cost_estimate=cost(400 * 64 * 128 * 4),
        in_specs=[smem(), vmem(), vmem()],
        out_specs=vmem(),
        out_shape=shape((128, 256), BF),
        scratch_shapes=[pltpu.VMEM((64, 64), F32)],
        compiler_params=params(),
    )(pos, part, other)

    return pl.pallas_call(
        final_kernel,
        name="final",
        cost_estimate=cost(100 * 16 * cols * 4),
        in_specs=[vmem()] * 9,
        out_specs=hbm(),
        out_shape=shape(prior_replicas.shape, F32),
        scratch_shapes=[
            pltpu.VMEM((8, 16, cols), F32),
            pltpu.VMEM((2, 16, 8, cols), F32),
            pltpu.SemaphoreType.DMA((4,)),
        ],
        compiler_params=params(),
    )(
        weights, one, mate_one, far_one, diag_one, more, mate_more, far_more, diag_more
    )


def solution(mesh):
    in_specs = (
        P(("parts", "mem"), None, "space", None),
        P("parts", None, "space", None),
        P(("parts", "space")),
        P(("parts", "space")),
        P(("parts", "space")),
        P(("parts", "space")),
    )
    out_specs = P(("parts", "mem"), None, "space", None)
    strips = mesh.shape["space"]
    fast = mesh.shape["mem"] == 4 and strips > 1 and strips & (strips - 1) == 0
    body = local if fast else local_generic
    return jax.shard_map(body, mesh=mesh, in_specs=in_specs, out_specs=out_specs, check_vma=False)
```

```python
import functools

import jax
import jax.numpy as jnp
from jax import lax
from jax.experimental import pallas as pl
from jax.experimental.pallas import tpu as pltpu
from jax.sharding import PartitionSpec as P

REPLICA_COUNT = 64
NS_ITERS = 5


DIFFUSION = (0.05, 0.15)


def padded(value, sides, width):
    for axis, dim in sides:
        peers, length = (lax.axis_size(axis), value.shape[dim])
        up = [(i, (i + 1) % peers) for i in range(peers - 1)]
        down = [(j, i) for i, j in up]
        last = lax.slice_in_dim(value, length - width, length, axis=dim)
        initial = lax.slice_in_dim(value, 0, width, axis=dim)
        before = lax.ppermute(last, axis, up)
        after = lax.ppermute(initial, axis, down)
        value = jnp.concatenate([before, value, after], axis=dim)
    return value


def shift_columns(field, offset):
    width = field.shape[-1]
    blank = jnp.zeros(field.shape[:-1] + (abs(offset),), field.dtype)
    if offset > 0:
        return jnp.concatenate([field[..., offset:], blank], -1)
    return jnp.concatenate([blank, field[..., : width + offset]], -1)


def advance(extended, wind_rows):
    center = extended[:, :, 2:-2]
    north_one = extended[:, :, 3:-1]
    south_one = extended[:, :, 1:-3]
    north_two = extended[:, :, 4:]
    south_two = extended[:, :, :-4]
    east_one = shift_columns(center, 1)
    west_one = shift_columns(center, -1)
    east_two = shift_columns(center, 2)
    west_two = shift_columns(center, -2)
    grad_row = (8.0 * (north_one - south_one) - (north_two - south_two)) / 12.0
    grad_col = (8.0 * (east_one - west_one) - (east_two - west_two)) / 12.0
    laplace = north_one + south_one + east_one + west_one - 4.0 * center
    diffusion = jnp.array(DIFFUSION, jnp.float32).reshape(2, 1, 1)
    return center - wind_rows[0] * grad_row - wind_rows[1] * grad_col + diffusion * laplace


def shard_terms(observed, slot_weight, obs_value):
    obs_mean = jnp.sum(observed, 0) / REPLICA_COUNT
    obs_anomaly = observed - obs_mean
    weighted = obs_anomaly * slot_weight
    gram = jnp.dot(
        weighted, obs_anomaly.T, precision=lax.Precision.HIGHEST, preferred_element_type=jnp.float32
    )
    drive = jnp.dot(
        weighted,
        obs_value - obs_mean,
        precision=lax.Precision.HIGHEST,
        preferred_element_type=jnp.float32,
    )
    return (gram, drive)


def ensemble_weights(gram, drive):
    ident = jnp.eye(REPLICA_COUNT, dtype=jnp.float32)
    system = (REPLICA_COUNT - 1.0) * ident + gram
    scale = jnp.sqrt(jnp.sum(system * system))

    def newton_turn(turn, carry):
        root, inverse_root = carry
        middle_term = 0.5 * (
            3.0 * ident
            - jnp.dot(
                inverse_root,
                root,
                precision=lax.Precision.HIGHEST,
                preferred_element_type=jnp.float32,
            )
        )
        root = jnp.dot(
            root, middle_term, precision=lax.Precision.HIGHEST, preferred_element_type=jnp.float32
        )
        inverse_root = jnp.dot(
            middle_term,
            inverse_root,
            precision=lax.Precision.HIGHEST,
            preferred_element_type=jnp.float32,
        )
        return (root, inverse_root)

    root, inverse_root = lax.fori_loop(0, NS_ITERS, newton_turn, (system / scale, ident))
    half = inverse_root / jnp.sqrt(scale)
    precision_matrix = jnp.dot(
        half, half, precision=lax.Precision.HIGHEST, preferred_element_type=jnp.float32
    )
    mean_weight = jnp.dot(
        precision_matrix, drive, precision=lax.Precision.HIGHEST, preferred_element_type=jnp.float32
    )
    spread = jnp.sqrt(REPLICA_COUNT - 1.0) * half
    return (mean_weight[:, None] + spread).astype(jnp.bfloat16)


def local_generic(prior_replicas, wind_field, obs_index, obs_count, obs_value, obs_weight):
    member_count, field_count, row_count, col_count = prior_replicas.shape
    state = prior_replicas
    for step_index in range(2):
        extended = padded(state, (("space", 2),), 2)
        state = advance(extended, wind_field[step_index])
    capacity = obs_index.shape[0]
    raveled_vector = state.reshape(member_count, -1)
    local_obs = jnp.take(raveled_vector, obs_index, axis=1)
    slot_number = jnp.arange(capacity, dtype=jnp.int32)
    slot_weight = obs_weight * (slot_number < obs_count[0]).astype(jnp.float32)
    gathered = lax.all_gather(local_obs, "mem", axis=0, tiled=True)
    gram, drive = shard_terms(gathered, slot_weight, obs_value)
    gram, drive = lax.psum((gram, drive), "space")
    transform = ensemble_weights(gram, drive)
    transform_rows = transform.T
    block = lax.all_to_all(state, "mem", split_axis=3, concat_axis=0, tiled=True)
    replica_centroid = jnp.sum(block, 0) / REPLICA_COUNT
    replica_departure = (block - replica_centroid).astype(jnp.bfloat16)
    posterior_correction = jnp.dot(
        transform_rows,
        replica_departure.reshape(REPLICA_COUNT, -1),
        preferred_element_type=jnp.float32,
    )
    analysed = posterior_correction.reshape(block.shape) + replica_centroid
    return lax.all_to_all(analysed, "mem", split_axis=0, concat_axis=3, tiled=True)


BF = jnp.bfloat16
F32 = jnp.float32
PAD = 128


def vmem():
    return pl.BlockSpec(memory_space=pltpu.VMEM)


def smem():
    return pl.BlockSpec(memory_space=pltpu.SMEM)


def hbm():
    return pl.BlockSpec(memory_space=pltpu.MemorySpace.HBM)


def params():
    return pltpu.CompilerParams(vmem_limit_bytes=44 * 1024 * 1024)


def cost(touched):
    return pl.CostEstimate(flops=touched, bytes_accessed=touched, transcendentals=0)


def blank_edges(rows):
    width = rows.shape[2]
    for r in (0, 1, 10, 11):
        rows[r] = jnp.zeros((16, width), F32)
    for r in range(2, 10):
        rows[r, :, width - PAD :] = jnp.zeros((16, PAD), F32)


def pack_kernel(
    pos, prior, wind, turned_0, turned_1, pay_a, pay_b, state, edge, sems
):
    winds = pltpu.make_async_copy(wind.at[0], edge, sems.at[4])
    loads = {}
    for f in range(2):
        for g in range(2):
            span = slice(8 * g, 8 * g + 8)
            loads[f, g] = pltpu.make_async_copy(
                prior.at[span, f], state.at[f, span], sems.at[2 * f + g]
            )
            loads[f, g].start()
    winds.start()
    even = (pos[0] % 2) == 0
    start_a = jnp.where(even, 4, 0)
    start_b = 4 - start_a
    cols = state.shape[3]
    blank_edges(turned_0)
    blank_edges(turned_1)
    for f in range(2):
        turned = (turned_0, turned_1)[f]
        for g in range(2):
            span = slice(8 * g, 8 * g + 8)
            loads[f, g].wait()
            turned[2:10, span, :cols] = jnp.swapaxes(state[f, span], 0, 1)
        for r in range(4):
            at = (f * 4 + r) * 16
            pay_a[at : at + 16, :] = turned[2 + start_a + r, :, :cols].astype(BF)
            pay_b[at : at + 16, :] = turned[2 + start_b + r, :, :cols].astype(BF)
    winds.wait()
    first = jnp.concatenate([edge[0, 0:2], edge[1, 0:2]], 0)
    last = jnp.concatenate([edge[0, 6:8], edge[1, 6:8]], 0)
    first_high = first.astype(BF).astype(F32)
    last_high = last.astype(BF).astype(F32)
    first = jnp.concatenate([first_high, first - first_high], 0)
    last = jnp.concatenate([last_high, last - last_high], 0)
    pay_a[128:136, :] = jnp.where(even, last, first).astype(BF)
    pay_b[128:136, :] = jnp.where(even, first, last).astype(BF)


def slots_kernel(parts, pos, index, count, weight, value, place, chunk, root_out, rooted_out):
    slots = index.shape[1]
    width = place.shape[0]
    n = index[...]
    used = lax.broadcasted_iota(jnp.int32, (1, slots), 1) < count[0]
    root = jnp.where(used, jnp.sqrt(weight[...]), 0.0)
    root_out[...] = root
    rooted_out[...] = root * value[...]
    cell = n // width
    row = (cell // parts) % 8
    first = jnp.where((pos[0] % 2) == 0, 1, 0)
    phase = jnp.where(row // 4 == first, 0, 1)
    stand = (phase * 2 + cell // (8 * parts)) * 4 + row % 4
    chunk[...] = jnp.broadcast_to(stand * parts + cell % parts, (16, slots))
    column = n % width
    step = 64
    for r in range(0, width, step):
        hit = lax.broadcasted_iota(jnp.int32, (step, slots), 0) == column - r
        place[r : r + step, :] = jnp.where(hit, 1.0, 0.0).astype(BF)


def pick_kernel(place, chunk, one, more, out, tall):
    width, slots = place.shape
    parts = one.shape[2] // width
    at = 0
    for ref in (one, more):
        for r in range(ref.shape[0]):
            for p in range(parts):
                tall[at * 16 : at * 16 + 16, :] = ref[r, :, p * width : (p + 1) * width]
                at += 1
    count = at
    step = 256
    for o in range(0, slots, step):
        cut = slice(o, o + step)
        seen = jnp.dot(tall[...], place[:, cut], preferred_element_type=F32)
        number = chunk[:, cut]
        total = jnp.zeros((16, step), F32)
        for at in range(count):
            total = total + jnp.where(number == at, seen[at * 16 : at * 16 + 16], 0.0)
        out[:, cut] = total.astype(BF)


def stencil_row(rows, wind_r, wind_c, nu):
    south_two, south_one, center, north_one, north_two = rows
    width = [v for v in rows if v is not None][0].shape[1]
    keep = width - PAD

    def less(a, b):
        if a is None:
            return None if b is None else -b
        return a if b is None else a - b

    def more(a, b):
        if a is None or b is None:
            return b if a is None else a
        return a + b

    rows = [None if v is None else v[:, :keep] for v in rows]
    one = less(rows[3], rows[1])
    grad_r = less(None if one is None else 8.0 * one, less(rows[4], rows[0]))
    ring = more(rows[3], rows[1])
    out = -(wind_r * grad_r)
    if center is not None:
        east_one = pltpu.roll(center, width - 1, 1)
        west_one = pltpu.roll(center, 1, 1)
        east_two = pltpu.roll(center, width - 2, 1)
        west_two = pltpu.roll(center, 2, 1)
        grad_c = 8.0 * (east_one - west_one) - (east_two - west_two)
        ring = more(ring, (east_one + west_one)[:, :keep])
        out = (1.0 - 4.0 * nu) * rows[2] + out - wind_c * grad_c[:, :keep]
    return out if ring is None else out + nu * ring


TWELFTH = 1.0 / 12.0


def pre_kernel(nu, turned, wind, out, mid, wide):
    cols = out.shape[2]
    blank_edges(mid)
    for step in range(2):
        for c in range(2):
            for r in range(8):
                wide[step, c, r] = jnp.broadcast_to(wind[step, c, r : r + 1] * TWELFTH, (8, cols))

    def first_step(r, carry):
        for g in range(2):
            span = pl.ds(g * 8, 8)
            rows = [turned[r + i, span, :] for i in range(5)]
            mid[r + 2, span, :cols] = stencil_row(rows, wide[0, 0, r], wide[0, 1, r], nu)
        return carry

    lax.fori_loop(0, 8, first_step, 0)

    def second_step(r, carry):
        for g in range(2):
            span = pl.ds(g * 8, 8)
            rows = [mid[r + i, span, :] for i in range(5)]
            out[r, span, :] = stencil_row(rows, wide[1, 0, r], wide[1, 1, r], nu)
        return carry

    lax.fori_loop(0, 8, second_step, 0)


def post_kernel(field, phase, pos, turned, begun, recv, wind, *refs):
    out, halo, delta = refs[-3:]
    ahead = refs[0] if len(refs) == 4 else None
    nu = DIFFUSION[field]
    cols = begun.shape[2]
    even = (pos[0] % 2) == 0
    blank = jnp.zeros((16, PAD), F32)
    start = 0
    if ahead is not None:
        start = ahead.shape[0]
        out[0:start] = ahead[...]
    for r in range(4):
        at = (field * 4 + r) * 16
        halo[r, :, :cols] = recv[at : at + 16, :].astype(F32)
        halo[r, :, cols:] = blank
        delta[r, :, cols:] = blank
    outer = recv[128:136, :].astype(F32)
    outer = (outer[0:4] + outer[4:8]) * TWELFTH
    scale = (
        jnp.where(pos[0] == 0, 0.0, 1.0),
        jnp.where(pos[0] == pos[1] - 1, 0.0, 1.0),
    )

    def broad(row):
        return jnp.broadcast_to(row, (8, cols))

    def own_wind(step, c, r):
        return broad(wind[step, c, r : r + 1] * TWELFTH)

    def work(side):
        for g in range(2):
            span = slice(g * 8, g * 8 + 8)
            h = lambda i: halo[i, span, :]
            x = lambda r: turned[2 + r, span, :]
            if side == 0:
                line = [h(0), h(1), h(2), h(3), x(0), x(1)]
                inner = (
                    (2, 0, [h(2), h(3), None, None, None]),
                    (3, 1, [h(3), None, None, None, None]),
                )
            else:
                line = [x(6), x(7), h(0), h(1), h(2), h(3)]
                inner = (
                    (0, 6, [None, None, None, None, h(0)]),
                    (1, 7, [None, None, None, h(0), h(1)]),
                )
            for i in range(2):
                value = stencil_row(
                    line[i : i + 5], broad(outer[i : i + 1]), broad(outer[2 + i : 3 + i]), nu
                )
                delta[2 * side + i, span, :cols] = value * scale[side]
            for at, r, near in inner:
                delta[at, span, :cols] = stencil_row(near, own_wind(0, 0, r), None, nu)
        low = 6 if side else -2
        for k in range(4):
            r = 4 * side + k
            both = []
            for g in range(2):
                span = slice(g * 8, g * 8 + 8)
                near = []
                for i in range(r - 2, r + 3):
                    near.append(delta[i - low, span, :] if low <= i < low + 4 else None)
                center = near[2] is not None
                value = stencil_row(
                    near, own_wind(1, 0, r), own_wind(1, 1, r) if center else None, nu
                )
                both.append(begun[r, span, :] + value)
            out[start + k] = jnp.concatenate(both, 0).astype(BF)

    pl.when(even)(lambda: work(1 - phase))
    pl.when(jnp.logical_not(even))(lambda: work(phase))


def gram_kernel(pos, own, mate, far, diag, root, rooted, out, spread):
    parts = [v[...].astype(F32) for v in (own, mate, far, diag)]
    total = (parts[0] + parts[1]) + (parts[2] + parts[3])
    mean = jnp.sum(total, 0, keepdims=True) * (1.0 / REPLICA_COUNT)
    weight = root[...]
    gap = rooted[...] - weight * mean
    for g in range(4):
        spread[jnp.bitwise_xor(pos[2], g)] = ((parts[g] - mean) * weight).astype(BF)
    high = gap.astype(BF).astype(F32)
    slots = root.shape[1]
    pair = jnp.concatenate([high, gap - high, jnp.zeros((14, slots), F32)], 0)
    spread[4] = pair.astype(BF)
    left = spread[...].reshape(80, slots)
    right = spread[0:4].reshape(64, slots)
    out[...] = lax.dot_general(
        left, right, (((1,), (1,)), ((), ())), preferred_element_type=F32
    )


def exact(a, b):
    a_high = a.astype(BF)
    b_high = b.astype(BF)
    a_low = (a - a_high.astype(F32)).astype(BF)
    b_low = (b - b_high.astype(F32)).astype(BF)

    def product(x, y):
        return jnp.dot(x, y, preferred_element_type=F32)

    return product(a_high, b_high) + (product(a_high, b_low) + product(a_low, b_high))


def weights_kernel(pos, one, two, out, keep):
    total = one[...] + two[...]
    gram = total[0:64]
    drive = total[64:65] + total[65:66]
    row = lax.broadcasted_iota(jnp.int32, (64, 64), 0)
    col = lax.broadcasted_iota(jnp.int32, (64, 64), 1)
    ident = jnp.where(row == col, 1.0, 0.0)
    system = (REPLICA_COUNT - 1.0) * ident + gram
    square = jnp.sum(jnp.sum(system * system, 1, keepdims=True), 0, keepdims=True)
    scale = jnp.sqrt(square)
    root = system / scale
    inverse_root = ident
    for turn in range(NS_ITERS):
        if turn == 0:
            middle = 0.5 * (3.0 * ident - root)
            inverse_next = middle
        else:
            middle = 0.5 * (3.0 * ident - exact(inverse_root, root))
            inverse_next = exact(middle, inverse_root)
        if turn < NS_ITERS - 1:
            root = exact(root, middle)
        inverse_root = inverse_next
    half = inverse_root / jnp.sqrt(scale)
    drive8 = jnp.broadcast_to(drive, (8, 64))
    mean_weight = exact(exact(drive8, half), half)[0:1]
    transform_t = (mean_weight + (REPLICA_COUNT - 1.0) ** 0.5 * half).astype(BF).astype(F32)
    total_t = jnp.sum(transform_t, 1, keepdims=True)
    keep[...] = transform_t + (1.0 - total_t) * (1.0 / REPLICA_COUNT)
    mine = keep[pl.ds(pl.multiple_of(pos[2] * 16, 16), 16), :]
    swap1 = jnp.concatenate([mine[:, 16:32], mine[:, 0:16], mine[:, 48:64], mine[:, 32:48]], 1)
    mine = jnp.where((pos[2] % 2) == 1, swap1, mine)
    swap2 = jnp.concatenate([mine[:, 32:64], mine[:, 0:32]], 1)
    mine = jnp.where(pos[2] >= 2, swap2, mine)
    high = mine.astype(BF).astype(F32)
    pair = jnp.concatenate([high, mine - high], 0)
    blank = jnp.zeros((32, 64), F32)
    for r in range(4):
        line = [pair if k == r else blank for k in range(4)]
        out[r * 32 : r * 32 + 32, :] = jnp.concatenate(line, 1).astype(BF)


def final_kernel(
    pos, weights, own, mate, far, diag, own_more, mate_more, far_more, diag_more, out, keep, ready, sems
):
    cols = own.shape[2]
    step = 512
    half = cols // 2
    copies = {}
    for f in range(2):
        for part in range(2):
            span = slice(part * half, part * half + half)
            copies[f, part] = pltpu.make_async_copy(
                ready.at[f, :, :, span], out.at[:, f, :, span], sems.at[2 * f + part]
            )

    def work(early):
        for f in range(2):
            for part in range(2):
                span = slice(part * half, part * half + half)
                for turn in range(2):
                    first = f == 0 and turn == 0
                    refs = (own, mate, far, diag)
                    if not first:
                        refs = (own_more, mate_more, far_more, diag_more)
                    at = 4 + 4 * f if turn else 0
                    base = 4 - early if turn else early
                    for c in range(part * half, part * half + half, step):
                        cut = slice(c, c + step)
                        parts = [v[at + r, :, cut] for r in range(4) for v in refs]
                        both = jnp.dot(
                            weights[...], jnp.concatenate(parts, 0), preferred_element_type=F32
                        )
                        for r in range(4):
                            high = both[r * 32 : r * 32 + 16]
                            keep[base + r, :, cut] = high + both[r * 32 + 16 : r * 32 + 32]
                ready[f, :, :, span] = jnp.swapaxes(keep[:, :, span], 0, 1)
                copies[f, part].start()

    even = (pos[0] % 2) == 0
    pl.when(even)(lambda: work(4))
    pl.when(jnp.logical_not(even))(lambda: work(0))
    for copy in copies.values():
        copy.wait()


def local(prior_replicas, wind_field, obs_index, obs_count, obs_value, obs_weight):
    cols = prior_replicas.shape[3]
    strips = lax.axis_size("space")
    here = lax.axis_index("space")
    group = lax.axis_index("mem")
    pos = jnp.stack([here, jnp.int32(strips), group]).astype(jnp.int32)
    shape = jax.ShapeDtypeStruct
    pairs_a = [(i, i ^ 1) for i in range(strips)]
    pairs_b = [(i, i + 1) for i in range(1, strips - 1, 2)]
    pairs_b = pairs_b + [(j, i) for i, j in pairs_b]

    def swap(value, bits):
        return lax.ppermute(value, "mem", [(i, i ^ bits) for i in range(4)])

    prior_here = pltpu.with_memory_space_constraint(prior_replicas, pltpu.MemorySpace.HBM)
    wind_here = pltpu.with_memory_space_constraint(wind_field, pltpu.MemorySpace.HBM)

    packed = pl.pallas_call(
        pack_kernel,
        name="pack",
        cost_estimate=cost(80 * 16 * cols * 4),
        in_specs=[smem(), hbm(), hbm()],
        out_specs=[vmem()] * 4,
        out_shape=[shape((12, 16, cols + PAD), F32)] * 2
        + [shape((136, cols), BF)] * 2,
        scratch_shapes=[
            pltpu.VMEM((2, 16, 8, cols), F32),
            pltpu.VMEM((2, 8, cols), F32),
            pltpu.SemaphoreType.DMA((5,)),
        ],
        compiler_params=params(),
    )(pos, prior_here, wind_here)
    turned = packed[0:2]
    recv_a = lax.ppermute(packed[2], "space", pairs_a)
    recv_b = lax.ppermute(packed[3], "space", pairs_b)

    def pre(f, rows):
        return pl.pallas_call(
            functools.partial(pre_kernel, DIFFUSION[f]),
            name="pre",
            cost_estimate=cost(150 * 16 * cols * 4),
            in_specs=[vmem()] * 2,
            out_specs=vmem(),
            out_shape=shape((8, 16, cols), F32),
            scratch_shapes=[
                pltpu.VMEM((12, 16, cols + PAD), F32),
                pltpu.VMEM((2, 2, 8, 8, cols), F32),
            ],
            compiler_params=params(),
        )(rows, wind_field)

    begun = [pre(f, turned[f]) for f in range(2)]

    slots = obs_index.shape[0]
    width = 512
    place, chunk, root, rooted = pl.pallas_call(
        functools.partial(slots_kernel, cols // width),
        name="slots",
        cost_estimate=cost(width * slots * 2),
        in_specs=[smem(), vmem(), smem(), vmem(), vmem()],
        out_specs=[vmem()] * 4,
        out_shape=[
            shape((width, slots), BF),
            shape((16, slots), jnp.int32),
            shape((1, slots), F32),
            shape((1, slots), F32),
        ],
        compiler_params=params(),
    )(
        pos,
        obs_index.reshape(1, slots),
        obs_count,
        obs_weight.reshape(1, slots),
        obs_value.reshape(1, slots),
    )
    recv_a, begun[0], begun[1], place = lax.optimization_barrier(
        (recv_a, begun[0], begun[1], place)
    )

    def post(f, phase, recv, extra):
        height = 4 + sum(v.shape[0] for v in extra)
        return pl.pallas_call(
            functools.partial(post_kernel, f, phase),
            name="post",
            cost_estimate=cost(8),
            in_specs=[smem()] + [vmem()] * (4 + len(extra)),
            out_specs=vmem(),
            out_shape=shape((height, 16, cols), BF),
            scratch_shapes=[
                pltpu.VMEM((4, 16, cols + PAD), F32),
                pltpu.VMEM((4, 16, cols + PAD), F32),
            ],
            compiler_params=params(),
        )(pos, turned[f], begun[f], recv, wind_field, *extra)

    one = post(0, 0, recv_a, [])
    far_one = swap(one, 2)
    more = post(1, 0, recv_a, [])
    recv_b, more = lax.optimization_barrier((recv_b, more))
    more = post(0, 1, recv_b, [more])
    more = post(1, 1, recv_b, [more])
    seen = pl.pallas_call(
        pick_kernel,
        name="pick",
        cost_estimate=cost(8),
        in_specs=[vmem()] * 4,
        out_specs=vmem(),
        out_shape=shape((16, slots), BF),
        scratch_shapes=[pltpu.VMEM((16 * 16 * cols // width, width), BF)],
        compiler_params=params(),
    )(place, chunk, one, more)

    seen_far = swap(seen, 2)
    seen_mate = swap(seen, 1)
    seen_far, far_one, late = lax.optimization_barrier((seen_far, far_one, more))
    far_more = swap(late, 2)
    seen_diag = swap(seen_far, 1)

    part = pl.pallas_call(
        gram_kernel,
        name="gram",
        cost_estimate=cost(24 * 64 * slots),
        in_specs=[smem()] + [vmem()] * 6,
        out_specs=vmem(),
        out_shape=shape((80, 64), F32),
        scratch_shapes=[pltpu.VMEM((5, 16, slots), BF)],
        compiler_params=params(),
    )(pos, seen, seen_mate, seen_far, seen_diag, root, rooted)

    mate_more = swap(more, 1)
    mate_one = swap(one, 1)
    diag_one = swap(far_one, 1)
    bits = 1
    other = None
    while bits < strips:
        if other is not None:
            part = part + other
            part, mate_one, diag_one = lax.optimization_barrier((part, mate_one, diag_one))
        other = lax.ppermute(part, "space", [(i, i ^ bits) for i in range(strips)])
        bits *= 2
    late, _ = lax.optimization_barrier((far_more, other))
    diag_more = swap(late, 1)

    weights = pl.pallas_call(
        weights_kernel,
        name="weights",
        cost_estimate=cost(400 * 64 * 128 * 4),
        in_specs=[smem(), vmem(), vmem()],
        out_specs=vmem(),
        out_shape=shape((128, 256), BF),
        scratch_shapes=[pltpu.VMEM((64, 64), F32)],
        compiler_params=params(),
    )(pos, part, other)

    return pl.pallas_call(
        final_kernel,
        name="final",
        cost_estimate=cost(100 * 16 * cols * 4),
        in_specs=[smem()] + [vmem()] * 9,
        out_specs=hbm(),
        out_shape=shape(prior_replicas.shape, F32),
        scratch_shapes=[
            pltpu.VMEM((8, 16, cols), F32),
            pltpu.VMEM((2, 16, 8, cols), F32),
            pltpu.SemaphoreType.DMA((4,)),
        ],
        compiler_params=params(),
    )(
        pos, weights, one, mate_one, far_one, diag_one, more, mate_more, far_more, diag_more
    )


def solution(mesh):
    in_specs = (
        P(("parts", "mem"), None, "space", None),
        P("parts", None, "space", None),
        P(("parts", "space")),
        P(("parts", "space")),
        P(("parts", "space")),
        P(("parts", "space")),
    )
    out_specs = P(("parts", "mem"), None, "space", None)
    strips = mesh.shape["space"]
    fast = mesh.shape["mem"] == 4 and strips > 1 and strips & (strips - 1) == 0
    body = local if fast else local_generic
    return jax.shard_map(body, mesh=mesh, in_specs=in_specs, out_specs=out_specs, check_vma=False)
```

```python
import functools

import jax
import jax.numpy as jnp
from jax import lax
from jax.experimental import pallas as pl
from jax.experimental.pallas import tpu as pltpu
from jax.sharding import PartitionSpec as P

REPLICA_COUNT = 64
NS_ITERS = 5


DIFFUSION = (0.05, 0.15)


def padded(value, sides, width):
    for axis, dim in sides:
        peers, length = (lax.axis_size(axis), value.shape[dim])
        up = [(i, (i + 1) % peers) for i in range(peers - 1)]
        down = [(j, i) for i, j in up]
        last = lax.slice_in_dim(value, length - width, length, axis=dim)
        initial = lax.slice_in_dim(value, 0, width, axis=dim)
        before = lax.ppermute(last, axis, up)
        after = lax.ppermute(initial, axis, down)
        value = jnp.concatenate([before, value, after], axis=dim)
    return value


def shift_columns(field, offset):
    width = field.shape[-1]
    blank = jnp.zeros(field.shape[:-1] + (abs(offset),), field.dtype)
    if offset > 0:
        return jnp.concatenate([field[..., offset:], blank], -1)
    return jnp.concatenate([blank, field[..., : width + offset]], -1)


def advance(extended, wind_rows):
    center = extended[:, :, 2:-2]
    north_one = extended[:, :, 3:-1]
    south_one = extended[:, :, 1:-3]
    north_two = extended[:, :, 4:]
    south_two = extended[:, :, :-4]
    east_one = shift_columns(center, 1)
    west_one = shift_columns(center, -1)
    east_two = shift_columns(center, 2)
    west_two = shift_columns(center, -2)
    grad_row = (8.0 * (north_one - south_one) - (north_two - south_two)) / 12.0
    grad_col = (8.0 * (east_one - west_one) - (east_two - west_two)) / 12.0
    laplace = north_one + south_one + east_one + west_one - 4.0 * center
    diffusion = jnp.array(DIFFUSION, jnp.float32).reshape(2, 1, 1)
    return center - wind_rows[0] * grad_row - wind_rows[1] * grad_col + diffusion * laplace


def shard_terms(observed, slot_weight, obs_value):
    obs_mean = jnp.sum(observed, 0) / REPLICA_COUNT
    obs_anomaly = observed - obs_mean
    weighted = obs_anomaly * slot_weight
    gram = jnp.dot(
        weighted, obs_anomaly.T, precision=lax.Precision.HIGHEST, preferred_element_type=jnp.float32
    )
    drive = jnp.dot(
        weighted,
        obs_value - obs_mean,
        precision=lax.Precision.HIGHEST,
        preferred_element_type=jnp.float32,
    )
    return (gram, drive)


def ensemble_weights(gram, drive):
    ident = jnp.eye(REPLICA_COUNT, dtype=jnp.float32)
    system = (REPLICA_COUNT - 1.0) * ident + gram
    scale = jnp.sqrt(jnp.sum(system * system))

    def newton_turn(turn, carry):
        root, inverse_root = carry
        middle_term = 0.5 * (
            3.0 * ident
            - jnp.dot(
                inverse_root,
                root,
                precision=lax.Precision.HIGHEST,
                preferred_element_type=jnp.float32,
            )
        )
        root = jnp.dot(
            root, middle_term, precision=lax.Precision.HIGHEST, preferred_element_type=jnp.float32
        )
        inverse_root = jnp.dot(
            middle_term,
            inverse_root,
            precision=lax.Precision.HIGHEST,
            preferred_element_type=jnp.float32,
        )
        return (root, inverse_root)

    root, inverse_root = lax.fori_loop(0, NS_ITERS, newton_turn, (system / scale, ident))
    half = inverse_root / jnp.sqrt(scale)
    precision_matrix = jnp.dot(
        half, half, precision=lax.Precision.HIGHEST, preferred_element_type=jnp.float32
    )
    mean_weight = jnp.dot(
        precision_matrix, drive, precision=lax.Precision.HIGHEST, preferred_element_type=jnp.float32
    )
    spread = jnp.sqrt(REPLICA_COUNT - 1.0) * half
    return (mean_weight[:, None] + spread).astype(jnp.bfloat16)


def local_generic(prior_replicas, wind_field, obs_index, obs_count, obs_value, obs_weight):
    member_count, field_count, row_count, col_count = prior_replicas.shape
    state = prior_replicas
    for step_index in range(2):
        extended = padded(state, (("space", 2),), 2)
        state = advance(extended, wind_field[step_index])
    capacity = obs_index.shape[0]
    raveled_vector = state.reshape(member_count, -1)
    local_obs = jnp.take(raveled_vector, obs_index, axis=1)
    slot_number = jnp.arange(capacity, dtype=jnp.int32)
    slot_weight = obs_weight * (slot_number < obs_count[0]).astype(jnp.float32)
    gathered = lax.all_gather(local_obs, "mem", axis=0, tiled=True)
    gram, drive = shard_terms(gathered, slot_weight, obs_value)
    gram, drive = lax.psum((gram, drive), "space")
    transform = ensemble_weights(gram, drive)
    transform_rows = transform.T
    block = lax.all_to_all(state, "mem", split_axis=3, concat_axis=0, tiled=True)
    replica_centroid = jnp.sum(block, 0) / REPLICA_COUNT
    replica_departure = (block - replica_centroid).astype(jnp.bfloat16)
    posterior_correction = jnp.dot(
        transform_rows,
        replica_departure.reshape(REPLICA_COUNT, -1),
        preferred_element_type=jnp.float32,
    )
    analysed = posterior_correction.reshape(block.shape) + replica_centroid
    return lax.all_to_all(analysed, "mem", split_axis=0, concat_axis=3, tiled=True)


BF = jnp.bfloat16
F32 = jnp.float32
PAD = 128


def vmem():
    return pl.BlockSpec(memory_space=pltpu.VMEM)


def smem():
    return pl.BlockSpec(memory_space=pltpu.SMEM)


def hbm():
    return pl.BlockSpec(memory_space=pltpu.MemorySpace.HBM)


def params():
    return pltpu.CompilerParams(vmem_limit_bytes=44 * 1024 * 1024)


def cost(touched):
    return pl.CostEstimate(flops=touched, bytes_accessed=touched, transcendentals=0)


def blank_edges(rows):
    width = rows.shape[2]
    for r in (0, 1, 10, 11):
        rows[r] = jnp.zeros((16, width), F32)
    for r in range(2, 10):
        rows[r, :, width - PAD :] = jnp.zeros((16, PAD), F32)


def pack_kernel(
    pos, prior, wind, turned_0, turned_1, pay_a, pay_b, state, edge, sems
):
    winds = pltpu.make_async_copy(wind.at[0], edge, sems.at[4])
    loads = {}
    for f in range(2):
        for g in range(2):
            span = slice(8 * g, 8 * g + 8)
            loads[f, g] = pltpu.make_async_copy(
                prior.at[span, f], state.at[f, span], sems.at[2 * f + g]
            )
            loads[f, g].start()
    winds.start()
    even = (pos[0] % 2) == 0
    start_a = jnp.where(even, 4, 0)
    start_b = 4 - start_a
    cols = state.shape[3]
    blank_edges(turned_0)
    blank_edges(turned_1)
    for f in range(2):
        turned = (turned_0, turned_1)[f]
        for g in range(2):
            span = slice(8 * g, 8 * g + 8)
            loads[f, g].wait()
            turned[2:10, span, :cols] = jnp.swapaxes(state[f, span], 0, 1)
        for r in range(4):
            at = (f * 4 + r) * 16
            pay_a[at : at + 16, :] = turned[2 + start_a + r, :, :cols].astype(BF)
            pay_b[at : at + 16, :] = turned[2 + start_b + r, :, :cols].astype(BF)
    winds.wait()
    first = jnp.concatenate([edge[0, 0:2], edge[1, 0:2]], 0)
    last = jnp.concatenate([edge[0, 6:8], edge[1, 6:8]], 0)
    first_high = first.astype(BF).astype(F32)
    last_high = last.astype(BF).astype(F32)
    first = jnp.concatenate([first_high, first - first_high], 0)
    last = jnp.concatenate([last_high, last - last_high], 0)
    pay_a[128:136, :] = jnp.where(even, last, first).astype(BF)
    pay_b[128:136, :] = jnp.where(even, first, last).astype(BF)


def slots_kernel(parts, pos, index, count, weight, value, place, chunk, root_out, rooted_out):
    slots = index.shape[1]
    width = place.shape[0]
    n = index[...]
    used = lax.broadcasted_iota(jnp.int32, (1, slots), 1) < count[0]
    root = jnp.where(used, jnp.sqrt(weight[...]), 0.0)
    root_out[...] = root
    rooted_out[...] = root * value[...]
    cell = n // width
    row = (cell // parts) % 8
    first = jnp.where((pos[0] % 2) == 0, 1, 0)
    phase = jnp.where(row // 4 == first, 0, 1)
    stand = (phase * 2 + cell // (8 * parts)) * 4 + row % 4
    chunk[...] = jnp.broadcast_to(stand * parts + cell % parts, (16, slots))
    column = n % width
    step = 64
    for r in range(0, width, step):
        hit = lax.broadcasted_iota(jnp.int32, (step, slots), 0) == column - r
        place[r : r + step, :] = jnp.where(hit, 1.0, 0.0).astype(BF)


def pick_kernel(place, chunk, one, more, out, tall):
    width, slots = place.shape
    parts = one.shape[2] // width
    at = 0
    for ref in (one, more):
        for r in range(ref.shape[0]):
            for p in range(parts):
                tall[at * 16 : at * 16 + 16, :] = ref[r, :, p * width : (p + 1) * width]
                at += 1
    count = at
    step = 256
    for o in range(0, slots, step):
        cut = slice(o, o + step)
        seen = jnp.dot(tall[...], place[:, cut], preferred_element_type=F32)
        number = chunk[:, cut]
        total = jnp.zeros((16, step), F32)
        for at in range(count):
            total = total + jnp.where(number == at, seen[at * 16 : at * 16 + 16], 0.0)
        out[:, cut] = total.astype(BF)


def stencil_row(rows, wind_r, wind_c, nu):
    south_two, south_one, center, north_one, north_two = rows
    width = [v for v in rows if v is not None][0].shape[1]
    keep = width - PAD

    def less(a, b):
        if a is None:
            return None if b is None else -b
        return a if b is None else a - b

    def more(a, b):
        if a is None or b is None:
            return b if a is None else a
        return a + b

    rows = [None if v is None else v[:, :keep] for v in rows]
    one = less(rows[3], rows[1])
    grad_r = less(None if one is None else 8.0 * one, less(rows[4], rows[0]))
    ring = more(rows[3], rows[1])
    out = -(wind_r * grad_r)
    if center is not None:
        east_one = pltpu.roll(center, width - 1, 1)
        west_one = pltpu.roll(center, 1, 1)
        east_two = pltpu.roll(center, width - 2, 1)
        west_two = pltpu.roll(center, 2, 1)
        grad_c = 8.0 * (east_one - west_one) - (east_two - west_two)
        ring = more(ring, (east_one + west_one)[:, :keep])
        out = (1.0 - 4.0 * nu) * rows[2] + out - wind_c * grad_c[:, :keep]
    return out if ring is None else out + nu * ring


TWELFTH = 1.0 / 12.0


def pre_kernel(nu, turned, wind, out, mid, wide):
    cols = out.shape[2]
    blank_edges(mid)
    for step in range(2):
        for c in range(2):
            for r in range(8):
                wide[step, c, r] = jnp.broadcast_to(wind[step, c, r : r + 1] * TWELFTH, (8, cols))

    def first_step(r, carry):
        for g in range(2):
            span = pl.ds(g * 8, 8)
            rows = [turned[r + i, span, :] for i in range(5)]
            mid[r + 2, span, :cols] = stencil_row(rows, wide[0, 0, r], wide[0, 1, r], nu)
        return carry

    lax.fori_loop(0, 8, first_step, 0)

    def second_step(r, carry):
        for g in range(2):
            span = pl.ds(g * 8, 8)
            rows = [mid[r + i, span, :] for i in range(5)]
            out[r, span, :] = stencil_row(rows, wide[1, 0, r], wide[1, 1, r], nu)
        return carry

    lax.fori_loop(0, 8, second_step, 0)


def post_kernel(field, phase, pos, turned, begun, recv, wind, *refs):
    out, halo, delta = refs[-3:]
    ahead = refs[0] if len(refs) == 4 else None
    nu = DIFFUSION[field]
    cols = begun.shape[2]
    even = (pos[0] % 2) == 0
    blank = jnp.zeros((16, PAD), F32)
    start = 0
    if ahead is not None:
        start = ahead.shape[0]
        out[0:start] = ahead[...]
    for r in range(4):
        at = (field * 4 + r) * 16
        halo[r, :, :cols] = recv[at : at + 16, :].astype(F32)
        halo[r, :, cols:] = blank
        delta[r, :, cols:] = blank
    outer = recv[128:136, :].astype(F32)
    outer = (outer[0:4] + outer[4:8]) * TWELFTH
    scale = (
        jnp.where(pos[0] == 0, 0.0, 1.0),
        jnp.where(pos[0] == pos[1] - 1, 0.0, 1.0),
    )

    def broad(row):
        return jnp.broadcast_to(row, (8, cols))

    def own_wind(step, c, r):
        return broad(wind[step, c, r : r + 1] * TWELFTH)

    def work(side):
        for g in range(2):
            span = slice(g * 8, g * 8 + 8)
            h = lambda i: halo[i, span, :]
            x = lambda r: turned[2 + r, span, :]
            if side == 0:
                line = [h(0), h(1), h(2), h(3), x(0), x(1)]
                inner = (
                    (2, 0, [h(2), h(3), None, None, None]),
                    (3, 1, [h(3), None, None, None, None]),
                )
            else:
                line = [x(6), x(7), h(0), h(1), h(2), h(3)]
                inner = (
                    (0, 6, [None, None, None, None, h(0)]),
                    (1, 7, [None, None, None, h(0), h(1)]),
                )
            for i in range(2):
                value = stencil_row(
                    line[i : i + 5], broad(outer[i : i + 1]), broad(outer[2 + i : 3 + i]), nu
                )
                delta[2 * side + i, span, :cols] = value * scale[side]
            for at, r, near in inner:
                delta[at, span, :cols] = stencil_row(near, own_wind(0, 0, r), None, nu)
        low = 6 if side else -2
        for k in range(4):
            r = 4 * side + k
            both = []
            for g in range(2):
                span = slice(g * 8, g * 8 + 8)
                near = []
                for i in range(r - 2, r + 3):
                    near.append(delta[i - low, span, :] if low <= i < low + 4 else None)
                center = near[2] is not None
                value = stencil_row(
                    near, own_wind(1, 0, r), own_wind(1, 1, r) if center else None, nu
                )
                both.append(begun[r, span, :] + value)
            out[start + k] = jnp.concatenate(both, 0).astype(BF)

    pl.when(even)(lambda: work(1 - phase))
    pl.when(jnp.logical_not(even))(lambda: work(phase))


def gram_kernel(pos, own, mate, far, diag, root, rooted, out, spread):
    parts = [v[...].astype(F32) for v in (own, mate, far, diag)]
    total = (parts[0] + parts[1]) + (parts[2] + parts[3])
    mean = jnp.sum(total, 0, keepdims=True) * (1.0 / REPLICA_COUNT)
    weight = root[...]
    gap = rooted[...] - weight * mean
    for g in range(4):
        spread[jnp.bitwise_xor(pos[2], g)] = ((parts[g] - mean) * weight).astype(BF)
    high = gap.astype(BF).astype(F32)
    slots = root.shape[1]
    pair = jnp.concatenate([high, gap - high, jnp.zeros((14, slots), F32)], 0)
    spread[4] = pair.astype(BF)
    left = spread[...].reshape(80, slots)
    right = spread[0:4].reshape(64, slots)
    out[...] = lax.dot_general(
        left, right, (((1,), (1,)), ((), ())), preferred_element_type=F32
    )


def exact(a, b):
    a_high = a.astype(BF)
    b_high = b.astype(BF)
    a_low = (a - a_high.astype(F32)).astype(BF)
    b_low = (b - b_high.astype(F32)).astype(BF)

    def product(x, y):
        return jnp.dot(x, y, preferred_element_type=F32)

    return product(a_high, b_high) + (product(a_high, b_low) + product(a_low, b_high))


def weights_kernel(pos, one, two, out, keep):
    total = one[...] + two[...]
    gram = total[0:64]
    drive = total[64:65] + total[65:66]
    row = lax.broadcasted_iota(jnp.int32, (64, 64), 0)
    col = lax.broadcasted_iota(jnp.int32, (64, 64), 1)
    ident = jnp.where(row == col, 1.0, 0.0)
    system = (REPLICA_COUNT - 1.0) * ident + gram
    square = jnp.sum(jnp.sum(system * system, 1, keepdims=True), 0, keepdims=True)
    scale = jnp.sqrt(square)
    root = system / scale
    inverse_root = ident
    for turn in range(NS_ITERS):
        if turn == 0:
            middle = 0.5 * (3.0 * ident - root)
            inverse_next = middle
        else:
            middle = 0.5 * (3.0 * ident - exact(inverse_root, root))
            inverse_next = exact(middle, inverse_root)
        if turn < NS_ITERS - 1:
            root = exact(root, middle)
        inverse_root = inverse_next
    half = inverse_root / jnp.sqrt(scale)
    drive8 = jnp.broadcast_to(drive, (8, 64))
    mean_weight = exact(exact(drive8, half), half)[0:1]
    transform_t = (mean_weight + (REPLICA_COUNT - 1.0) ** 0.5 * half).astype(BF).astype(F32)
    total_t = jnp.sum(transform_t, 1, keepdims=True)
    keep[...] = transform_t + (1.0 - total_t) * (1.0 / REPLICA_COUNT)
    mine = keep[pl.ds(pl.multiple_of(pos[2] * 16, 16), 16), :]
    swap1 = jnp.concatenate([mine[:, 16:32], mine[:, 0:16], mine[:, 48:64], mine[:, 32:48]], 1)
    mine = jnp.where((pos[2] % 2) == 1, swap1, mine)
    swap2 = jnp.concatenate([mine[:, 32:64], mine[:, 0:32]], 1)
    mine = jnp.where(pos[2] >= 2, swap2, mine)
    high = mine.astype(BF).astype(F32)
    pair = jnp.concatenate([high, mine - high], 0)
    blank = jnp.zeros((32, 64), F32)
    for r in range(4):
        line = [pair if k == r else blank for k in range(4)]
        out[r * 32 : r * 32 + 32, :] = jnp.concatenate(line, 1).astype(BF)


def final_kernel(
    pos, weights, own, mate, far, diag, own_more, mate_more, far_more, diag_more, out, keep, ready, sems
):
    cols = own.shape[2]
    step = 512
    half = cols // 2
    copies = {}
    for f in range(2):
        for part in range(2):
            span = slice(part * half, part * half + half)
            copies[f, part] = pltpu.make_async_copy(
                ready.at[f, :, :, span], out.at[:, f, :, span], sems.at[2 * f + part]
            )

    def work(early):
        for f in range(2):
            for part in range(2):
                span = slice(part * half, part * half + half)
                for turn in range(2):
                    first = f == 0 and turn == 0
                    refs = (own, mate, far, diag)
                    if not first:
                        refs = (own_more, mate_more, far_more, diag_more)
                    at = 4 + 4 * f if turn else 0
                    base = 4 - early if turn else early
                    for c in range(part * half, part * half + half, step):
                        cut = slice(c, c + step)
                        parts = [v[at + r, :, cut] for r in range(4) for v in refs]
                        both = jnp.dot(
                            weights[...], jnp.concatenate(parts, 0), preferred_element_type=F32
                        )
                        for r in range(4):
                            high = both[r * 32 : r * 32 + 16]
                            keep[base + r, :, cut] = high + both[r * 32 + 16 : r * 32 + 32]
                ready[f, :, :, span] = jnp.swapaxes(keep[:, :, span], 0, 1)
                copies[f, part].start()

    even = (pos[0] % 2) == 0
    pl.when(even)(lambda: work(4))
    pl.when(jnp.logical_not(even))(lambda: work(0))
    for copy in copies.values():
        copy.wait()


def local(prior_replicas, wind_field, obs_index, obs_count, obs_value, obs_weight):
    cols = prior_replicas.shape[3]
    strips = lax.axis_size("space")
    here = lax.axis_index("space")
    group = lax.axis_index("mem")
    pos = jnp.stack([here, jnp.int32(strips), group]).astype(jnp.int32)
    shape = jax.ShapeDtypeStruct
    pairs_a = [(i, i ^ 1) for i in range(strips)]
    pairs_b = [(i, i + 1) for i in range(1, strips - 1, 2)]
    pairs_b = pairs_b + [(j, i) for i, j in pairs_b]

    def swap(value, bits):
        return lax.ppermute(value, "mem", [(i, i ^ bits) for i in range(4)])

    prior_here = pltpu.with_memory_space_constraint(prior_replicas, pltpu.MemorySpace.HBM)
    wind_here = pltpu.with_memory_space_constraint(wind_field, pltpu.MemorySpace.HBM)

    packed = pl.pallas_call(
        pack_kernel,
        name="pack",
        cost_estimate=cost(80 * 16 * cols * 4),
        in_specs=[smem(), hbm(), hbm()],
        out_specs=[vmem()] * 4,
        out_shape=[shape((12, 16, cols + PAD), F32)] * 2
        + [shape((136, cols), BF)] * 2,
        scratch_shapes=[
            pltpu.VMEM((2, 16, 8, cols), F32),
            pltpu.VMEM((2, 8, cols), F32),
            pltpu.SemaphoreType.DMA((5,)),
        ],
        compiler_params=params(),
    )(pos, prior_here, wind_here)
    turned = packed[0:2]
    recv_a = lax.ppermute(packed[2], "space", pairs_a)
    recv_b = lax.ppermute(packed[3], "space", pairs_b)

    def pre(f, rows):
        return pl.pallas_call(
            functools.partial(pre_kernel, DIFFUSION[f]),
            name="pre",
            cost_estimate=cost(150 * 16 * cols * 4),
            in_specs=[vmem()] * 2,
            out_specs=vmem(),
            out_shape=shape((8, 16, cols), F32),
            scratch_shapes=[
                pltpu.VMEM((12, 16, cols + PAD), F32),
                pltpu.VMEM((2, 2, 8, 8, cols), F32),
            ],
            compiler_params=params(),
        )(rows, wind_field)

    begun = [pre(f, turned[f]) for f in range(2)]

    slots = obs_index.shape[0]
    width = 512
    place, chunk, root, rooted = pl.pallas_call(
        functools.partial(slots_kernel, cols // width),
        name="slots",
        cost_estimate=cost(width * slots * 2),
        in_specs=[smem(), vmem(), smem(), vmem(), vmem()],
        out_specs=[vmem()] * 4,
        out_shape=[
            shape((width, slots), BF),
            shape((16, slots), jnp.int32),
            shape((1, slots), F32),
            shape((1, slots), F32),
        ],
        compiler_params=params(),
    )(
        pos,
        obs_index.reshape(1, slots),
        obs_count,
        obs_weight.reshape(1, slots),
        obs_value.reshape(1, slots),
    )
    recv_a, begun[0], begun[1], place = lax.optimization_barrier(
        (recv_a, begun[0], begun[1], place)
    )

    def post(f, phase, recv, extra):
        height = 4 + sum(v.shape[0] for v in extra)
        return pl.pallas_call(
            functools.partial(post_kernel, f, phase),
            name="post",
            cost_estimate=cost(8),
            in_specs=[smem()] + [vmem()] * (4 + len(extra)),
            out_specs=vmem(),
            out_shape=shape((height, 16, cols), BF),
            scratch_shapes=[
                pltpu.VMEM((4, 16, cols + PAD), F32),
                pltpu.VMEM((4, 16, cols + PAD), F32),
            ],
            compiler_params=params(),
        )(pos, turned[f], begun[f], recv, wind_field, *extra)

    one = post(0, 0, recv_a, [])
    far_one = swap(one, 2)
    more = post(1, 0, recv_a, [])
    recv_b, more = lax.optimization_barrier((recv_b, more))
    more = post(0, 1, recv_b, [more])
    more = post(1, 1, recv_b, [more])
    seen = pl.pallas_call(
        pick_kernel,
        name="pick",
        cost_estimate=cost(8),
        in_specs=[vmem()] * 4,
        out_specs=vmem(),
        out_shape=shape((16, slots), BF),
        scratch_shapes=[pltpu.VMEM((16 * 16 * cols // width, width), BF)],
        compiler_params=params(),
    )(place, chunk, one, more)

    seen_far = swap(seen, 2)
    seen_mate = swap(seen, 1)
    seen_far, far_one, late = lax.optimization_barrier((seen_far, far_one, more))
    far_more = swap(late, 2)
    seen_diag = swap(seen_far, 1)

    part = pl.pallas_call(
        gram_kernel,
        name="gram",
        cost_estimate=cost(24 * 64 * slots),
        in_specs=[smem()] + [vmem()] * 6,
        out_specs=vmem(),
        out_shape=shape((80, 64), F32),
        scratch_shapes=[pltpu.VMEM((5, 16, slots), BF)],
        compiler_params=params(),
    )(pos, seen, seen_mate, seen_far, seen_diag, root, rooted)

    mate_more = swap(more, 1)
    mate_one = swap(one, 1)
    diag_one = swap(far_one, 1)
    bits = 1
    other = None
    while bits < strips:
        if other is not None:
            part = part + other
            part, mate_one, diag_one = lax.optimization_barrier((part, mate_one, diag_one))
        other = lax.ppermute(part, "space", [(i, i ^ bits) for i in range(strips)])
        bits *= 2
    weights = pl.pallas_call(
        weights_kernel,
        name="weights",
        cost_estimate=cost(400 * 64 * 128 * 4),
        in_specs=[smem(), vmem(), vmem()],
        out_specs=vmem(),
        out_shape=shape((128, 256), BF),
        scratch_shapes=[pltpu.VMEM((64, 64), F32)],
        compiler_params=params(),
    )(pos, part, other)

    late, weights = lax.optimization_barrier((far_more, weights))
    diag_more = swap(late, 1)

    return pl.pallas_call(
        final_kernel,
        name="final",
        cost_estimate=cost(100 * 16 * cols * 4),
        in_specs=[smem()] + [vmem()] * 9,
        out_specs=hbm(),
        out_shape=shape(prior_replicas.shape, F32),
        scratch_shapes=[
            pltpu.VMEM((8, 16, cols), F32),
            pltpu.VMEM((2, 16, 8, cols), F32),
            pltpu.SemaphoreType.DMA((4,)),
        ],
        compiler_params=params(),
    )(
        pos, weights, one, mate_one, far_one, diag_one, more, mate_more, far_more, diag_more
    )


def solution(mesh):
    in_specs = (
        P(("parts", "mem"), None, "space", None),
        P("parts", None, "space", None),
        P(("parts", "space")),
        P(("parts", "space")),
        P(("parts", "space")),
        P(("parts", "space")),
    )
    out_specs = P(("parts", "mem"), None, "space", None)
    strips = mesh.shape["space"]
    fast = mesh.shape["mem"] == 4 and strips > 1 and strips & (strips - 1) == 0
    body = local if fast else local_generic
    return jax.shard_map(body, mesh=mesh, in_specs=in_specs, out_specs=out_specs, check_vma=False)
```
